512 devices in a mesh: gx: 16 (over z_hi, y, core), gy: 32 (over z_lo, x).
Axes of the slice: x: 4, y: 4, z: 16 (z_hi: 2, z_lo: 8; z = z_hi * 8 + z_lo), core: 2. Of those that a mesh axis runs over, the one named last changes fastest.
Arguments:
- adjoint_in: float32 [19, 256, 4, 4096], P(None, 'gx', None, 'gy'), may hold values from -6 to 6
- velocity: bfloat16 [2, 3, 256, 4, 4096], P(None, None, 'gx', None, 'gy')
- solid_tiles: int32 [64, 4, 1024], P('gx', None, 'gy'), may hold values from 0 to 1, as said below
- link_blocked: int32 [18, 256, 4, 4096], P(None, 'gx', None, 'gy'), may hold values from 0 to 1, as said below
Outputs:
- adjoint_out: float32 [19, 256, 4, 4096], P(None, 'gx', None, 'gy')
- drag_sens: float32 [1], replicated
The draws below stay inside these ranges and needn't reach their ends.
Inputs may be any that keep to these rules, and one draw needn't show every extreme that they name: `solid_tiles`: 1 on the levels below a tile's building height, heights 0 to 3 per tile. `link_blocked`: entry i - 1 is 1 exactly where the cell x + c_i (periodic in the plane) is solid or lies outside the 4 levels.
All inputs are finite; a program needn't handle non-finite values.
Results may differ from the reference program's by a relative error of at most 0.0003.
Values sent between devices are 32-bit elements; how exact they have to be, the bound alone decides.
A program may use at most 64 MiB of HBM per device.

```python
import math
import jax
import jax.numpy as jnp
from jax import lax

Q = 19
Z = 4
TILE = 4
STEPS = 2
NX = 256
NY = 4096


lattice_speeds = ((0, 0, 0), (1, 0, 0), (-1, 0, 0), (0, 1, 0), (0, -1, 0), (0, 0, 1), (0, 0, -1), (1, 1, 0), (-1, -1, 0), (1, -1, 0), (-1, 1, 0), (1, 0, 1), (-1, 0, -1), (1, 0, -1), (-1, 0, 1), (0, 1, 1), (0, -1, -1), (0, 1, -1), (0, -1, 1))


def solid_tile_grid(key):
    heights = jnp.maximum(jax.random.randint(jax.random.fold_in(key, 11), (NX // TILE, NY // TILE), -4, Z), 0)
    level = lax.broadcasted_iota(jnp.int32, (NX // TILE, Z, NY // TILE), 1)
    return (level < heights[:, None, :]).astype(jnp.int32)


def draw_solid_tiles(key, part):
    return solid_tile_grid(key)


def draw_link_blocked(key, part):
    tiles = solid_tile_grid(key)
    cells = jnp.repeat(jnp.repeat(tiles, TILE, axis=0), TILE, axis=2)
    flags = []
    for number in range(1, 19):
        speed = lattice_speeds[number]
        target = jnp.roll(cells, (-speed[0], -speed[1]), axis=(0, 2))
        if speed[2] == 1:
            target = jnp.concatenate([target[:, 1:], jnp.ones_like(target[:, :1])], axis=1)
        elif speed[2] == -1:
            target = jnp.concatenate([jnp.ones_like(target[:, :1]), target[:, :-1]], axis=1)
        flags.append(target)
    return jnp.stack(flags).astype(jnp.int32)


def draw_velocity(key, part):
    shape = (STEPS, 3, NX, Z, NY)
    position = lax.broadcasted_iota(jnp.float32, shape, 2) / (NX - 1)
    raw = jnp.clip(jax.random.normal(key, shape, jnp.float32), -3.0, 3.0)
    scale = 0.03 * (1.0 + 2.0 * position)
    return (raw * scale).astype(jnp.bfloat16)


def block_scale(own_key, shape, split, least, largest):
    gain = 1.0
    for dim, parts in split:
        steps = jax.random.uniform(jax.random.fold_in(jax.random.fold_in(own_key, 6), dim), (parts,), jnp.float32, least / len(split), largest / len(split))
        gain = gain * jnp.repeat(jnp.exp(steps), shape[dim] // parts).reshape((-1,) + (1,) * (len(shape) - 1 - dim))
    return gain


def noise(rng, shape, spread, limit, shards=(), dtype=jnp.bfloat16):
    array = spread * jax.random.normal(rng, shape, jnp.float32)
    if shards:
        array = array * block_scale(rng, shape, shards, -0.22, 0.18)
    return jnp.clip(array, -limit, limit).astype(dtype)


def setup_inputs(seed: int = 0) -> dict:
    seeds = jax.random.split(jax.random.key(seed), 5)
    adjoint_in = noise(seeds[0], (Q, NX, Z, NY), 1.0, 6.0, ((1, 16), (3, 32)), jnp.float32)
    velocity = draw_velocity(jax.random.fold_in(seeds[4], 71), 0)
    solid_tiles = draw_solid_tiles(jax.random.fold_in(seeds[4], 71), 0)
    link_blocked = draw_link_blocked(jax.random.fold_in(seeds[4], 71), 0)
    return dict(adjoint_in=adjoint_in, velocity=velocity, solid_tiles=solid_tiles, link_blocked=link_blocked)


lattice_speeds = ((0, 0, 0), (1, 0, 0), (-1, 0, 0), (0, 1, 0), (0, -1, 0), (0, 0, 1), (0, 0, -1), (1, 1, 0), (-1, -1, 0), (1, -1, 0), (-1, 1, 0), (1, 0, 1), (-1, 0, -1), (1, 0, -1), (-1, 0, 1), (0, 1, 1), (0, -1, -1), (0, 1, -1), (0, -1, 1))
lattice_weights = (1.0 / 3.0,) + (1.0 / 18.0,) * 6 + (1.0 / 36.0,) * 12
relax_rate = 1.6
drag_factor = 20.0

def opposite_of(number):
    return number + 1 if number % 2 == 1 else number - 1

def shift_level(field, lift):
    if lift == 1:
        return jnp.concatenate([field[:, 1:], jnp.zeros_like(field[:, :1])], axis=1)
    if lift == -1:
        return jnp.concatenate([jnp.zeros_like(field[:, :1]), field[:, :-1]], axis=1)
    return field

def adjoint_collide(moved, flow, fluid):
    speed_sq = flow[0] * flow[0] + flow[1] * flow[1] + flow[2] * flow[2]
    scalar_part = jnp.zeros_like(speed_sq)
    vector_part = [jnp.zeros_like(speed_sq) for axis_number in range(3)]
    drag_local = jnp.zeros_like(speed_sq)
    for number in range(19):
        speed = lattice_speeds[number]
        along = speed[0] * flow[0] + speed[1] * flow[1] + speed[2] * flow[2]
        weighted = lattice_weights[number] * moved[number]
        scalar_part = scalar_part + weighted * (1.0 + 3.0 * along + 4.5 * along * along - 1.5 * speed_sq)
        for axis_number in range(3):
            vector_part[axis_number] = vector_part[axis_number] + weighted * (3.0 * speed[axis_number] + 9.0 * along * speed[axis_number] - 3.0 * flow[axis_number])
        drag_local = drag_local + 3.0 * weighted * along
    results = []
    for number in range(19):
        speed = lattice_speeds[number]
        projected = scalar_part
        for axis_number in range(3):
            projected = projected + vector_part[axis_number] * (speed[axis_number] - flow[axis_number])
        results.append(fluid * ((1.0 - relax_rate) * moved[number] + relax_rate * projected))
    return (jnp.stack(results), jnp.sum(fluid * drag_local))

def reference(adjoint_in, velocity, solid_tiles, link_blocked):
    solid = jnp.repeat(jnp.repeat(solid_tiles, TILE, axis=0), TILE, axis=2)
    fluid = 1.0 - solid.astype(jnp.float32)
    state = adjoint_in
    total = jnp.zeros((), jnp.float32)
    for adjoint_step in range(STEPS):
        flow = velocity[adjoint_step].astype(jnp.float32)
        moved = [state[0]]
        for number in range(1, 19):
            speed = lattice_speeds[number]
            source = jnp.roll(state[number], (-speed[0], -speed[1]), axis=(0, 2))
            source = shift_level(source, speed[2])
            bounced = state[opposite_of(number)] + 2.0 * speed[0]
            moved.append(jnp.where(link_blocked[number - 1] == 1, bounced, source))
        state, drag_local = adjoint_collide(moved, flow, fluid)
        total = total + drag_local
    scale = drag_factor / math.sqrt(NX * NY * Z)
    return (state, (-scale * total).reshape(1))
```

```python
import functools
import math

import jax
import jax.numpy as jnp
from jax import lax
from jax.experimental import pallas as pl
from jax.experimental.pallas import tpu as pltpu
from jax.sharding import PartitionSpec as P

MESH = pl.DeviceIdType.MESH

TILE = 4
STEPS = 2


lattice_speeds = (
    (0, 0, 0),
    (1, 0, 0),
    (-1, 0, 0),
    (0, 1, 0),
    (0, -1, 0),
    (0, 0, 1),
    (0, 0, -1),
    (1, 1, 0),
    (-1, -1, 0),
    (1, -1, 0),
    (-1, 1, 0),
    (1, 0, 1),
    (-1, 0, -1),
    (1, 0, -1),
    (-1, 0, 1),
    (0, 1, 1),
    (0, -1, -1),
    (0, 1, -1),
    (0, -1, 1),
)
lattice_weights = (1.0 / 3.0,) + (1.0 / 18.0,) * 6 + (1.0 / 36.0,) * 12
relax_rate = 1.6
drag_factor = 20.0


def with_halo(block, sides, width):
    for axis, dim in sides:
        count = lax.axis_size(axis)
        forward = [(i, i + 1) for i in range(count - 1)]
        forward.append((count - 1, 0))
        backward = [(target, source) for source, target in forward]
        low = lax.ppermute(
            lax.slice_in_dim(block, block.shape[dim] - width, None, axis=dim), axis, forward
        )
        high = lax.ppermute(lax.slice_in_dim(block, 0, width, axis=dim), axis, backward)
        block = jnp.concatenate([low, block, high], axis=dim)
    return block


def opposite_of(number):
    return number + 1 if number % 2 == 1 else number - 1


def shift_level(field, lift):
    if lift == 1:
        return jnp.concatenate([field[:, 1:], jnp.zeros_like(field[:, :1])], axis=1)
    if lift == -1:
        return jnp.concatenate([jnp.zeros_like(field[:, :1]), field[:, :-1]], axis=1)
    return field


def adjoint_collide(moved, flow, fluid):
    speed_sq = flow[0] * flow[0] + flow[1] * flow[1] + flow[2] * flow[2]
    scalar_part = jnp.zeros_like(speed_sq)
    vector_part = [jnp.zeros_like(speed_sq) for axis_number in range(3)]
    drag_local = jnp.zeros_like(speed_sq)
    for number in range(19):
        speed = lattice_speeds[number]
        along = speed[0] * flow[0] + speed[1] * flow[1] + speed[2] * flow[2]
        weighted = lattice_weights[number] * moved[number]
        scalar_part = scalar_part + weighted * (
            1.0 + 3.0 * along + 4.5 * along * along - 1.5 * speed_sq
        )
        for axis_number in range(3):
            vector_part[axis_number] = vector_part[axis_number] + weighted * (
                3.0 * speed[axis_number]
                + 9.0 * along * speed[axis_number]
                - 3.0 * flow[axis_number]
            )
        drag_local = drag_local + 3.0 * weighted * along
    results = []
    for number in range(19):
        speed = lattice_speeds[number]
        projected = scalar_part
        for axis_number in range(3):
            projected = projected + vector_part[axis_number] * (
                speed[axis_number] - flow[axis_number]
            )
        results.append(fluid * ((1.0 - relax_rate) * moved[number] + relax_rate * projected))
    return (jnp.stack(results), fluid * drag_local)


def stream_back(padded, centre, blocked, span_x, span_y):
    moved = [centre[0]]
    for number in range(1, 19):
        speed = lattice_speeds[number]
        source = padded[
            number, 1 + speed[0] : 1 + speed[0] + span_x, :, 1 + speed[1] : 1 + speed[1] + span_y
        ]
        source = shift_level(source, speed[2])
        bounced = centre[opposite_of(number)] + 2.0 * speed[0]
        moved.append(jnp.where(blocked[number - 1] == 1, bounced, source))
    return moved


def sum_kernel(nx, ny, part_ref, out_ref, row_buf, col_buf, row_sum, send_a, recv_a, send_b, recv_b):
    me_x = lax.axis_index("gx")
    me_y = lax.axis_index("gy")
    barrier = pltpu.get_barrier_semaphore()
    for k in range(1, ny):
        peer = lax.rem(me_y + k, ny)
        pl.semaphore_signal(barrier, inc=1, device_id=(me_x, peer), device_id_type=MESH)
    for k in range(1, nx):
        peer = lax.rem(me_x + k, nx)
        pl.semaphore_signal(barrier, inc=1, device_id=(peer, me_y), device_id_type=MESH)
    pl.semaphore_wait(barrier, nx + ny - 2)

    row_copies = []
    for k in range(1, ny):
        peer = lax.rem(me_y + k, ny)
        copy = pltpu.make_async_remote_copy(
            src_ref=part_ref,
            dst_ref=row_buf.at[me_y],
            send_sem=send_a.at[k],
            recv_sem=recv_a.at[k],
            device_id=(me_x, peer),
            device_id_type=MESH,
        )
        copy.start()
        row_copies.append(copy)
    row_buf[me_y] = part_ref[...]
    for copy in row_copies:
        copy.wait()
    total = row_buf[0]
    for j in range(1, ny):
        total = total + row_buf[j]
    row_sum[...] = total

    col_copies = []
    for k in range(1, nx):
        peer = lax.rem(me_x + k, nx)
        copy = pltpu.make_async_remote_copy(
            src_ref=row_sum,
            dst_ref=col_buf.at[me_x],
            send_sem=send_b.at[k],
            recv_sem=recv_b.at[k],
            device_id=(peer, me_y),
            device_id_type=MESH,
        )
        copy.start()
        col_copies.append(copy)
    col_buf[me_x] = total
    for copy in col_copies:
        copy.wait()
    total = col_buf[0]
    for j in range(1, nx):
        total = total + col_buf[j]
    out_ref[...] = total


def mesh_sum(value):
    nx = lax.axis_size("gx")
    ny = lax.axis_size("gy")
    part = jnp.broadcast_to(value, (8, 128)).astype(jnp.float32)
    out = pl.pallas_call(
        functools.partial(sum_kernel, nx, ny),
        out_shape=jax.ShapeDtypeStruct((8, 128), jnp.float32),
        in_specs=[pl.BlockSpec(memory_space=pltpu.VMEM)],
        out_specs=pl.BlockSpec(memory_space=pltpu.VMEM),
        scratch_shapes=[
            pltpu.VMEM((ny, 8, 128), jnp.float32),
            pltpu.VMEM((nx, 8, 128), jnp.float32),
            pltpu.VMEM((8, 128), jnp.float32),
            pltpu.SemaphoreType.DMA((ny,)),
            pltpu.SemaphoreType.DMA((ny,)),
            pltpu.SemaphoreType.DMA((nx,)),
            pltpu.SemaphoreType.DMA((nx,)),
        ],
        compiler_params=pltpu.CompilerParams(collective_id=0, has_side_effects=True),
    )(part)
    return out[0, 0]


def per_device(adjoint_in, velocity, solid_tiles, link_blocked):
    rows_x = adjoint_in.shape[1]
    rows_y = adjoint_in.shape[3]
    levels = adjoint_in.shape[2]
    solid = jnp.repeat(jnp.repeat(solid_tiles, TILE, axis=0), TILE, axis=2)
    fluid = 1.0 - solid.astype(jnp.float32)
    state = adjoint_in
    step_terms = []
    for adjoint_step in range(STEPS):
        flow = velocity[adjoint_step].astype(jnp.float32)
        padded = with_halo(state, (("gx", 1), ("gy", 3)), 1)
        moved = stream_back(padded, state, link_blocked, rows_x, rows_y)
        state, drag_field = adjoint_collide(moved, flow, fluid)
        step_terms.append(jnp.sum(drag_field))
    local = step_terms[0]
    for adjoint_step in range(1, STEPS):
        local = local + step_terms[adjoint_step]
    total = mesh_sum(local)
    cell_count = rows_x * lax.axis_size("gx") * rows_y * lax.axis_size("gy") * levels
    scale = drag_factor / math.sqrt(cell_count)
    return (state, (-scale * total).reshape(1))


def solution(mesh):
    placed = (
        P(None, "gx", None, "gy"),
        P(None, None, "gx", None, "gy"),
        P("gx", None, "gy"),
        P(None, "gx", None, "gy"),
    )
    return jax.shard_map(
        per_device,
        mesh=mesh,
        in_specs=placed,
        out_specs=(P(None, "gx", None, "gy"), P()),
        check_vma=False,
    )
```

```python
import functools
import math

import jax
import jax.numpy as jnp
from jax import lax
from jax.experimental import pallas as pl
from jax.experimental.pallas import tpu as pltpu
from jax.sharding import PartitionSpec as P

MESH = pl.DeviceIdType.MESH
TILE = 4
STEPS = 2

lattice_speeds = (
    (0, 0, 0),
    (1, 0, 0),
    (-1, 0, 0),
    (0, 1, 0),
    (0, -1, 0),
    (0, 0, 1),
    (0, 0, -1),
    (1, 1, 0),
    (-1, -1, 0),
    (1, -1, 0),
    (-1, 1, 0),
    (1, 0, 1),
    (-1, 0, -1),
    (1, 0, -1),
    (-1, 0, 1),
    (0, 1, 1),
    (0, -1, -1),
    (0, 1, -1),
    (0, -1, 1),
)
lattice_weights = (1.0 / 3.0,) + (1.0 / 18.0,) * 6 + (1.0 / 36.0,) * 12
relax_rate = 1.6
drag_factor = 20.0

FROM_X_HIGH = tuple(i for i in range(19) if lattice_speeds[i][0] == 1)
FROM_X_LOW = tuple(i for i in range(19) if lattice_speeds[i][0] == -1)
FROM_Y_HIGH = tuple(i for i in range(19) if lattice_speeds[i][1] == 1)
FROM_Y_LOW = tuple(i for i in range(19) if lattice_speeds[i][1] == -1)
CORNERS = tuple(i for i in range(19) if lattice_speeds[i][0] != 0 and lattice_speeds[i][1] != 0)


def opposite_of(number):
    return number + 1 if number % 2 == 1 else number - 1


def along_of(speed, flow):
    along = None
    for axis in range(3):
        if speed[axis] == 0:
            continue
        term = flow[axis] if speed[axis] == 1 else -flow[axis]
        along = term if along is None else along + term
    return along


def collide(moved, flow, fluid):
    speed_sq = flow[0] * flow[0] + flow[1] * flow[1] + flow[2] * flow[2]
    scalar_part = None
    vector_part = [None, None, None]
    drag_local = None
    for number in range(19):
        speed = lattice_speeds[number]
        weighted = lattice_weights[number] * moved[number]
        along = along_of(speed, flow)
        if along is None:
            scalar_term = weighted * (1.0 - 1.5 * speed_sq)
        else:
            scalar_term = weighted * (1.0 + 3.0 * along + 4.5 * along * along - 1.5 * speed_sq)
            drag_term = 3.0 * weighted * along
            drag_local = drag_term if drag_local is None else drag_local + drag_term
        scalar_part = scalar_term if scalar_part is None else scalar_part + scalar_term
        for axis in range(3):
            if speed[axis] == 0:
                term = weighted * (-3.0 * flow[axis])
            else:
                term = weighted * (3.0 * speed[axis] + 9.0 * along * speed[axis] - 3.0 * flow[axis])
            vector_part[axis] = term if vector_part[axis] is None else vector_part[axis] + term
    results = []
    for number in range(19):
        speed = lattice_speeds[number]
        projected = scalar_part
        for axis in range(3):
            projected = projected + vector_part[axis] * (speed[axis] - flow[axis])
        results.append(fluid * ((1.0 - relax_rate) * moved[number] + relax_rate * projected))
    return results, fluid * drag_local


def lbm_kernel(nx, ny, rows, lam_ref, vel_ref, blk_ref, fluid_ref, out_ref, drag_ref,
               moved, state, xhi, xlo, yhi, ylo, corner, part, row_buf, col_buf, row_sum,
               ssem, rsem, sum_send_a, sum_recv_a, sum_send_b, sum_recv_b):
    me_x = lax.axis_index("gx")
    me_y = lax.axis_index("gy")
    up_x = lax.rem(me_x + 1, nx)
    dn_x = lax.rem(me_x + nx - 1, nx)
    up_y = lax.rem(me_y + 1, ny)
    dn_y = lax.rem(me_y + ny - 1, ny)

    barrier = pltpu.get_barrier_semaphore()
    for k in range(1, ny):
        pl.semaphore_signal(barrier, inc=1, device_id=(me_x, lax.rem(me_y + k, ny)), device_id_type=MESH)
    for k in range(1, nx):
        pl.semaphore_signal(barrier, inc=1, device_id=(lax.rem(me_x + k, nx), me_y), device_id_type=MESH)
    for dev in ((up_x, up_y), (up_x, dn_y), (dn_x, up_y), (dn_x, dn_y)):
        pl.semaphore_signal(barrier, inc=1, device_id=dev, device_id_type=MESH)
    pl.semaphore_wait(barrier, nx + ny + 2)

    row8 = lax.broadcasted_iota(jnp.int32, (8, 128), 0)
    lane = lax.broadcasted_iota(jnp.int32, (rows, 128), 1)
    level = lax.rem(lax.broadcasted_iota(jnp.int32, (rows, 128), 0), 4)
    top = rows - 8
    drag_acc = jnp.zeros((8, 128), jnp.float32)

    for step in range(STEPS):
        src = lam_ref if step == 0 else state
        plan = []
        for j, number in enumerate(FROM_X_HIGH):
            plan.append((src.at[number, pl.ds(0, 8)], xhi.at[step, j], (dn_x, me_y)))
        for j, number in enumerate(FROM_X_LOW):
            plan.append((src.at[number, pl.ds(top, 8)], xlo.at[step, j], (up_x, me_y)))
        for j, number in enumerate(FROM_Y_HIGH):
            plan.append((src.at[number], yhi.at[step, j], (me_x, dn_y)))
        for j, number in enumerate(FROM_Y_LOW):
            plan.append((src.at[number], ylo.at[step, j], (me_x, up_y)))
        for j, number in enumerate(CORNERS):
            cx, cy, _ = lattice_speeds[number]
            rows_at = pl.ds(0, 8) if cx == 1 else pl.ds(top, 8)
            dev_x = dn_x if cx == 1 else up_x
            dev_y = dn_y if cy == 1 else up_y
            plan.append((src.at[number, rows_at], corner.at[step, j], (dev_x, dev_y)))
        copies = []
        for k, (from_ref, to_ref, dev) in enumerate(plan):
            copy = pltpu.make_async_remote_copy(
                src_ref=from_ref, dst_ref=to_ref, send_sem=ssem.at[step, k],
                recv_sem=rsem.at[step, k], device_id=dev, device_id_type=MESH)
            copy.start()
            copies.append(copy)
        for copy in copies:
            copy.wait()

        def patch_x(block, cx, tile):
            if cx == 1:
                head = jnp.where(row8 < 4, tile, block[0:8])
                return jnp.concatenate([head, block[8:]], axis=0)
            tail = jnp.where(row8 >= 4, tile, block[top:])
            return jnp.concatenate([block[:top], tail], axis=0)

        moved[0] = src[0]
        for number in range(1, 19):
            cx, cy, cz = lattice_speeds[number]
            own = src[number]
            if cx == 1:
                own = patch_x(own, cx, xhi[step, FROM_X_HIGH.index(number)])
            elif cx == -1:
                own = patch_x(own, cx, xlo[step, FROM_X_LOW.index(number)])
            if cy != 0:
                if cy == 1:
                    side = yhi[step, FROM_Y_HIGH.index(number)]
                else:
                    side = ylo[step, FROM_Y_LOW.index(number)]
                if cx != 0:
                    side = patch_x(side, cx, corner[step, CORNERS.index(number)])
                edge = 0 if cy == 1 else 127
                own = jnp.where(lane == edge, side, own)
            shift = 4 * cx + cz
            if shift % rows:
                own = pltpu.roll(own, (-shift) % rows, 0)
            if cy != 0:
                own = pltpu.roll(own, (-cy) % 128, 1)
            if cz == 1:
                own = jnp.where(level == 3, 0.0, own)
            elif cz == -1:
                own = jnp.where(level == 0, 0.0, own)
            bounced = src[opposite_of(number)] + 2.0 * cx
            moved[number] = jnp.where(blk_ref[number - 1] == 1, bounced, own)

        dest = out_ref if step == STEPS - 1 else state

        def chunk(c, acc):
            at = pl.ds(pl.multiple_of(c * 8, 8), 8)
            flow = [vel_ref[step, axis, at] for axis in range(3)]
            mu = [moved[number, at] for number in range(19)]
            fresh, drag = collide(mu, flow, fluid_ref[at])
            for number in range(19):
                dest[number, at] = fresh[number]
            return acc + drag

        drag_acc = lax.fori_loop(0, rows // 8, chunk, drag_acc)

    part[...] = jnp.broadcast_to(jnp.sum(drag_acc), (8, 128))

    row_copies = []
    for k in range(1, ny):
        copy = pltpu.make_async_remote_copy(
            src_ref=part, dst_ref=row_buf.at[me_y], send_sem=sum_send_a.at[k],
            recv_sem=sum_recv_a.at[k], device_id=(me_x, lax.rem(me_y + k, ny)),
            device_id_type=MESH)
        copy.start()
        row_copies.append(copy)
    row_buf[me_y] = part[...]
    for copy in row_copies:
        copy.wait()
    total = row_buf[0]
    for j in range(1, ny):
        total = total + row_buf[j]
    row_sum[...] = total

    col_copies = []
    for k in range(1, nx):
        copy = pltpu.make_async_remote_copy(
            src_ref=row_sum, dst_ref=col_buf.at[me_x], send_sem=sum_send_b.at[k],
            recv_sem=sum_recv_b.at[k], device_id=(lax.rem(me_x + k, nx), me_y),
            device_id_type=MESH)
        copy.start()
        col_copies.append(copy)
    col_buf[me_x] = total
    for copy in col_copies:
        copy.wait()
    total = col_buf[0]
    for j in range(1, nx):
        total = total + col_buf[j]
    drag_ref[...] = total


def per_device(adjoint_in, velocity, solid_tiles, link_blocked):
    nx = lax.axis_size("gx")
    ny = lax.axis_size("gy")
    q, rows_x, levels, rows_y = adjoint_in.shape
    rows = rows_x * levels
    lam = adjoint_in.reshape(q, rows, rows_y)
    flow = velocity.astype(jnp.float32).reshape(STEPS, 3, rows, rows_y)
    blocked = link_blocked.reshape(q - 1, rows, rows_y)
    solid = jnp.repeat(jnp.repeat(solid_tiles, TILE, axis=0), TILE, axis=2)
    fluid = (1.0 - solid.astype(jnp.float32)).reshape(rows, rows_y)
    n_copies = len(FROM_X_HIGH) + len(FROM_X_LOW) + len(FROM_Y_HIGH) + len(FROM_Y_LOW) + len(CORNERS)
    vmem = pl.BlockSpec(memory_space=pltpu.VMEM)
    state, drag = pl.pallas_call(
        functools.partial(lbm_kernel, nx, ny, rows),
        out_shape=(
            jax.ShapeDtypeStruct((q, rows, rows_y), jnp.float32),
            jax.ShapeDtypeStruct((8, 128), jnp.float32),
        ),
        in_specs=[vmem] * 4,
        out_specs=(vmem, vmem),
        scratch_shapes=[
            pltpu.VMEM((q, rows, rows_y), jnp.float32),
            pltpu.VMEM((q, rows, rows_y), jnp.float32),
            pltpu.VMEM((STEPS, len(FROM_X_HIGH), 8, rows_y), jnp.float32),
            pltpu.VMEM((STEPS, len(FROM_X_LOW), 8, rows_y), jnp.float32),
            pltpu.VMEM((STEPS, len(FROM_Y_HIGH), rows, rows_y), jnp.float32),
            pltpu.VMEM((STEPS, len(FROM_Y_LOW), rows, rows_y), jnp.float32),
            pltpu.VMEM((STEPS, len(CORNERS), 8, rows_y), jnp.float32),
            pltpu.VMEM((8, 128), jnp.float32),
            pltpu.VMEM((ny, 8, 128), jnp.float32),
            pltpu.VMEM((nx, 8, 128), jnp.float32),
            pltpu.VMEM((8, 128), jnp.float32),
            pltpu.SemaphoreType.DMA((STEPS, n_copies)),
            pltpu.SemaphoreType.DMA((STEPS, n_copies)),
            pltpu.SemaphoreType.DMA((ny,)),
            pltpu.SemaphoreType.DMA((ny,)),
            pltpu.SemaphoreType.DMA((nx,)),
            pltpu.SemaphoreType.DMA((nx,)),
        ],
        compiler_params=pltpu.CompilerParams(collective_id=0, has_side_effects=True),
    )(lam, flow, blocked, fluid)
    cell_count = rows_x * nx * rows_y * ny * levels
    scale = drag_factor / math.sqrt(cell_count)
    return (state.reshape(q, rows_x, levels, rows_y), (-scale * drag[0, 0]).reshape(1))


def solution(mesh):
    placed = (
        P(None, "gx", None, "gy"),
        P(None, None, "gx", None, "gy"),
        P("gx", None, "gy"),
        P(None, "gx", None, "gy"),
    )
    return jax.shard_map(
        per_device,
        mesh=mesh,
        in_specs=placed,
        out_specs=(P(None, "gx", None, "gy"), P()),
        check_vma=False,
    )
```

```python
import functools
import math

import jax
import jax.numpy as jnp
from jax import lax
from jax.experimental import pallas as pl
from jax.experimental.pallas import tpu as pltpu
from jax.sharding import PartitionSpec as P

MESH = pl.DeviceIdType.MESH
TILE = 4
STEPS = 2

lattice_speeds = (
    (0, 0, 0),
    (1, 0, 0),
    (-1, 0, 0),
    (0, 1, 0),
    (0, -1, 0),
    (0, 0, 1),
    (0, 0, -1),
    (1, 1, 0),
    (-1, -1, 0),
    (1, -1, 0),
    (-1, 1, 0),
    (1, 0, 1),
    (-1, 0, -1),
    (1, 0, -1),
    (-1, 0, 1),
    (0, 1, 1),
    (0, -1, -1),
    (0, 1, -1),
    (0, -1, 1),
)
lattice_weights = (1.0 / 3.0,) + (1.0 / 18.0,) * 6 + (1.0 / 36.0,) * 12
relax_rate = 1.6
drag_factor = 20.0


def crossing(speeds):
    return (
        tuple(n for n, c in speeds if c[0] == 1),
        tuple(n for n, c in speeds if c[0] == -1),
        tuple(n for n, c in speeds if c[1] == 1),
        tuple(n for n, c in speeds if c[1] == -1),
        tuple(n for n, c in speeds if c[0] != 0 and c[1] != 0),
    )


MOVING = tuple((n, lattice_speeds[n]) for n in range(1, 19))
REVERSED = tuple((n, tuple(-v for v in lattice_speeds[n])) for n in range(1, 19))
N_COPIES = sum(len(s) for s in crossing(MOVING))


def opposite_of(number):
    return number + 1 if number % 2 == 1 else number - 1


def along_of(speed, flow):
    along = None
    for axis in range(3):
        if speed[axis] == 0:
            continue
        term = flow[axis] if speed[axis] == 1 else -flow[axis]
        along = term if along is None else along + term
    return along


def collide(moved, flow, fluid):
    speed_sq = flow[0] * flow[0] + flow[1] * flow[1] + flow[2] * flow[2]
    scalar_part = None
    vector_part = [None, None, None]
    drag_local = None
    for number in range(19):
        speed = lattice_speeds[number]
        weighted = lattice_weights[number] * moved[number]
        along = along_of(speed, flow)
        if along is None:
            scalar_term = weighted * (1.0 - 1.5 * speed_sq)
        else:
            scalar_term = weighted * (1.0 + 3.0 * along + 4.5 * along * along - 1.5 * speed_sq)
            drag_term = 3.0 * weighted * along
            drag_local = drag_term if drag_local is None else drag_local + drag_term
        scalar_part = scalar_term if scalar_part is None else scalar_part + scalar_term
        for axis in range(3):
            if speed[axis] == 0:
                term = weighted * (-3.0 * flow[axis])
            else:
                term = weighted * (3.0 * speed[axis] + 9.0 * along * speed[axis] - 3.0 * flow[axis])
            vector_part[axis] = term if vector_part[axis] is None else vector_part[axis] + term
    results = []
    for number in range(19):
        speed = lattice_speeds[number]
        projected = scalar_part
        for axis in range(3):
            projected = projected + vector_part[axis] * (speed[axis] - flow[axis])
        results.append(fluid * ((1.0 - relax_rate) * moved[number] + relax_rate * projected))
    return results, fluid * drag_local


def send_plan(sets, speeds, field, bufs, top, near):
    up_x, dn_x, up_y, dn_y, me_x, me_y = near
    x_high, x_low, y_high, y_low, corners = sets
    xhi, xlo, yhi, ylo, corner = bufs
    plan = []
    for j, n in enumerate(x_high):
        plan.append((field(n).at[pl.ds(0, 8)], xhi.at[j], (dn_x, me_y)))
    for j, n in enumerate(x_low):
        plan.append((field(n).at[pl.ds(top, 8)], xlo.at[j], (up_x, me_y)))
    for j, n in enumerate(y_high):
        plan.append((field(n), yhi.at[j], (me_x, dn_y)))
    for j, n in enumerate(y_low):
        plan.append((field(n), ylo.at[j], (me_x, up_y)))
    for j, n in enumerate(corners):
        cx, cy, _ = speeds[n]
        rows_at = pl.ds(0, 8) if cx == 1 else pl.ds(top, 8)
        dev_x = dn_x if cx == 1 else up_x
        dev_y = dn_y if cy == 1 else up_y
        plan.append((field(n).at[rows_at], corner.at[j], (dev_x, dev_y)))
    return plan


def start_copies(plan, send_sems, recv_sems):
    copies = []
    for k, (from_ref, to_ref, dev) in enumerate(plan):
        copy = pltpu.make_async_remote_copy(
            src_ref=from_ref, dst_ref=to_ref, send_sem=send_sems.at[k],
            recv_sem=recv_sems.at[k], device_id=dev, device_id_type=MESH)
        copy.start()
        copies.append(copy)
    return copies


def shifted(own, speed, n, sets, bufs, rows):
    x_high, x_low, y_high, y_low, corners = sets
    xhi, xlo, yhi, ylo, corner = bufs
    cx, cy, cz = speed
    top = rows - 8
    row8 = lax.broadcasted_iota(jnp.int32, (8, 128), 0)
    lane = lax.broadcasted_iota(jnp.int32, (rows, 128), 1)
    level = lax.rem(lax.broadcasted_iota(jnp.int32, (rows, 128), 0), 4)

    def patch_x(block, tile):
        if cx == 1:
            head = jnp.where(row8 < 4, tile, block[0:8])
            return jnp.concatenate([head, block[8:]], axis=0)
        tail = jnp.where(row8 >= 4, tile, block[top:])
        return jnp.concatenate([block[:top], tail], axis=0)

    if cx == 1:
        own = patch_x(own, xhi[x_high.index(n)])
    elif cx == -1:
        own = patch_x(own, xlo[x_low.index(n)])
    if cy != 0:
        side = yhi[y_high.index(n)] if cy == 1 else ylo[y_low.index(n)]
        if cx != 0:
            side = patch_x(side, corner[corners.index(n)])
        edge = 0 if cy == 1 else 127
        own = jnp.where(lane == edge, side, own)
    shift = 4 * cx + cz
    if shift % rows:
        own = pltpu.roll(own, (-shift) % rows, 0)
    if cy != 0:
        own = pltpu.roll(own, (-cy) % 128, 1)
    if cz == 1:
        own = jnp.where(level == 3, 0.0, own)
    elif cz == -1:
        own = jnp.where(level == 0, 0.0, own)
    return own


def drag_weight(number, flow, fluid):
    return (3.0 * lattice_weights[number]) * along_of(lattice_speeds[number], flow) * fluid


def lbm_kernel(nx, ny, rows, lam_ref, vel_ref, blk_ref, fluid_ref, out_ref, drag_ref,
               moved, state, hfield, xhi, xlo, yhi, ylo, corner, hxhi, hxlo, hyhi, hylo, hcorner,
               part, row_buf, col_buf, row_sum,
               ssem, rsem, hsend, hrecv, sum_send_a, sum_recv_a, sum_send_b, sum_recv_b):
    me_x = lax.axis_index("gx")
    me_y = lax.axis_index("gy")
    up_x = lax.rem(me_x + 1, nx)
    dn_x = lax.rem(me_x + nx - 1, nx)
    up_y = lax.rem(me_y + 1, ny)
    dn_y = lax.rem(me_y + ny - 1, ny)
    near = (up_x, dn_x, up_y, dn_y, me_x, me_y)
    top = rows - 8

    barrier = pltpu.get_barrier_semaphore()
    for k in range(1, ny):
        pl.semaphore_signal(barrier, inc=1, device_id=(me_x, lax.rem(me_y + k, ny)), device_id_type=MESH)
    for k in range(1, nx):
        pl.semaphore_signal(barrier, inc=1, device_id=(lax.rem(me_x + k, nx), me_y), device_id_type=MESH)
    for dev in ((up_x, up_y), (up_x, dn_y), (dn_x, up_y), (dn_x, dn_y)):
        pl.semaphore_signal(barrier, inc=1, device_id=dev, device_id_type=MESH)

    last_flow = [vel_ref[STEPS - 1, axis] for axis in range(3)]
    fluid_all = fluid_ref[...]
    for number in range(1, 19):
        weight = drag_weight(number, last_flow, fluid_all)
        hfield[number - 1] = jnp.where(blk_ref[number - 1] == 1, 0.0, weight)

    pl.semaphore_wait(barrier, nx + ny + 2)

    lam_sets = crossing(MOVING)
    h_sets = crossing(REVERSED)
    h_speeds = dict(REVERSED)
    lam_speeds = dict(MOVING)
    h_bufs = (hxhi, hxlo, hyhi, hylo, hcorner)
    h_copies = None
    drag_acc = jnp.zeros((8, 128), jnp.float32)

    for step in range(STEPS):
        src = lam_ref if step == 0 else state
        bufs = (xhi.at[step], xlo.at[step], yhi.at[step], ylo.at[step], corner.at[step])
        plan = send_plan(lam_sets, lam_speeds, lambda n: src.at[n], bufs, top, near)
        copies = start_copies(plan, ssem.at[step], rsem.at[step])
        if step == 0:
            h_plan = send_plan(h_sets, h_speeds, lambda n: hfield.at[n - 1], h_bufs, top, near)
            h_copies = start_copies(h_plan, hsend, hrecv)
        if step == STEPS - 1:
            for copy in h_copies:
                copy.wait()
            total = drag_acc
            for number in range(1, 19):
                gathered = shifted(hfield[number - 1], h_speeds[number], number, h_sets, h_bufs, rows)
                total = total + jnp.sum((src[number] * gathered).reshape(rows // 8, 8, 128), axis=0)
            for number in range(1, 19):
                cx = lattice_speeds[number][0]
                weight = drag_weight(number, last_flow, fluid_all)
                bounced = jnp.where(blk_ref[number - 1] == 1, src[opposite_of(number)] + 2.0 * cx, 0.0)
                total = total + jnp.sum((weight * bounced).reshape(rows // 8, 8, 128), axis=0)
            part[...] = jnp.broadcast_to(jnp.sum(total), (8, 128))
            row_copies = []
            for k in range(1, ny):
                copy = pltpu.make_async_remote_copy(
                    src_ref=part, dst_ref=row_buf.at[me_y], send_sem=sum_send_a.at[k],
                    recv_sem=sum_recv_a.at[k], device_id=(me_x, lax.rem(me_y + k, ny)),
                    device_id_type=MESH)
                copy.start()
                row_copies.append(copy)
            row_buf[me_y] = part[...]
        for copy in copies:
            copy.wait()

        moved[0] = src[0]
        for number in range(1, 19):
            source = shifted(src[number], lam_speeds[number], number, lam_sets, bufs, rows)
            bounced = src[opposite_of(number)] + 2.0 * lam_speeds[number][0]
            moved[number] = jnp.where(blk_ref[number - 1] == 1, bounced, source)

        if step == STEPS - 1:
            for copy in row_copies:
                copy.wait()
            total = row_buf[0]
            for j in range(1, ny):
                total = total + row_buf[j]
            row_sum[...] = total
            col_copies = []
            for k in range(1, nx):
                copy = pltpu.make_async_remote_copy(
                    src_ref=row_sum, dst_ref=col_buf.at[me_x], send_sem=sum_send_b.at[k],
                    recv_sem=sum_recv_b.at[k], device_id=(lax.rem(me_x + k, nx), me_y),
                    device_id_type=MESH)
                copy.start()
                col_copies.append(copy)
            col_buf[me_x] = total

        dest = out_ref if step == STEPS - 1 else state

        def chunk(c, acc):
            at = pl.ds(pl.multiple_of(c * 8, 8), 8)
            flow = [vel_ref[step, axis, at] for axis in range(3)]
            mu = [moved[number, at] for number in range(19)]
            fresh, drag = collide(mu, flow, fluid_ref[at])
            for number in range(19):
                dest[number, at] = fresh[number]
            return acc + drag

        if step < STEPS - 1:
            drag_acc = lax.fori_loop(0, rows // 8, chunk, drag_acc)
        else:
            lax.fori_loop(0, rows // 8, chunk, drag_acc)

    for copy in col_copies:
        copy.wait()
    total = col_buf[0]
    for j in range(1, nx):
        total = total + col_buf[j]
    drag_ref[...] = total


def per_device(adjoint_in, velocity, solid_tiles, link_blocked):
    nx = lax.axis_size("gx")
    ny = lax.axis_size("gy")
    q, rows_x, levels, rows_y = adjoint_in.shape
    rows = rows_x * levels
    lam = adjoint_in.reshape(q, rows, rows_y)
    flow = velocity.astype(jnp.float32).reshape(STEPS, 3, rows, rows_y)
    blocked = link_blocked.reshape(q - 1, rows, rows_y)
    solid = jnp.repeat(jnp.repeat(solid_tiles, TILE, axis=0), TILE, axis=2)
    fluid = (1.0 - solid.astype(jnp.float32)).reshape(rows, rows_y)
    vmem = pl.BlockSpec(memory_space=pltpu.VMEM)
    state, drag = pl.pallas_call(
        functools.partial(lbm_kernel, nx, ny, rows),
        out_shape=(
            jax.ShapeDtypeStruct((q, rows, rows_y), jnp.float32),
            jax.ShapeDtypeStruct((8, 128), jnp.float32),
        ),
        in_specs=[vmem] * 4,
        out_specs=(vmem, vmem),
        scratch_shapes=[
            pltpu.VMEM((q, rows, rows_y), jnp.float32),
            pltpu.VMEM((q, rows, rows_y), jnp.float32),
            pltpu.VMEM((q - 1, rows, rows_y), jnp.float32),
        ]
        + [
            pltpu.VMEM((STEPS, len(s), rows if face >= 2 and face < 4 else 8, rows_y), jnp.float32)
            for face, s in enumerate(crossing(MOVING))
        ]
        + [
            pltpu.VMEM((len(s), rows if face >= 2 and face < 4 else 8, rows_y), jnp.float32)
            for face, s in enumerate(crossing(REVERSED))
        ]
        + [
            pltpu.VMEM((8, 128), jnp.float32),
            pltpu.VMEM((ny, 8, 128), jnp.float32),
            pltpu.VMEM((nx, 8, 128), jnp.float32),
            pltpu.VMEM((8, 128), jnp.float32),
            pltpu.SemaphoreType.DMA((STEPS, N_COPIES)),
            pltpu.SemaphoreType.DMA((STEPS, N_COPIES)),
            pltpu.SemaphoreType.DMA((N_COPIES,)),
            pltpu.SemaphoreType.DMA((N_COPIES,)),
            pltpu.SemaphoreType.DMA((ny,)),
            pltpu.SemaphoreType.DMA((ny,)),
            pltpu.SemaphoreType.DMA((nx,)),
            pltpu.SemaphoreType.DMA((nx,)),
        ],
        compiler_params=pltpu.CompilerParams(collective_id=0, has_side_effects=True),
    )(lam, flow, blocked, fluid)
    cell_count = rows_x * nx * rows_y * ny * levels
    scale = drag_factor / math.sqrt(cell_count)
    return (state.reshape(q, rows_x, levels, rows_y), (-scale * drag[0, 0]).reshape(1))


def solution(mesh):
    placed = (
        P(None, "gx", None, "gy"),
        P(None, None, "gx", None, "gy"),
        P("gx", None, "gy"),
        P(None, "gx", None, "gy"),
    )
    return jax.shard_map(
        per_device,
        mesh=mesh,
        in_specs=placed,
        out_specs=(P(None, "gx", None, "gy"), P()),
        check_vma=False,
    )
```

```python
import functools
import math

import jax
import jax.numpy as jnp
from jax import lax
from jax.experimental import pallas as pl
from jax.experimental.pallas import tpu as pltpu
from jax.sharding import PartitionSpec as P

MESH = pl.DeviceIdType.MESH
TILE = 4
STEPS = 2

lattice_speeds = (
    (0, 0, 0),
    (1, 0, 0),
    (-1, 0, 0),
    (0, 1, 0),
    (0, -1, 0),
    (0, 0, 1),
    (0, 0, -1),
    (1, 1, 0),
    (-1, -1, 0),
    (1, -1, 0),
    (-1, 1, 0),
    (1, 0, 1),
    (-1, 0, -1),
    (1, 0, -1),
    (-1, 0, 1),
    (0, 1, 1),
    (0, -1, -1),
    (0, 1, -1),
    (0, -1, 1),
)
lattice_weights = (1.0 / 3.0,) + (1.0 / 18.0,) * 6 + (1.0 / 36.0,) * 12
relax_rate = 1.6
drag_factor = 20.0


def crossing(speeds):
    return (
        tuple(n for n, c in speeds if c[0] == 1),
        tuple(n for n, c in speeds if c[0] == -1),
        tuple(n for n, c in speeds if c[1] == 1),
        tuple(n for n, c in speeds if c[1] == -1),
        tuple(n for n, c in speeds if c[0] != 0 and c[1] != 0),
    )


MOVING = tuple((n, lattice_speeds[n]) for n in range(1, 19))
REVERSED = tuple((n, tuple(-v for v in lattice_speeds[n])) for n in range(1, 19))
N_COPIES = sum(len(s) for s in crossing(MOVING))


def opposite_of(number):
    return number + 1 if number % 2 == 1 else number - 1


def along_of(speed, flow):
    along = None
    for axis in range(3):
        if speed[axis] == 0:
            continue
        term = flow[axis] if speed[axis] == 1 else -flow[axis]
        along = term if along is None else along + term
    return along


def collide(moved, flow, fluid):
    speed_sq = flow[0] * flow[0] + flow[1] * flow[1] + flow[2] * flow[2]
    scalar_part = None
    vector_part = [None, None, None]
    drag_local = None
    for number in range(19):
        speed = lattice_speeds[number]
        weighted = lattice_weights[number] * moved[number]
        along = along_of(speed, flow)
        if along is None:
            scalar_term = weighted * (1.0 - 1.5 * speed_sq)
        else:
            scalar_term = weighted * (1.0 + 3.0 * along + 4.5 * along * along - 1.5 * speed_sq)
            drag_term = 3.0 * weighted * along
            drag_local = drag_term if drag_local is None else drag_local + drag_term
        scalar_part = scalar_term if scalar_part is None else scalar_part + scalar_term
        for axis in range(3):
            if speed[axis] == 0:
                term = weighted * (-3.0 * flow[axis])
            else:
                term = weighted * (3.0 * speed[axis] + 9.0 * along * speed[axis] - 3.0 * flow[axis])
            vector_part[axis] = term if vector_part[axis] is None else vector_part[axis] + term
    results = []
    for number in range(19):
        speed = lattice_speeds[number]
        projected = scalar_part
        for axis in range(3):
            projected = projected + vector_part[axis] * (speed[axis] - flow[axis])
        results.append(fluid * ((1.0 - relax_rate) * moved[number] + relax_rate * projected))
    return results, fluid * drag_local


def send_plan(sets, speeds, field, bufs, top, near):
    up_x, dn_x, up_y, dn_y, me_x, me_y = near
    x_high, x_low, y_high, y_low, corners = sets
    xhi, xlo, yhi, ylo, corner = bufs
    plan = []
    for j, n in enumerate(x_high):
        plan.append((field(n).at[pl.ds(0, 8)], xhi.at[j], (dn_x, me_y)))
    for j, n in enumerate(x_low):
        plan.append((field(n).at[pl.ds(top, 8)], xlo.at[j], (up_x, me_y)))
    for j, n in enumerate(y_high):
        plan.append((field(n), yhi.at[j], (me_x, dn_y)))
    for j, n in enumerate(y_low):
        plan.append((field(n), ylo.at[j], (me_x, up_y)))
    for j, n in enumerate(corners):
        cx, cy, _ = speeds[n]
        rows_at = pl.ds(0, 8) if cx == 1 else pl.ds(top, 8)
        dev_x = dn_x if cx == 1 else up_x
        dev_y = dn_y if cy == 1 else up_y
        plan.append((field(n).at[rows_at], corner.at[j], (dev_x, dev_y)))
    return plan


def start_copies(plan, send_sems, recv_sems):
    copies = []
    for k, (from_ref, to_ref, dev) in enumerate(plan):
        copy = pltpu.make_async_remote_copy(
            src_ref=from_ref, dst_ref=to_ref, send_sem=send_sems.at[k],
            recv_sem=recv_sems.at[k], device_id=dev, device_id_type=MESH)
        copy.start()
        copies.append(copy)
    return copies


def shifted(own, speed, n, sets, bufs, rows):
    x_high, x_low, y_high, y_low, corners = sets
    xhi, xlo, yhi, ylo, corner = bufs
    cx, cy, cz = speed
    top = rows - 8
    row8 = lax.broadcasted_iota(jnp.int32, (8, 128), 0)
    lane = lax.broadcasted_iota(jnp.int32, (rows, 128), 1)
    level = lax.rem(lax.broadcasted_iota(jnp.int32, (rows, 128), 0), 4)

    def patch_x(block, tile):
        if cx == 1:
            head = jnp.where(row8 < 4, tile, block[0:8])
            return jnp.concatenate([head, block[8:]], axis=0)
        tail = jnp.where(row8 >= 4, tile, block[top:])
        return jnp.concatenate([block[:top], tail], axis=0)

    if cx == 1:
        own = patch_x(own, xhi[x_high.index(n)])
    elif cx == -1:
        own = patch_x(own, xlo[x_low.index(n)])
    if cy != 0:
        side = yhi[y_high.index(n)] if cy == 1 else ylo[y_low.index(n)]
        if cx != 0:
            side = patch_x(side, corner[corners.index(n)])
        edge = 0 if cy == 1 else 127
        own = jnp.where(lane == edge, side, own)
    shift = 4 * cx + cz
    if shift % rows:
        own = pltpu.roll(own, (-shift) % rows, 0)
    if cy != 0:
        own = pltpu.roll(own, (-cy) % 128, 1)
    if cz == 1:
        own = jnp.where(level == 3, 0.0, own)
    elif cz == -1:
        own = jnp.where(level == 0, 0.0, own)
    return own


def drag_weight(number, flow, fluid):
    return (3.0 * lattice_weights[number]) * along_of(lattice_speeds[number], flow) * fluid


def lbm_kernel(nx, ny, rows, scale, lam_ref, vel_in, blk_ref, out_ref, drag_ref,
               vel_ref, fluid_ref, moved, state, hfield, xhi, xlo, yhi, ylo, corner, hxhi, hxlo, hyhi, hylo, hcorner,
               part, row_buf, col_buf, row_sum,
               ssem, rsem, hsend, hrecv, sum_send_a, sum_recv_a, sum_send_b, sum_recv_b):
    me_x = lax.axis_index("gx")
    me_y = lax.axis_index("gy")
    up_x = lax.rem(me_x + 1, nx)
    dn_x = lax.rem(me_x + nx - 1, nx)
    up_y = lax.rem(me_y + 1, ny)
    dn_y = lax.rem(me_y + ny - 1, ny)
    near = (up_x, dn_x, up_y, dn_y, me_x, me_y)
    top = rows - 8

    barrier = pltpu.get_barrier_semaphore()
    for k in range(1, ny):
        pl.semaphore_signal(barrier, inc=1, device_id=(me_x, lax.rem(me_y + k, ny)), device_id_type=MESH)
    for k in range(1, nx):
        pl.semaphore_signal(barrier, inc=1, device_id=(lax.rem(me_x + k, nx), me_y), device_id_type=MESH)
    for dev in ((up_x, up_y), (up_x, dn_y), (dn_x, up_y), (dn_x, dn_y)):
        pl.semaphore_signal(barrier, inc=1, device_id=dev, device_id_type=MESH)

    for step in range(STEPS):
        for axis in range(3):
            vel_ref[step, axis] = vel_in[step, axis].astype(jnp.float32)
    level = lax.rem(lax.broadcasted_iota(jnp.int32, (rows, 128), 0), 4)
    from_below = pltpu.roll(blk_ref[4], 1, 0)
    from_above = pltpu.roll(blk_ref[5], rows - 1, 0)
    solid = jnp.where(level == 3, from_below, from_above)
    fluid_ref[...] = 1.0 - solid.astype(jnp.float32)

    last_flow = [vel_ref[STEPS - 1, axis] for axis in range(3)]
    fluid_all = fluid_ref[...]
    for number in range(1, 19):
        weight = drag_weight(number, last_flow, fluid_all)
        hfield[number - 1] = jnp.where(blk_ref[number - 1] == 1, 0.0, weight)

    pl.semaphore_wait(barrier, nx + ny + 2)

    lam_sets = crossing(MOVING)
    h_sets = crossing(REVERSED)
    h_speeds = dict(REVERSED)
    lam_speeds = dict(MOVING)
    h_bufs = (hxhi, hxlo, hyhi, hylo, hcorner)
    h_copies = None
    drag_acc = jnp.zeros((8, 128), jnp.float32)

    for step in range(STEPS):
        src = lam_ref if step == 0 else state
        bufs = (xhi.at[step], xlo.at[step], yhi.at[step], ylo.at[step], corner.at[step])
        plan = send_plan(lam_sets, lam_speeds, lambda n: src.at[n], bufs, top, near)
        copies = start_copies(plan, ssem.at[step], rsem.at[step])
        if step == 0:
            h_plan = send_plan(h_sets, h_speeds, lambda n: hfield.at[n - 1], h_bufs, top, near)
            h_copies = start_copies(h_plan, hsend, hrecv)
        if step == STEPS - 1:
            for copy in h_copies:
                copy.wait()
            total = drag_acc
            for number in range(1, 19):
                gathered = shifted(hfield[number - 1], h_speeds[number], number, h_sets, h_bufs, rows)
                total = total + jnp.sum((src[number] * gathered).reshape(rows // 8, 8, 128), axis=0)
            for number in range(1, 19):
                cx = lattice_speeds[number][0]
                weight = drag_weight(number, last_flow, fluid_all)
                bounced = jnp.where(blk_ref[number - 1] == 1, src[opposite_of(number)] + 2.0 * cx, 0.0)
                total = total + jnp.sum((weight * bounced).reshape(rows // 8, 8, 128), axis=0)
            part[...] = jnp.broadcast_to(jnp.sum(total), (8, 128))
            row_copies = []
            for k in range(1, ny):
                copy = pltpu.make_async_remote_copy(
                    src_ref=part, dst_ref=row_buf.at[me_y], send_sem=sum_send_a.at[k],
                    recv_sem=sum_recv_a.at[k], device_id=(me_x, lax.rem(me_y + k, ny)),
                    device_id_type=MESH)
                copy.start()
                row_copies.append(copy)
            row_buf[me_y] = part[...]
        for copy in copies:
            copy.wait()

        moved[0] = src[0]
        for number in range(1, 19):
            source = shifted(src[number], lam_speeds[number], number, lam_sets, bufs, rows)
            bounced = src[opposite_of(number)] + 2.0 * lam_speeds[number][0]
            moved[number] = jnp.where(blk_ref[number - 1] == 1, bounced, source)

        if step == STEPS - 1:
            for copy in row_copies:
                copy.wait()
            total = row_buf[0]
            for j in range(1, ny):
                total = total + row_buf[j]
            row_sum[...] = total
            col_copies = []
            for k in range(1, nx):
                copy = pltpu.make_async_remote_copy(
                    src_ref=row_sum, dst_ref=col_buf.at[me_x], send_sem=sum_send_b.at[k],
                    recv_sem=sum_recv_b.at[k], device_id=(lax.rem(me_x + k, nx), me_y),
                    device_id_type=MESH)
                copy.start()
                col_copies.append(copy)
            col_buf[me_x] = total

        dest = out_ref if step == STEPS - 1 else state

        def chunk(c, acc):
            at = pl.ds(pl.multiple_of(c * 8, 8), 8)
            flow = [vel_ref[step, axis, at] for axis in range(3)]
            mu = [moved[number, at] for number in range(19)]
            fresh, drag = collide(mu, flow, fluid_ref[at])
            for number in range(19):
                dest[number, at] = fresh[number]
            return acc + drag

        if step < STEPS - 1:
            drag_acc = lax.fori_loop(0, rows // 8, chunk, drag_acc)
        else:
            lax.fori_loop(0, rows // 8, chunk, drag_acc)

    for copy in col_copies:
        copy.wait()
    total = col_buf[0]
    for j in range(1, nx):
        total = total + col_buf[j]
    drag_ref[0] = -scale * total[0, 0]


def per_device(adjoint_in, velocity, solid_tiles, link_blocked):
    nx = lax.axis_size("gx")
    ny = lax.axis_size("gy")
    q, rows_x, levels, rows_y = adjoint_in.shape
    rows = rows_x * levels
    lam = adjoint_in.reshape(q, rows, rows_y)
    flow = velocity.reshape(STEPS, 3, rows, rows_y)
    blocked = link_blocked.reshape(q - 1, rows, rows_y)
    cell_count = rows_x * nx * rows_y * ny * levels
    scale = drag_factor / math.sqrt(cell_count)
    vmem = pl.BlockSpec(memory_space=pltpu.VMEM)
    state, drag = pl.pallas_call(
        functools.partial(lbm_kernel, nx, ny, rows, scale),
        out_shape=(
            jax.ShapeDtypeStruct((q, rows, rows_y), jnp.float32),
            jax.ShapeDtypeStruct((1,), jnp.float32),
        ),
        in_specs=[vmem] * 3,
        out_specs=(vmem, pl.BlockSpec(memory_space=pltpu.SMEM)),
        scratch_shapes=[
            pltpu.VMEM((STEPS, 3, rows, rows_y), jnp.float32),
            pltpu.VMEM((rows, rows_y), jnp.float32),
            pltpu.VMEM((q, rows, rows_y), jnp.float32),
            pltpu.VMEM((q, rows, rows_y), jnp.float32),
            pltpu.VMEM((q - 1, rows, rows_y), jnp.float32),
        ]
        + [
            pltpu.VMEM((STEPS, len(s), rows if face >= 2 and face < 4 else 8, rows_y), jnp.float32)
            for face, s in enumerate(crossing(MOVING))
        ]
        + [
            pltpu.VMEM((len(s), rows if face >= 2 and face < 4 else 8, rows_y), jnp.float32)
            for face, s in enumerate(crossing(REVERSED))
        ]
        + [
            pltpu.VMEM((8, 128), jnp.float32),
            pltpu.VMEM((ny, 8, 128), jnp.float32),
            pltpu.VMEM((nx, 8, 128), jnp.float32),
            pltpu.VMEM((8, 128), jnp.float32),
            pltpu.SemaphoreType.DMA((STEPS, N_COPIES)),
            pltpu.SemaphoreType.DMA((STEPS, N_COPIES)),
            pltpu.SemaphoreType.DMA((N_COPIES,)),
            pltpu.SemaphoreType.DMA((N_COPIES,)),
            pltpu.SemaphoreType.DMA((ny,)),
            pltpu.SemaphoreType.DMA((ny,)),
            pltpu.SemaphoreType.DMA((nx,)),
            pltpu.SemaphoreType.DMA((nx,)),
        ],
        compiler_params=pltpu.CompilerParams(collective_id=0, has_side_effects=True),
    )(lam, flow, blocked)
    return (state.reshape(q, rows_x, levels, rows_y), drag)


def solution(mesh):
    placed = (
        P(None, "gx", None, "gy"),
        P(None, None, "gx", None, "gy"),
        P("gx", None, "gy"),
        P(None, "gx", None, "gy"),
    )
    return jax.shard_map(
        per_device,
        mesh=mesh,
        in_specs=placed,
        out_specs=(P(None, "gx", None, "gy"), P()),
        check_vma=False,
    )
```

```python
import functools
import math

import jax
import jax.numpy as jnp
from jax import lax
from jax.experimental import pallas as pl
from jax.experimental.pallas import tpu as pltpu
from jax.sharding import PartitionSpec as P

MESH = pl.DeviceIdType.MESH
TILE = 4
STEPS = 2

lattice_speeds = (
    (0, 0, 0),
    (1, 0, 0),
    (-1, 0, 0),
    (0, 1, 0),
    (0, -1, 0),
    (0, 0, 1),
    (0, 0, -1),
    (1, 1, 0),
    (-1, -1, 0),
    (1, -1, 0),
    (-1, 1, 0),
    (1, 0, 1),
    (-1, 0, -1),
    (1, 0, -1),
    (-1, 0, 1),
    (0, 1, 1),
    (0, -1, -1),
    (0, 1, -1),
    (0, -1, 1),
)
lattice_weights = (1.0 / 3.0,) + (1.0 / 18.0,) * 6 + (1.0 / 36.0,) * 12
relax_rate = 1.6
drag_factor = 20.0


def crossing(speeds):
    return (
        tuple(n for n, c in speeds if c[0] == 1),
        tuple(n for n, c in speeds if c[0] == -1),
        tuple(n for n, c in speeds if c[1] == 1),
        tuple(n for n, c in speeds if c[1] == -1),
        tuple(n for n, c in speeds if c[0] != 0 and c[1] != 0),
    )


MOVING = tuple((n, lattice_speeds[n]) for n in range(1, 19))
REVERSED = tuple((n, tuple(-v for v in lattice_speeds[n])) for n in range(1, 19))
N_COPIES = sum(len(s) for s in crossing(MOVING))


def opposite_of(number):
    return number + 1 if number % 2 == 1 else number - 1


def along_of(speed, flow):
    along = None
    for axis in range(3):
        if speed[axis] == 0:
            continue
        term = flow[axis] if speed[axis] == 1 else -flow[axis]
        along = term if along is None else along + term
    return along


def collide(moved, flow, fluid):
    speed_sq = flow[0] * flow[0] + flow[1] * flow[1] + flow[2] * flow[2]
    scalar_part = None
    vector_part = [None, None, None]
    drag_local = None
    for number in range(19):
        speed = lattice_speeds[number]
        weighted = lattice_weights[number] * moved[number]
        along = along_of(speed, flow)
        if along is None:
            scalar_term = weighted * (1.0 - 1.5 * speed_sq)
        else:
            scalar_term = weighted * (1.0 + 3.0 * along + 4.5 * along * along - 1.5 * speed_sq)
            drag_term = 3.0 * weighted * along
            drag_local = drag_term if drag_local is None else drag_local + drag_term
        scalar_part = scalar_term if scalar_part is None else scalar_part + scalar_term
        for axis in range(3):
            if speed[axis] == 0:
                term = weighted * (-3.0 * flow[axis])
            else:
                term = weighted * (3.0 * speed[axis] + 9.0 * along * speed[axis] - 3.0 * flow[axis])
            vector_part[axis] = term if vector_part[axis] is None else vector_part[axis] + term
    results = []
    for number in range(19):
        speed = lattice_speeds[number]
        projected = scalar_part
        for axis in range(3):
            projected = projected + vector_part[axis] * (speed[axis] - flow[axis])
        results.append(fluid * ((1.0 - relax_rate) * moved[number] + relax_rate * projected))
    return results, fluid * drag_local


def send_plan(sets, speeds, field, bufs, top, near):
    up_x, dn_x, up_y, dn_y, me_x, me_y = near
    x_high, x_low, y_high, y_low, corners = sets
    xhi, xlo, yhi, ylo, corner = bufs
    plan = []
    for j, n in enumerate(x_high):
        plan.append((field(n).at[pl.ds(0, 8)], xhi.at[j], (dn_x, me_y)))
    for j, n in enumerate(x_low):
        plan.append((field(n).at[pl.ds(top, 8)], xlo.at[j], (up_x, me_y)))
    for j, n in enumerate(y_high):
        plan.append((field(n), yhi.at[j], (me_x, dn_y)))
    for j, n in enumerate(y_low):
        plan.append((field(n), ylo.at[j], (me_x, up_y)))
    for j, n in enumerate(corners):
        cx, cy, _ = speeds[n]
        rows_at = pl.ds(0, 8) if cx == 1 else pl.ds(top, 8)
        dev_x = dn_x if cx == 1 else up_x
        dev_y = dn_y if cy == 1 else up_y
        plan.append((field(n).at[rows_at], corner.at[j], (dev_x, dev_y)))
    return plan


def start_copies(plan, send_sems, recv_sems):
    copies = []
    for k, (from_ref, to_ref, dev) in enumerate(plan):
        copy = pltpu.make_async_remote_copy(
            src_ref=from_ref, dst_ref=to_ref, send_sem=send_sems.at[k],
            recv_sem=recv_sems.at[k], device_id=dev, device_id_type=MESH)
        copy.start()
        copies.append(copy)
    return copies


def shifted(own, speed, n, sets, bufs, rows):
    x_high, x_low, y_high, y_low, corners = sets
    xhi, xlo, yhi, ylo, corner = bufs
    cx, cy, cz = speed
    top = rows - 8
    row8 = lax.broadcasted_iota(jnp.int32, (8, 128), 0)
    lane = lax.broadcasted_iota(jnp.int32, (rows, 128), 1)
    level = lax.rem(lax.broadcasted_iota(jnp.int32, (rows, 128), 0), 4)

    def patch_x(block, tile):
        if cx == 1:
            head = jnp.where(row8 < 4, tile, block[0:8])
            return jnp.concatenate([head, block[8:]], axis=0)
        tail = jnp.where(row8 >= 4, tile, block[top:])
        return jnp.concatenate([block[:top], tail], axis=0)

    if cx == 1:
        own = patch_x(own, xhi[x_high.index(n)])
    elif cx == -1:
        own = patch_x(own, xlo[x_low.index(n)])
    if cy != 0:
        side = yhi[y_high.index(n)] if cy == 1 else ylo[y_low.index(n)]
        if cx != 0:
            side = patch_x(side, corner[corners.index(n)])
        edge = 0 if cy == 1 else 127
        own = jnp.where(lane == edge, side, own)
    shift = 4 * cx + cz
    if shift % rows:
        own = pltpu.roll(own, (-shift) % rows, 0)
    if cy != 0:
        own = pltpu.roll(own, (-cy) % 128, 1)
    if cz == 1:
        own = jnp.where(level == 3, 0.0, own)
    elif cz == -1:
        own = jnp.where(level == 0, 0.0, own)
    return own


def drag_weight(number, flow, fluid):
    return (3.0 * lattice_weights[number]) * along_of(lattice_speeds[number], flow) * fluid


def lbm_kernel(nx, ny, rows, scale, lam_ref, vel_in, blk_ref, out_ref, drag_ref,
               vel_ref, fluid_ref, moved, state, hfield, xhi, xlo, yhi, ylo, corner, hxhi, hxlo, hyhi, hylo, hcorner,
               part, row_buf, col_buf, row_sum,
               ssem, rsem, hsend, hrecv, sum_send_a, sum_recv_a, sum_send_b, sum_recv_b):
    me_x = lax.axis_index("gx")
    me_y = lax.axis_index("gy")
    up_x = lax.rem(me_x + 1, nx)
    dn_x = lax.rem(me_x + nx - 1, nx)
    up_y = lax.rem(me_y + 1, ny)
    dn_y = lax.rem(me_y + ny - 1, ny)
    near = (up_x, dn_x, up_y, dn_y, me_x, me_y)
    top = rows - 8

    barrier = pltpu.get_barrier_semaphore()
    for k in range(1, ny):
        pl.semaphore_signal(barrier, inc=1, device_id=(me_x, lax.rem(me_y + k, ny)), device_id_type=MESH)
    for k in range(1, nx):
        pl.semaphore_signal(barrier, inc=1, device_id=(lax.rem(me_x + k, nx), me_y), device_id_type=MESH)
    for dev in ((up_x, up_y), (up_x, dn_y), (dn_x, up_y), (dn_x, dn_y)):
        pl.semaphore_signal(barrier, inc=1, device_id=dev, device_id_type=MESH)

    for step in range(STEPS):
        for axis in range(3):
            vel_ref[step, axis] = vel_in[step, axis].astype(jnp.float32)
    level = lax.rem(lax.broadcasted_iota(jnp.int32, (rows, 128), 0), 4)
    from_below = pltpu.roll(blk_ref[4], 1, 0)
    from_above = pltpu.roll(blk_ref[5], rows - 1, 0)
    solid = jnp.where(level == 3, from_below, from_above)
    fluid_ref[...] = 1.0 - solid.astype(jnp.float32)

    last_flow = [vel_ref[STEPS - 1, axis] for axis in range(3)]
    fluid_all = fluid_ref[...]
    for number in range(1, 19):
        weight = drag_weight(number, last_flow, fluid_all)
        hfield[number - 1] = jnp.where(blk_ref[number - 1] == 1, 0.0, weight)

    pl.semaphore_wait(barrier, nx + ny + 2)

    lam_sets = crossing(MOVING)
    h_sets = crossing(REVERSED)
    h_speeds = dict(REVERSED)
    lam_speeds = dict(MOVING)
    h_bufs = (hxhi, hxlo, hyhi, hylo, hcorner)
    h_copies = None
    sent = []
    drag_acc = jnp.zeros((8, 128), jnp.float32)

    for step in range(STEPS):
        src = lam_ref if step == 0 else state
        bufs = (xhi.at[step], xlo.at[step], yhi.at[step], ylo.at[step], corner.at[step])
        plan = send_plan(lam_sets, lam_speeds, lambda n: src.at[n], bufs, top, near)
        copies = start_copies(plan, ssem.at[step], rsem.at[step])
        if step == 0:
            h_plan = send_plan(h_sets, h_speeds, lambda n: hfield.at[n - 1], h_bufs, top, near)
            h_copies = start_copies(h_plan, hsend, hrecv)
        if step == STEPS - 1:
            for copy in h_copies:
                copy.wait_recv()
            sent += h_copies
            total = drag_acc
            for number in range(1, 19):
                gathered = shifted(hfield[number - 1], h_speeds[number], number, h_sets, h_bufs, rows)
                total = total + jnp.sum((src[number] * gathered).reshape(rows // 8, 8, 128), axis=0)
            for number in range(1, 19):
                cx = lattice_speeds[number][0]
                weight = drag_weight(number, last_flow, fluid_all)
                bounced = jnp.where(blk_ref[number - 1] == 1, src[opposite_of(number)] + 2.0 * cx, 0.0)
                total = total + jnp.sum((weight * bounced).reshape(rows // 8, 8, 128), axis=0)
            part[...] = jnp.broadcast_to(jnp.sum(total), (8, 128))
            row_copies = []
            for k in range(1, ny):
                copy = pltpu.make_async_remote_copy(
                    src_ref=part, dst_ref=row_buf.at[me_y], send_sem=sum_send_a.at[k],
                    recv_sem=sum_recv_a.at[k], device_id=(me_x, lax.rem(me_y + k, ny)),
                    device_id_type=MESH)
                copy.start()
                row_copies.append(copy)
            row_buf[me_y] = part[...]
        for copy in copies:
            copy.wait_recv()
        sent += copies

        moved[0] = src[0]
        for number in range(1, 19):
            source = shifted(src[number], lam_speeds[number], number, lam_sets, bufs, rows)
            bounced = src[opposite_of(number)] + 2.0 * lam_speeds[number][0]
            moved[number] = jnp.where(blk_ref[number - 1] == 1, bounced, source)

        if step == STEPS - 1:
            for copy in row_copies:
                copy.wait_recv()
            sent += row_copies
            total = row_buf[0]
            for j in range(1, ny):
                total = total + row_buf[j]
            row_sum[...] = total
            col_copies = []
            for k in range(1, nx):
                copy = pltpu.make_async_remote_copy(
                    src_ref=row_sum, dst_ref=col_buf.at[me_x], send_sem=sum_send_b.at[k],
                    recv_sem=sum_recv_b.at[k], device_id=(lax.rem(me_x + k, nx), me_y),
                    device_id_type=MESH)
                copy.start()
                col_copies.append(copy)
            col_buf[me_x] = total

        dest = out_ref if step == STEPS - 1 else state

        def chunk(c, acc):
            at = pl.ds(pl.multiple_of(c * 8, 8), 8)
            flow = [vel_ref[step, axis, at] for axis in range(3)]
            mu = [moved[number, at] for number in range(19)]
            fresh, drag = collide(mu, flow, fluid_ref[at])
            for number in range(19):
                dest[number, at] = fresh[number]
            return acc + drag

        if step < STEPS - 1:
            drag_acc = lax.fori_loop(0, rows // 8, chunk, drag_acc)
        else:
            lax.fori_loop(0, rows // 8, chunk, drag_acc)

    for copy in col_copies:
        copy.wait_recv()
    sent += col_copies
    total = col_buf[0]
    for j in range(1, nx):
        total = total + col_buf[j]
    drag_ref[0] = -scale * total[0, 0]
    for copy in sent:
        copy.wait_send()


def per_device(adjoint_in, velocity, solid_tiles, link_blocked):
    nx = lax.axis_size("gx")
    ny = lax.axis_size("gy")
    q, rows_x, levels, rows_y = adjoint_in.shape
    rows = rows_x * levels
    lam = adjoint_in.reshape(q, rows, rows_y)
    flow = velocity.reshape(STEPS, 3, rows, rows_y)
    blocked = link_blocked.reshape(q - 1, rows, rows_y)
    cell_count = rows_x * nx * rows_y * ny * levels
    scale = drag_factor / math.sqrt(cell_count)
    vmem = pl.BlockSpec(memory_space=pltpu.VMEM)
    state, drag = pl.pallas_call(
        functools.partial(lbm_kernel, nx, ny, rows, scale),
        out_shape=(
            jax.ShapeDtypeStruct((q, rows, rows_y), jnp.float32),
            jax.ShapeDtypeStruct((1,), jnp.float32),
        ),
        in_specs=[vmem] * 3,
        out_specs=(vmem, pl.BlockSpec(memory_space=pltpu.SMEM)),
        scratch_shapes=[
            pltpu.VMEM((STEPS, 3, rows, rows_y), jnp.float32),
            pltpu.VMEM((rows, rows_y), jnp.float32),
            pltpu.VMEM((q, rows, rows_y), jnp.float32),
            pltpu.VMEM((q, rows, rows_y), jnp.float32),
            pltpu.VMEM((q - 1, rows, rows_y), jnp.float32),
        ]
        + [
            pltpu.VMEM((STEPS, len(s), rows if face >= 2 and face < 4 else 8, rows_y), jnp.float32)
            for face, s in enumerate(crossing(MOVING))
        ]
        + [
            pltpu.VMEM((len(s), rows if face >= 2 and face < 4 else 8, rows_y), jnp.float32)
            for face, s in enumerate(crossing(REVERSED))
        ]
        + [
            pltpu.VMEM((8, 128), jnp.float32),
            pltpu.VMEM((ny, 8, 128), jnp.float32),
            pltpu.VMEM((nx, 8, 128), jnp.float32),
            pltpu.VMEM((8, 128), jnp.float32),
            pltpu.SemaphoreType.DMA((STEPS, N_COPIES)),
            pltpu.SemaphoreType.DMA((STEPS, N_COPIES)),
            pltpu.SemaphoreType.DMA((N_COPIES,)),
            pltpu.SemaphoreType.DMA((N_COPIES,)),
            pltpu.SemaphoreType.DMA((ny,)),
            pltpu.SemaphoreType.DMA((ny,)),
            pltpu.SemaphoreType.DMA((nx,)),
            pltpu.SemaphoreType.DMA((nx,)),
        ],
        compiler_params=pltpu.CompilerParams(collective_id=0, has_side_effects=True),
    )(lam, flow, blocked)
    return (state.reshape(q, rows_x, levels, rows_y), drag)


def solution(mesh):
    placed = (
        P(None, "gx", None, "gy"),
        P(None, None, "gx", None, "gy"),
        P("gx", None, "gy"),
        P(None, "gx", None, "gy"),
    )
    return jax.shard_map(
        per_device,
        mesh=mesh,
        in_specs=placed,
        out_specs=(P(None, "gx", None, "gy"), P()),
        check_vma=False,
    )
```

```python
import functools
import math

import jax
import jax.numpy as jnp
from jax import lax
from jax.experimental import pallas as pl
from jax.experimental.pallas import tpu as pltpu
from jax.sharding import PartitionSpec as P

MESH = pl.DeviceIdType.MESH
TILE = 4
STEPS = 2

lattice_speeds = (
    (0, 0, 0),
    (1, 0, 0),
    (-1, 0, 0),
    (0, 1, 0),
    (0, -1, 0),
    (0, 0, 1),
    (0, 0, -1),
    (1, 1, 0),
    (-1, -1, 0),
    (1, -1, 0),
    (-1, 1, 0),
    (1, 0, 1),
    (-1, 0, -1),
    (1, 0, -1),
    (-1, 0, 1),
    (0, 1, 1),
    (0, -1, -1),
    (0, 1, -1),
    (0, -1, 1),
)
lattice_weights = (1.0 / 3.0,) + (1.0 / 18.0,) * 6 + (1.0 / 36.0,) * 12
relax_rate = 1.6
drag_factor = 20.0


def crossing(speeds):
    return (
        tuple(n for n, c in speeds if c[0] == 1),
        tuple(n for n, c in speeds if c[0] == -1),
        tuple(n for n, c in speeds if c[1] == 1),
        tuple(n for n, c in speeds if c[1] == -1),
        tuple(n for n, c in speeds if c[0] != 0 and c[1] != 0),
    )


MOVING = tuple((n, lattice_speeds[n]) for n in range(1, 19))
REVERSED = tuple((n, tuple(-v for v in lattice_speeds[n])) for n in range(1, 19))
N_COPIES = sum(len(s) for s in crossing(MOVING))


def opposite_of(number):
    return number + 1 if number % 2 == 1 else number - 1


def along_of(speed, flow):
    along = None
    for axis in range(3):
        if speed[axis] == 0:
            continue
        term = flow[axis] if speed[axis] == 1 else -flow[axis]
        along = term if along is None else along + term
    return along


def collide(moved, flow, fluid):
    speed_sq = flow[0] * flow[0] + flow[1] * flow[1] + flow[2] * flow[2]
    scalar_part = None
    vector_part = [None, None, None]
    drag_local = None
    for number in range(19):
        speed = lattice_speeds[number]
        weighted = lattice_weights[number] * moved[number]
        along = along_of(speed, flow)
        if along is None:
            scalar_term = weighted * (1.0 - 1.5 * speed_sq)
        else:
            scalar_term = weighted * (1.0 + 3.0 * along + 4.5 * along * along - 1.5 * speed_sq)
            drag_term = 3.0 * weighted * along
            drag_local = drag_term if drag_local is None else drag_local + drag_term
        scalar_part = scalar_term if scalar_part is None else scalar_part + scalar_term
        for axis in range(3):
            if speed[axis] == 0:
                term = weighted * (-3.0 * flow[axis])
            else:
                term = weighted * (3.0 * speed[axis] + 9.0 * along * speed[axis] - 3.0 * flow[axis])
            vector_part[axis] = term if vector_part[axis] is None else vector_part[axis] + term
    results = []
    for number in range(19):
        speed = lattice_speeds[number]
        projected = scalar_part
        for axis in range(3):
            projected = projected + vector_part[axis] * (speed[axis] - flow[axis])
        results.append(fluid * ((1.0 - relax_rate) * moved[number] + relax_rate * projected))
    return results, fluid * drag_local


def send_plan(sets, speeds, field, bufs, top, near):
    up_x, dn_x, up_y, dn_y, me_x, me_y = near
    x_high, x_low, y_high, y_low, corners = sets
    xhi, xlo, yhi, ylo, corner = bufs
    plan = []
    for j, n in enumerate(x_high):
        plan.append((field(n).at[pl.ds(0, 8)], xhi.at[j], (dn_x, me_y)))
    for j, n in enumerate(x_low):
        plan.append((field(n).at[pl.ds(top, 8)], xlo.at[j], (up_x, me_y)))
    for j, n in enumerate(y_high):
        plan.append((field(n), yhi.at[j], (me_x, dn_y)))
    for j, n in enumerate(y_low):
        plan.append((field(n), ylo.at[j], (me_x, up_y)))
    for j, n in enumerate(corners):
        cx, cy, _ = speeds[n]
        rows_at = pl.ds(0, 8) if cx == 1 else pl.ds(top, 8)
        dev_x = dn_x if cx == 1 else up_x
        dev_y = dn_y if cy == 1 else up_y
        plan.append((field(n).at[rows_at], corner.at[j], (dev_x, dev_y)))
    return plan


def start_copies(plan, send_sems, recv_sems):
    copies = []
    for k, (from_ref, to_ref, dev) in enumerate(plan):
        copy = pltpu.make_async_remote_copy(
            src_ref=from_ref, dst_ref=to_ref, send_sem=send_sems.at[k],
            recv_sem=recv_sems.at[k], device_id=dev, device_id_type=MESH)
        copy.start()
        copies.append(copy)
    return copies


def shifted(own, speed, n, sets, bufs, rows):
    x_high, x_low, y_high, y_low, corners = sets
    xhi, xlo, yhi, ylo, corner = bufs
    cx, cy, cz = speed
    top = rows - 8
    row8 = lax.broadcasted_iota(jnp.int32, (8, 128), 0)
    lane = lax.broadcasted_iota(jnp.int32, (rows, 128), 1)
    level = lax.rem(lax.broadcasted_iota(jnp.int32, (rows, 128), 0), 4)

    def patch_x(block, tile):
        if cx == 1:
            head = jnp.where(row8 < 4, tile, block[0:8])
            return jnp.concatenate([head, block[8:]], axis=0)
        tail = jnp.where(row8 >= 4, tile, block[top:])
        return jnp.concatenate([block[:top], tail], axis=0)

    if cx == 1:
        own = patch_x(own, xhi[x_high.index(n)])
    elif cx == -1:
        own = patch_x(own, xlo[x_low.index(n)])
    if cy != 0:
        side = yhi[y_high.index(n)] if cy == 1 else ylo[y_low.index(n)]
        if cx != 0:
            side = patch_x(side, corner[corners.index(n)])
        edge = 0 if cy == 1 else 127
        own = jnp.where(lane == edge, side, own)
    shift = 4 * cx + cz
    if shift % rows:
        own = pltpu.roll(own, (-shift) % rows, 0)
    if cy != 0:
        own = pltpu.roll(own, (-cy) % 128, 1)
    if cz == 1:
        own = jnp.where(level == 3, 0.0, own)
    elif cz == -1:
        own = jnp.where(level == 0, 0.0, own)
    return own


def drag_weight(number, flow, fluid):
    return (3.0 * lattice_weights[number]) * along_of(lattice_speeds[number], flow) * fluid


def lbm_kernel(nx, ny, rows, scale, lam_hbm, vel_hbm, blk_hbm, out_ref, drag_ref,
               lam_ref, vel_in, blk_ref, load_sem, vel_ref, fluid_ref, moved, state, hfield, xhi, xlo, yhi, ylo, corner, hxhi, hxlo, hyhi, hylo, hcorner,
               part, row_buf, col_buf, row_sum,
               ssem, rsem, hsend, hrecv, sum_send_a, sum_recv_a, sum_send_b, sum_recv_b):
    me_x = lax.axis_index("gx")
    me_y = lax.axis_index("gy")
    up_x = lax.rem(me_x + 1, nx)
    dn_x = lax.rem(me_x + nx - 1, nx)
    up_y = lax.rem(me_y + 1, ny)
    dn_y = lax.rem(me_y + ny - 1, ny)
    near = (up_x, dn_x, up_y, dn_y, me_x, me_y)
    top = rows - 8

    loads = [
        pltpu.make_async_copy(hbm, vmem, load_sem.at[k])
        for k, (hbm, vmem) in enumerate(((lam_hbm, lam_ref), (vel_hbm, vel_in), (blk_hbm, blk_ref)))
    ]
    for load in loads:
        load.start()

    barrier = pltpu.get_barrier_semaphore()
    for k in range(1, ny):
        pl.semaphore_signal(barrier, inc=1, device_id=(me_x, lax.rem(me_y + k, ny)), device_id_type=MESH)
    for k in range(1, nx):
        pl.semaphore_signal(barrier, inc=1, device_id=(lax.rem(me_x + k, nx), me_y), device_id_type=MESH)
    for dev in ((up_x, up_y), (up_x, dn_y), (dn_x, up_y), (dn_x, dn_y)):
        pl.semaphore_signal(barrier, inc=1, device_id=dev, device_id_type=MESH)

    loads[1].wait()
    loads[2].wait()
    for step in range(STEPS):
        for axis in range(3):
            vel_ref[step, axis] = vel_in[step, axis].astype(jnp.float32)
    level = lax.rem(lax.broadcasted_iota(jnp.int32, (rows, 128), 0), 4)
    from_below = pltpu.roll(blk_ref[4], 1, 0)
    from_above = pltpu.roll(blk_ref[5], rows - 1, 0)
    solid = jnp.where(level == 3, from_below, from_above)
    fluid_ref[...] = 1.0 - solid.astype(jnp.float32)

    last_flow = [vel_ref[STEPS - 1, axis] for axis in range(3)]
    fluid_all = fluid_ref[...]
    for number in range(1, 19):
        weight = drag_weight(number, last_flow, fluid_all)
        hfield[number - 1] = jnp.where(blk_ref[number - 1] == 1, 0.0, weight)

    pl.semaphore_wait(barrier, nx + ny + 2)

    lam_sets = crossing(MOVING)
    h_sets = crossing(REVERSED)
    h_speeds = dict(REVERSED)
    lam_speeds = dict(MOVING)
    h_bufs = (hxhi, hxlo, hyhi, hylo, hcorner)
    h_copies = None
    sent = []
    drag_acc = jnp.zeros((8, 128), jnp.float32)

    for step in range(STEPS):
        src = lam_ref if step == 0 else state
        origin = lam_hbm if step == 0 else state
        bufs = (xhi.at[step], xlo.at[step], yhi.at[step], ylo.at[step], corner.at[step])
        plan = send_plan(lam_sets, lam_speeds, lambda n: origin.at[n], bufs, top, near)
        copies = start_copies(plan, ssem.at[step], rsem.at[step])
        if step == 0:
            h_plan = send_plan(h_sets, h_speeds, lambda n: hfield.at[n - 1], h_bufs, top, near)
            h_copies = start_copies(h_plan, hsend, hrecv)
        if step == STEPS - 1:
            for copy in h_copies:
                copy.wait_recv()
            sent += h_copies
            total = drag_acc
            for number in range(1, 19):
                gathered = shifted(hfield[number - 1], h_speeds[number], number, h_sets, h_bufs, rows)
                total = total + jnp.sum((src[number] * gathered).reshape(rows // 8, 8, 128), axis=0)
            for number in range(1, 19):
                cx = lattice_speeds[number][0]
                weight = drag_weight(number, last_flow, fluid_all)
                bounced = jnp.where(blk_ref[number - 1] == 1, src[opposite_of(number)] + 2.0 * cx, 0.0)
                total = total + jnp.sum((weight * bounced).reshape(rows // 8, 8, 128), axis=0)
            part[...] = jnp.broadcast_to(jnp.sum(total), (8, 128))
            row_copies = []
            for k in range(1, ny):
                copy = pltpu.make_async_remote_copy(
                    src_ref=part, dst_ref=row_buf.at[me_y], send_sem=sum_send_a.at[k],
                    recv_sem=sum_recv_a.at[k], device_id=(me_x, lax.rem(me_y + k, ny)),
                    device_id_type=MESH)
                copy.start()
                row_copies.append(copy)
            row_buf[me_y] = part[...]
        if step == 0:
            loads[0].wait()
        for copy in copies:
            copy.wait_recv()
        sent += copies

        moved[0] = src[0]
        for number in range(1, 19):
            source = shifted(src[number], lam_speeds[number], number, lam_sets, bufs, rows)
            bounced = src[opposite_of(number)] + 2.0 * lam_speeds[number][0]
            moved[number] = jnp.where(blk_ref[number - 1] == 1, bounced, source)

        if step == STEPS - 1:
            for copy in row_copies:
                copy.wait_recv()
            sent += row_copies
            total = row_buf[0]
            for j in range(1, ny):
                total = total + row_buf[j]
            row_sum[...] = total
            col_copies = []
            for k in range(1, nx):
                copy = pltpu.make_async_remote_copy(
                    src_ref=row_sum, dst_ref=col_buf.at[me_x], send_sem=sum_send_b.at[k],
                    recv_sem=sum_recv_b.at[k], device_id=(lax.rem(me_x + k, nx), me_y),
                    device_id_type=MESH)
                copy.start()
                col_copies.append(copy)
            col_buf[me_x] = total

        dest = out_ref if step == STEPS - 1 else state

        def chunk(c, acc):
            at = pl.ds(pl.multiple_of(c * 8, 8), 8)
            flow = [vel_ref[step, axis, at] for axis in range(3)]
            mu = [moved[number, at] for number in range(19)]
            fresh, drag = collide(mu, flow, fluid_ref[at])
            for number in range(19):
                dest[number, at] = fresh[number]
            return acc + drag

        if step < STEPS - 1:
            drag_acc = lax.fori_loop(0, rows // 8, chunk, drag_acc)
        else:
            lax.fori_loop(0, rows // 8, chunk, drag_acc)

    for copy in col_copies:
        copy.wait_recv()
    sent += col_copies
    total = col_buf[0]
    for j in range(1, nx):
        total = total + col_buf[j]
    drag_ref[0] = -scale * total[0, 0]
    for copy in sent:
        copy.wait_send()


def per_device(adjoint_in, velocity, solid_tiles, link_blocked):
    nx = lax.axis_size("gx")
    ny = lax.axis_size("gy")
    q, rows_x, levels, rows_y = adjoint_in.shape
    rows = rows_x * levels
    lam = adjoint_in.reshape(q, rows, rows_y)
    flow = velocity.reshape(STEPS, 3, rows, rows_y)
    blocked = link_blocked.reshape(q - 1, rows, rows_y)
    cell_count = rows_x * nx * rows_y * ny * levels
    scale = drag_factor / math.sqrt(cell_count)
    vmem = pl.BlockSpec(memory_space=pltpu.VMEM)
    state, drag = pl.pallas_call(
        functools.partial(lbm_kernel, nx, ny, rows, scale),
        out_shape=(
            jax.ShapeDtypeStruct((q, rows, rows_y), jnp.float32),
            jax.ShapeDtypeStruct((1,), jnp.float32),
        ),
        in_specs=[pl.BlockSpec(memory_space=pl.ANY)] * 3,
        out_specs=(vmem, pl.BlockSpec(memory_space=pltpu.SMEM)),
        scratch_shapes=[
            pltpu.VMEM((q, rows, rows_y), jnp.float32),
            pltpu.VMEM((STEPS, 3, rows, rows_y), velocity.dtype),
            pltpu.VMEM((q - 1, rows, rows_y), link_blocked.dtype),
            pltpu.SemaphoreType.DMA((3,)),
            pltpu.VMEM((STEPS, 3, rows, rows_y), jnp.float32),
            pltpu.VMEM((rows, rows_y), jnp.float32),
            pltpu.VMEM((q, rows, rows_y), jnp.float32),
            pltpu.VMEM((q, rows, rows_y), jnp.float32),
            pltpu.VMEM((q - 1, rows, rows_y), jnp.float32),
        ]
        + [
            pltpu.VMEM((STEPS, len(s), rows if face >= 2 and face < 4 else 8, rows_y), jnp.float32)
            for face, s in enumerate(crossing(MOVING))
        ]
        + [
            pltpu.VMEM((len(s), rows if face >= 2 and face < 4 else 8, rows_y), jnp.float32)
            for face, s in enumerate(crossing(REVERSED))
        ]
        + [
            pltpu.VMEM((8, 128), jnp.float32),
            pltpu.VMEM((ny, 8, 128), jnp.float32),
            pltpu.VMEM((nx, 8, 128), jnp.float32),
            pltpu.VMEM((8, 128), jnp.float32),
            pltpu.SemaphoreType.DMA((STEPS, N_COPIES)),
            pltpu.SemaphoreType.DMA((STEPS, N_COPIES)),
            pltpu.SemaphoreType.DMA((N_COPIES,)),
            pltpu.SemaphoreType.DMA((N_COPIES,)),
            pltpu.SemaphoreType.DMA((ny,)),
            pltpu.SemaphoreType.DMA((ny,)),
            pltpu.SemaphoreType.DMA((nx,)),
            pltpu.SemaphoreType.DMA((nx,)),
        ],
        compiler_params=pltpu.CompilerParams(collective_id=0, has_side_effects=True),
    )(lam, flow, blocked)
    return (state.reshape(q, rows_x, levels, rows_y), drag)


def solution(mesh):
    placed = (
        P(None, "gx", None, "gy"),
        P(None, None, "gx", None, "gy"),
        P("gx", None, "gy"),
        P(None, "gx", None, "gy"),
    )
    return jax.shard_map(
        per_device,
        mesh=mesh,
        in_specs=placed,
        out_specs=(P(None, "gx", None, "gy"), P()),
        check_vma=False,
    )
```

```python
import functools
import math

import jax
import jax.numpy as jnp
from jax import lax
from jax.experimental import pallas as pl
from jax.experimental.pallas import tpu as pltpu
from jax.sharding import PartitionSpec as P

MESH = pl.DeviceIdType.MESH
TILE = 4
STEPS = 2

lattice_speeds = (
    (0, 0, 0),
    (1, 0, 0),
    (-1, 0, 0),
    (0, 1, 0),
    (0, -1, 0),
    (0, 0, 1),
    (0, 0, -1),
    (1, 1, 0),
    (-1, -1, 0),
    (1, -1, 0),
    (-1, 1, 0),
    (1, 0, 1),
    (-1, 0, -1),
    (1, 0, -1),
    (-1, 0, 1),
    (0, 1, 1),
    (0, -1, -1),
    (0, 1, -1),
    (0, -1, 1),
)
lattice_weights = (1.0 / 3.0,) + (1.0 / 18.0,) * 6 + (1.0 / 36.0,) * 12
relax_rate = 1.6
drag_factor = 20.0


def crossing(speeds):
    return (
        tuple(n for n, c in speeds if c[0] == 1),
        tuple(n for n, c in speeds if c[0] == -1),
        tuple(n for n, c in speeds if c[1] == 1),
        tuple(n for n, c in speeds if c[1] == -1),
        tuple(n for n, c in speeds if c[0] != 0 and c[1] != 0),
    )


MOVING = tuple((n, lattice_speeds[n]) for n in range(1, 19))
REVERSED = tuple((n, tuple(-v for v in lattice_speeds[n])) for n in range(1, 19))
N_COPIES = sum(len(s) for face, s in enumerate(crossing(MOVING)) if face in (0, 1, 4))


def opposite_of(number):
    return number + 1 if number % 2 == 1 else number - 1


def along_of(speed, flow):
    along = None
    for axis in range(3):
        if speed[axis] == 0:
            continue
        term = flow[axis] if speed[axis] == 1 else -flow[axis]
        along = term if along is None else along + term
    return along


def collide(moved, flow, fluid):
    speed_sq = flow[0] * flow[0] + flow[1] * flow[1] + flow[2] * flow[2]
    scalar_part = None
    vector_part = [None, None, None]
    drag_local = None
    for number in range(19):
        speed = lattice_speeds[number]
        weighted = lattice_weights[number] * moved[number]
        along = along_of(speed, flow)
        if along is None:
            scalar_term = weighted * (1.0 - 1.5 * speed_sq)
        else:
            scalar_term = weighted * (1.0 + 3.0 * along + 4.5 * along * along - 1.5 * speed_sq)
            drag_term = 3.0 * weighted * along
            drag_local = drag_term if drag_local is None else drag_local + drag_term
        scalar_part = scalar_term if scalar_part is None else scalar_part + scalar_term
        for axis in range(3):
            if speed[axis] == 0:
                term = weighted * (-3.0 * flow[axis])
            else:
                term = weighted * (3.0 * speed[axis] + 9.0 * along * speed[axis] - 3.0 * flow[axis])
            vector_part[axis] = term if vector_part[axis] is None else vector_part[axis] + term
    results = []
    for number in range(19):
        speed = lattice_speeds[number]
        projected = scalar_part
        for axis in range(3):
            projected = projected + vector_part[axis] * (speed[axis] - flow[axis])
        results.append(fluid * ((1.0 - relax_rate) * moved[number] + relax_rate * projected))
    return results, fluid * drag_local


def send_plan(sets, speeds, field, bufs, top, near):
    up_x, dn_x, up_y, dn_y, me_x, me_y = near
    x_high, x_low, _, _, corners = sets
    xhi, xlo, _, _, corner = bufs
    plan = []
    for j, n in enumerate(x_high):
        plan.append((field(n).at[pl.ds(0, 8)], xhi.at[j], (dn_x, me_y)))
    for j, n in enumerate(x_low):
        plan.append((field(n).at[pl.ds(top, 8)], xlo.at[j], (up_x, me_y)))
    for j, n in enumerate(corners):
        cx, cy, _ = speeds[n]
        rows_at = pl.ds(0, 8) if cx == 1 else pl.ds(top, 8)
        dev_x = dn_x if cx == 1 else up_x
        dev_y = dn_y if cy == 1 else up_y
        plan.append((field(n).at[rows_at], corner.at[j], (dev_x, dev_y)))
    return plan


def start_copies(plan, send_sems, recv_sems):
    copies = []
    for k, (from_ref, to_ref, dev) in enumerate(plan):
        copy = pltpu.make_async_remote_copy(
            src_ref=from_ref, dst_ref=to_ref, send_sem=send_sems.at[k],
            recv_sem=recv_sems.at[k], device_id=dev, device_id_type=MESH)
        copy.start()
        copies.append(copy)
    return copies


def shifted(own, speed, n, sets, bufs, rows):
    x_high, x_low, y_high, y_low, corners = sets
    xhi, xlo, yhi, ylo, corner = bufs
    cx, cy, cz = speed
    top = rows - 8
    row8 = lax.broadcasted_iota(jnp.int32, (8, 128), 0)
    lane = lax.broadcasted_iota(jnp.int32, (rows, 128), 1)
    level = lax.rem(lax.broadcasted_iota(jnp.int32, (rows, 128), 0), 4)

    def patch_x(block, tile):
        if cx == 1:
            head = jnp.where(row8 < 4, tile, block[0:8])
            return jnp.concatenate([head, block[8:]], axis=0)
        tail = jnp.where(row8 >= 4, tile, block[top:])
        return jnp.concatenate([block[:top], tail], axis=0)

    if cx == 1:
        own = patch_x(own, xhi[x_high.index(n)])
    elif cx == -1:
        own = patch_x(own, xlo[x_low.index(n)])
    if cy != 0:
        side = yhi(n) if cy == 1 else ylo(n)
        if cx != 0:
            side = patch_x(side, corner[corners.index(n)])
        edge = 0 if cy == 1 else 127
        own = jnp.where(lane == edge, side, own)
    shift = 4 * cx + cz
    if shift % rows:
        own = pltpu.roll(own, (-shift) % rows, 0)
    if cy != 0:
        own = pltpu.roll(own, (-cy) % 128, 1)
    if cz == 1:
        own = jnp.where(level == 3, 0.0, own)
    elif cz == -1:
        own = jnp.where(level == 0, 0.0, own)
    return own


def pack_edge(fields, from_lane, rows):
    lane = lax.broadcasted_iota(jnp.int32, (rows, 128), 1)
    packed = jnp.zeros((rows, 128), jnp.float32)
    for k, field in enumerate(fields):
        moved = field if k == from_lane else pltpu.roll(field, (k - from_lane) % 128, 1)
        packed = jnp.where(lane == k, moved, packed)
    return packed


def unpack_edge(packed_ref, k, to_lane):
    packed = packed_ref[...]
    return packed if k == to_lane else pltpu.roll(packed, (to_lane - k) % 128, 1)


def drag_weight(number, flow, fluid):
    return (3.0 * lattice_weights[number]) * along_of(lattice_speeds[number], flow) * fluid


def lbm_kernel(nx, ny, rows, scale, lam_hbm, vel_hbm, blk_hbm, out_ref, drag_ref,
               lam_ref, vel_in, blk_ref, load_sem, vel_ref, fluid_ref, moved, state, hfield, xhi, xlo, yhi, ylo, corner, hxhi, hxlo, hcorner, ypack, ysend, yrecv,
               part, row_buf, col_buf, row_sum,
               ssem, rsem, hsend, hrecv, sum_send_a, sum_recv_a, sum_send_b, sum_recv_b):
    me_x = lax.axis_index("gx")
    me_y = lax.axis_index("gy")
    up_x = lax.rem(me_x + 1, nx)
    dn_x = lax.rem(me_x + nx - 1, nx)
    up_y = lax.rem(me_y + 1, ny)
    dn_y = lax.rem(me_y + ny - 1, ny)
    near = (up_x, dn_x, up_y, dn_y, me_x, me_y)
    top = rows - 8

    loads = [
        pltpu.make_async_copy(hbm, vmem, load_sem.at[k])
        for k, (hbm, vmem) in enumerate(((lam_hbm, lam_ref), (vel_hbm, vel_in), (blk_hbm, blk_ref)))
    ]
    for load in loads:
        load.start()

    barrier = pltpu.get_barrier_semaphore()
    for k in range(1, ny):
        pl.semaphore_signal(barrier, inc=1, device_id=(me_x, lax.rem(me_y + k, ny)), device_id_type=MESH)
    for k in range(1, nx):
        pl.semaphore_signal(barrier, inc=1, device_id=(lax.rem(me_x + k, nx), me_y), device_id_type=MESH)
    for dev in ((up_x, up_y), (up_x, dn_y), (dn_x, up_y), (dn_x, dn_y)):
        pl.semaphore_signal(barrier, inc=1, device_id=dev, device_id_type=MESH)

    loads[1].wait()
    loads[2].wait()
    for step in range(STEPS):
        for axis in range(3):
            vel_ref[step, axis] = vel_in[step, axis].astype(jnp.float32)
    level = lax.rem(lax.broadcasted_iota(jnp.int32, (rows, 128), 0), 4)
    from_below = pltpu.roll(blk_ref[4], 1, 0)
    from_above = pltpu.roll(blk_ref[5], rows - 1, 0)
    solid = jnp.where(level == 3, from_below, from_above)
    fluid_ref[...] = 1.0 - solid.astype(jnp.float32)

    last_flow = [vel_ref[STEPS - 1, axis] for axis in range(3)]
    fluid_all = fluid_ref[...]
    for number in range(1, 19):
        weight = drag_weight(number, last_flow, fluid_all)
        hfield[number - 1] = jnp.where(blk_ref[number - 1] == 1, 0.0, weight)

    pl.semaphore_wait(barrier, nx + ny + 2)

    lam_sets = crossing(MOVING)
    h_sets = crossing(REVERSED)
    h_speeds = dict(REVERSED)
    lam_speeds = dict(MOVING)
    n_hi = len(lam_sets[2])
    n_lo = len(lam_sets[3])
    h_bufs = (
        hxhi,
        hxlo,
        lambda n: unpack_edge(yhi.at[0], n_hi + h_sets[2].index(n), 0),
        lambda n: unpack_edge(ylo.at[0], n_lo + h_sets[3].index(n), 127),
        hcorner,
    )
    h_copies = None
    sent = []
    drag_acc = jnp.zeros((8, 128), jnp.float32)

    for step in range(STEPS):
        src = lam_ref if step == 0 else state
        origin = lam_hbm if step == 0 else state
        bufs = (
            xhi.at[step],
            xlo.at[step],
            lambda n, s=step: unpack_edge(yhi.at[s], lam_sets[2].index(n), 0),
            lambda n, s=step: unpack_edge(ylo.at[s], lam_sets[3].index(n), 127),
            corner.at[step],
        )
        plan = send_plan(lam_sets, lam_speeds, lambda n: origin.at[n], bufs, top, near)
        copies = start_copies(plan, ssem.at[step], rsem.at[step])
        if step == 0:
            h_plan = send_plan(h_sets, h_speeds, lambda n: hfield.at[n - 1], h_bufs, top, near)
            h_copies = start_copies(h_plan, hsend, hrecv)
            loads[0].wait()
        to_low = [src[n] for n in lam_sets[2]]
        to_high = [src[n] for n in lam_sets[3]]
        if step == 0:
            to_low += [hfield[n - 1] for n in h_sets[2]]
            to_high += [hfield[n - 1] for n in h_sets[3]]
        ypack[step, 0] = pack_edge(to_low, 0, rows)
        ypack[step, 1] = pack_edge(to_high, 127, rows)
        copies += start_copies(
            [(ypack.at[step, 0], yhi.at[step], (me_x, dn_y)), (ypack.at[step, 1], ylo.at[step], (me_x, up_y))],
            ysend.at[step],
            yrecv.at[step],
        )
        if step == STEPS - 1:
            for copy in h_copies:
                copy.wait_recv()
            sent += h_copies
            total = drag_acc
            for number in range(1, 19):
                gathered = shifted(hfield[number - 1], h_speeds[number], number, h_sets, h_bufs, rows)
                total = total + jnp.sum((src[number] * gathered).reshape(rows // 8, 8, 128), axis=0)
            for number in range(1, 19):
                cx = lattice_speeds[number][0]
                weight = drag_weight(number, last_flow, fluid_all)
                bounced = jnp.where(blk_ref[number - 1] == 1, src[opposite_of(number)] + 2.0 * cx, 0.0)
                total = total + jnp.sum((weight * bounced).reshape(rows // 8, 8, 128), axis=0)
            part[...] = jnp.broadcast_to(jnp.sum(total), (8, 128))
            row_copies = []
            for k in range(1, ny):
                copy = pltpu.make_async_remote_copy(
                    src_ref=part, dst_ref=row_buf.at[me_y], send_sem=sum_send_a.at[k],
                    recv_sem=sum_recv_a.at[k], device_id=(me_x, lax.rem(me_y + k, ny)),
                    device_id_type=MESH)
                copy.start()
                row_copies.append(copy)
            row_buf[me_y] = part[...]
        for copy in copies:
            copy.wait_recv()
        sent += copies

        moved[0] = src[0]
        for number in range(1, 19):
            source = shifted(src[number], lam_speeds[number], number, lam_sets, bufs, rows)
            bounced = src[opposite_of(number)] + 2.0 * lam_speeds[number][0]
            moved[number] = jnp.where(blk_ref[number - 1] == 1, bounced, source)

        if step == STEPS - 1:
            for copy in row_copies:
                copy.wait_recv()
            sent += row_copies
            total = row_buf[0]
            for j in range(1, ny):
                total = total + row_buf[j]
            row_sum[...] = total
            col_copies = []
            for k in range(1, nx):
                copy = pltpu.make_async_remote_copy(
                    src_ref=row_sum, dst_ref=col_buf.at[me_x], send_sem=sum_send_b.at[k],
                    recv_sem=sum_recv_b.at[k], device_id=(lax.rem(me_x + k, nx), me_y),
                    device_id_type=MESH)
                copy.start()
                col_copies.append(copy)
            col_buf[me_x] = total

        dest = out_ref if step == STEPS - 1 else state

        def chunk(c, acc):
            at = pl.ds(pl.multiple_of(c * 8, 8), 8)
            flow = [vel_ref[step, axis, at] for axis in range(3)]
            mu = [moved[number, at] for number in range(19)]
            fresh, drag = collide(mu, flow, fluid_ref[at])
            for number in range(19):
                dest[number, at] = fresh[number]
            return acc + drag

        if step < STEPS - 1:
            drag_acc = lax.fori_loop(0, rows // 8, chunk, drag_acc)
        else:
            lax.fori_loop(0, rows // 8, chunk, drag_acc)

    for copy in col_copies:
        copy.wait_recv()
    sent += col_copies
    total = col_buf[0]
    for j in range(1, nx):
        total = total + col_buf[j]
    drag_ref[0] = -scale * total[0, 0]
    for copy in sent:
        copy.wait_send()


def per_device(adjoint_in, velocity, solid_tiles, link_blocked):
    nx = lax.axis_size("gx")
    ny = lax.axis_size("gy")
    q, rows_x, levels, rows_y = adjoint_in.shape
    rows = rows_x * levels
    lam = adjoint_in.reshape(q, rows, rows_y)
    flow = velocity.reshape(STEPS, 3, rows, rows_y)
    blocked = link_blocked.reshape(q - 1, rows, rows_y)
    cell_count = rows_x * nx * rows_y * ny * levels
    scale = drag_factor / math.sqrt(cell_count)
    vmem = pl.BlockSpec(memory_space=pltpu.VMEM)
    state, drag = pl.pallas_call(
        functools.partial(lbm_kernel, nx, ny, rows, scale),
        out_shape=(
            jax.ShapeDtypeStruct((q, rows, rows_y), jnp.float32),
            jax.ShapeDtypeStruct((1,), jnp.float32),
        ),
        in_specs=[pl.BlockSpec(memory_space=pl.ANY)] * 3,
        out_specs=(vmem, pl.BlockSpec(memory_space=pltpu.SMEM)),
        scratch_shapes=[
            pltpu.VMEM((q, rows, rows_y), jnp.float32),
            pltpu.VMEM((STEPS, 3, rows, rows_y), velocity.dtype),
            pltpu.VMEM((q - 1, rows, rows_y), link_blocked.dtype),
            pltpu.SemaphoreType.DMA((3,)),
            pltpu.VMEM((STEPS, 3, rows, rows_y), jnp.float32),
            pltpu.VMEM((rows, rows_y), jnp.float32),
            pltpu.VMEM((q, rows, rows_y), jnp.float32),
            pltpu.VMEM((q, rows, rows_y), jnp.float32),
            pltpu.VMEM((q - 1, rows, rows_y), jnp.float32),
        ]
        + [
            pltpu.VMEM((STEPS, len(s), 8, rows_y), jnp.float32)
            for face, s in enumerate(crossing(MOVING)) if face in (0, 1)
        ]
        + [pltpu.VMEM((STEPS, rows, rows_y), jnp.float32)] * 2
        + [pltpu.VMEM((STEPS, len(crossing(MOVING)[4]), 8, rows_y), jnp.float32)]
        + [
            pltpu.VMEM((len(s), 8, rows_y), jnp.float32)
            for face, s in enumerate(crossing(REVERSED)) if face in (0, 1, 4)
        ]
        + [
            pltpu.VMEM((STEPS, 2, rows, rows_y), jnp.float32),
            pltpu.SemaphoreType.DMA((STEPS, 2)),
            pltpu.SemaphoreType.DMA((STEPS, 2)),
        ]
        + [
            pltpu.VMEM((8, 128), jnp.float32),
            pltpu.VMEM((ny, 8, 128), jnp.float32),
            pltpu.VMEM((nx, 8, 128), jnp.float32),
            pltpu.VMEM((8, 128), jnp.float32),
            pltpu.SemaphoreType.DMA((STEPS, N_COPIES)),
            pltpu.SemaphoreType.DMA((STEPS, N_COPIES)),
            pltpu.SemaphoreType.DMA((N_COPIES,)),
            pltpu.SemaphoreType.DMA((N_COPIES,)),
            pltpu.SemaphoreType.DMA((ny,)),
            pltpu.SemaphoreType.DMA((ny,)),
            pltpu.SemaphoreType.DMA((nx,)),
            pltpu.SemaphoreType.DMA((nx,)),
        ],
        compiler_params=pltpu.CompilerParams(collective_id=0, has_side_effects=True),
    )(lam, flow, blocked)
    return (state.reshape(q, rows_x, levels, rows_y), drag)


def solution(mesh):
    placed = (
        P(None, "gx", None, "gy"),
        P(None, None, "gx", None, "gy"),
        P("gx", None, "gy"),
        P(None, "gx", None, "gy"),
    )
    return jax.shard_map(
        per_device,
        mesh=mesh,
        in_specs=placed,
        out_specs=(P(None, "gx", None, "gy"), P()),
        check_vma=False,
    )
```

```python
import functools
import math

import jax
import jax.numpy as jnp
from jax import lax
from jax.experimental import pallas as pl
from jax.experimental.pallas import tpu as pltpu
from jax.sharding import PartitionSpec as P

MESH = pl.DeviceIdType.MESH
TILE = 4
STEPS = 2

lattice_speeds = (
    (0, 0, 0),
    (1, 0, 0),
    (-1, 0, 0),
    (0, 1, 0),
    (0, -1, 0),
    (0, 0, 1),
    (0, 0, -1),
    (1, 1, 0),
    (-1, -1, 0),
    (1, -1, 0),
    (-1, 1, 0),
    (1, 0, 1),
    (-1, 0, -1),
    (1, 0, -1),
    (-1, 0, 1),
    (0, 1, 1),
    (0, -1, -1),
    (0, 1, -1),
    (0, -1, 1),
)
lattice_weights = (1.0 / 3.0,) + (1.0 / 18.0,) * 6 + (1.0 / 36.0,) * 12
relax_rate = 1.6
drag_factor = 20.0


def crossing(speeds):
    return (
        tuple(n for n, c in speeds if c[0] == 1),
        tuple(n for n, c in speeds if c[0] == -1),
        tuple(n for n, c in speeds if c[1] == 1),
        tuple(n for n, c in speeds if c[1] == -1),
        tuple(n for n, c in speeds if c[0] != 0 and c[1] != 0),
    )


MOVING = tuple((n, lattice_speeds[n]) for n in range(1, 19))
REVERSED = tuple((n, tuple(-v for v in lattice_speeds[n])) for n in range(1, 19))
N_COPIES = len(crossing(MOVING)[4])


def opposite_of(number):
    return number + 1 if number % 2 == 1 else number - 1


def along_of(speed, flow):
    along = None
    for axis in range(3):
        if speed[axis] == 0:
            continue
        term = flow[axis] if speed[axis] == 1 else -flow[axis]
        along = term if along is None else along + term
    return along


def collide(moved, flow, fluid):
    speed_sq = flow[0] * flow[0] + flow[1] * flow[1] + flow[2] * flow[2]
    scalar_part = None
    vector_part = [None, None, None]
    drag_local = None
    for number in range(19):
        speed = lattice_speeds[number]
        weighted = lattice_weights[number] * moved[number]
        along = along_of(speed, flow)
        if along is None:
            scalar_term = weighted * (1.0 - 1.5 * speed_sq)
        else:
            scalar_term = weighted * (1.0 + 3.0 * along + 4.5 * along * along - 1.5 * speed_sq)
            drag_term = 3.0 * weighted * along
            drag_local = drag_term if drag_local is None else drag_local + drag_term
        scalar_part = scalar_term if scalar_part is None else scalar_part + scalar_term
        for axis in range(3):
            if speed[axis] == 0:
                term = weighted * (-3.0 * flow[axis])
            else:
                term = weighted * (3.0 * speed[axis] + 9.0 * along * speed[axis] - 3.0 * flow[axis])
            vector_part[axis] = term if vector_part[axis] is None else vector_part[axis] + term
    results = []
    for number in range(19):
        speed = lattice_speeds[number]
        projected = scalar_part
        for axis in range(3):
            projected = projected + vector_part[axis] * (speed[axis] - flow[axis])
        results.append(fluid * ((1.0 - relax_rate) * moved[number] + relax_rate * projected))
    return results, fluid * drag_local


def send_plan(sets, speeds, field, bufs, top, near):
    up_x, dn_x, up_y, dn_y, me_x, me_y = near
    x_high, x_low, _, _, corners = sets
    xhi, xlo, _, _, corner = bufs
    plan = []
    for j, n in enumerate(corners):
        cx, cy, _ = speeds[n]
        rows_at = pl.ds(0, 8) if cx == 1 else pl.ds(top, 8)
        dev_x = dn_x if cx == 1 else up_x
        dev_y = dn_y if cy == 1 else up_y
        plan.append((field(n).at[rows_at], corner.at[j], (dev_x, dev_y)))
    return plan


def start_copies(plan, send_sems, recv_sems):
    copies = []
    for k, (from_ref, to_ref, dev) in enumerate(plan):
        copy = pltpu.make_async_remote_copy(
            src_ref=from_ref, dst_ref=to_ref, send_sem=send_sems.at[k],
            recv_sem=recv_sems.at[k], device_id=dev, device_id_type=MESH)
        copy.start()
        copies.append(copy)
    return copies


def shifted(own, speed, n, sets, bufs, rows):
    x_high, x_low, y_high, y_low, corners = sets
    xhi, xlo, yhi, ylo, corner = bufs
    cx, cy, cz = speed
    top = rows - 8
    row8 = lax.broadcasted_iota(jnp.int32, (8, 128), 0)
    lane = lax.broadcasted_iota(jnp.int32, (rows, 128), 1)
    level = lax.rem(lax.broadcasted_iota(jnp.int32, (rows, 128), 0), 4)

    def patch_x(block, tile):
        if cx == 1:
            head = jnp.where(row8 < 4, tile, block[0:8])
            return jnp.concatenate([head, block[8:]], axis=0)
        tail = jnp.where(row8 >= 4, tile, block[top:])
        return jnp.concatenate([block[:top], tail], axis=0)

    if cx == 1:
        own = patch_x(own, xhi(n))
    elif cx == -1:
        own = patch_x(own, xlo(n))
    if cy != 0:
        side = yhi(n) if cy == 1 else ylo(n)
        if cx != 0:
            side = patch_x(side, corner[corners.index(n)])
        edge = 0 if cy == 1 else 127
        own = jnp.where(lane == edge, side, own)
    shift = 4 * cx + cz
    if shift % rows:
        own = pltpu.roll(own, (-shift) % rows, 0)
    if cy != 0:
        own = pltpu.roll(own, (-cy) % 128, 1)
    if cz == 1:
        own = jnp.where(level == 3, 0.0, own)
    elif cz == -1:
        own = jnp.where(level == 0, 0.0, own)
    return own


def pack_edge(fields, from_lane, rows):
    lane = lax.broadcasted_iota(jnp.int32, (rows, 128), 1)
    packed = jnp.zeros((rows, 128), jnp.float32)
    for k, field in enumerate(fields):
        moved = field if k == from_lane else pltpu.roll(field, (k - from_lane) % 128, 1)
        packed = jnp.where(lane == k, moved, packed)
    return packed


def pack_rows(tiles, low_half):
    row8 = lax.broadcasted_iota(jnp.int32, (8, 128), 0)
    if len(tiles) % 2:
        tiles = tiles + [jnp.zeros((8, 128), jnp.float32)]
    packed = []
    for a, b in zip(tiles[0::2], tiles[1::2]):
        if low_half:
            packed.append(jnp.where(row8 < 4, a, pltpu.roll(b, 4, 0)))
        else:
            packed.append(jnp.where(row8 >= 4, b, pltpu.roll(a, 4, 0)))
    return jnp.concatenate(packed, axis=0)


def unpack_rows(packed_ref, k, low_half):
    tile = packed_ref[pl.ds(8 * (k // 2), 8)]
    if (k % 2 == 0) == low_half:
        return tile
    return pltpu.roll(tile, 4, 0)


def unpack_edge(packed_ref, k, to_lane):
    packed = packed_ref[...]
    return packed if k == to_lane else pltpu.roll(packed, (to_lane - k) % 128, 1)


def drag_weight(number, flow, fluid):
    return (3.0 * lattice_weights[number]) * along_of(lattice_speeds[number], flow) * fluid


def lbm_kernel(nx, ny, rows, scale, lam_hbm, vel_hbm, blk_hbm, out_ref, drag_ref,
               lam_ref, vel_in, blk_ref, load_sem, vel_ref, fluid_ref, moved, state, hfield, xhi, xlo, yhi, ylo, corner, hcorner, ypack, ysend, yrecv,
               xpack_lo, xpack_hi, xsend, xrecv,
               part, row_buf, col_buf, row_sum,
               ssem, rsem, hsend, hrecv, sum_send_a, sum_recv_a, sum_send_b, sum_recv_b):
    me_x = lax.axis_index("gx")
    me_y = lax.axis_index("gy")
    up_x = lax.rem(me_x + 1, nx)
    dn_x = lax.rem(me_x + nx - 1, nx)
    up_y = lax.rem(me_y + 1, ny)
    dn_y = lax.rem(me_y + ny - 1, ny)
    near = (up_x, dn_x, up_y, dn_y, me_x, me_y)
    top = rows - 8

    loads = [
        pltpu.make_async_copy(hbm, vmem, load_sem.at[k])
        for k, (hbm, vmem) in enumerate(((lam_hbm, lam_ref), (vel_hbm, vel_in), (blk_hbm, blk_ref)))
    ]
    for load in loads:
        load.start()

    barrier = pltpu.get_barrier_semaphore()
    for k in range(1, ny):
        pl.semaphore_signal(barrier, inc=1, device_id=(me_x, lax.rem(me_y + k, ny)), device_id_type=MESH)
    for k in range(1, nx):
        pl.semaphore_signal(barrier, inc=1, device_id=(lax.rem(me_x + k, nx), me_y), device_id_type=MESH)
    for dev in ((up_x, up_y), (up_x, dn_y), (dn_x, up_y), (dn_x, dn_y)):
        pl.semaphore_signal(barrier, inc=1, device_id=dev, device_id_type=MESH)

    loads[1].wait()
    loads[2].wait()
    for step in range(STEPS):
        for axis in range(3):
            vel_ref[step, axis] = vel_in[step, axis].astype(jnp.float32)
    level = lax.rem(lax.broadcasted_iota(jnp.int32, (rows, 128), 0), 4)
    from_below = pltpu.roll(blk_ref[4], 1, 0)
    from_above = pltpu.roll(blk_ref[5], rows - 1, 0)
    solid = jnp.where(level == 3, from_below, from_above)
    fluid_ref[...] = 1.0 - solid.astype(jnp.float32)

    last_flow = [vel_ref[STEPS - 1, axis] for axis in range(3)]
    fluid_all = fluid_ref[...]
    for number in range(1, 19):
        weight = drag_weight(number, last_flow, fluid_all)
        hfield[number - 1] = jnp.where(blk_ref[number - 1] == 1, 0.0, weight)

    pl.semaphore_wait(barrier, nx + ny + 2)

    lam_sets = crossing(MOVING)
    h_sets = crossing(REVERSED)
    h_speeds = dict(REVERSED)
    lam_speeds = dict(MOVING)
    n_hi = len(lam_sets[2])
    n_lo = len(lam_sets[3])
    nx_hi = len(lam_sets[0])
    nx_lo = len(lam_sets[1])
    h_bufs = (
        lambda n: unpack_rows(xhi.at[0], nx_hi + h_sets[0].index(n), True),
        lambda n: unpack_rows(xlo.at[0], nx_lo + h_sets[1].index(n), False),
        lambda n: unpack_edge(yhi.at[0], n_hi + h_sets[2].index(n), 0),
        lambda n: unpack_edge(ylo.at[0], n_lo + h_sets[3].index(n), 127),
        hcorner,
    )
    h_copies = None
    sent = []
    drag_acc = jnp.zeros((8, 128), jnp.float32)

    for step in range(STEPS):
        src = lam_ref if step == 0 else state
        origin = lam_hbm if step == 0 else state
        bufs = (
            lambda n, s=step: unpack_rows(xhi.at[s], lam_sets[0].index(n), True),
            lambda n, s=step: unpack_rows(xlo.at[s], lam_sets[1].index(n), False),
            lambda n, s=step: unpack_edge(yhi.at[s], lam_sets[2].index(n), 0),
            lambda n, s=step: unpack_edge(ylo.at[s], lam_sets[3].index(n), 127),
            corner.at[step],
        )
        plan = send_plan(lam_sets, lam_speeds, lambda n: origin.at[n], bufs, top, near)
        copies = start_copies(plan, ssem.at[step], rsem.at[step])
        if step == 0:
            h_plan = send_plan(h_sets, h_speeds, lambda n: hfield.at[n - 1], h_bufs, top, near)
            h_copies = start_copies(h_plan, hsend, hrecv)
            loads[0].wait()
        to_low = [src[n] for n in lam_sets[2]]
        to_high = [src[n] for n in lam_sets[3]]
        if step == 0:
            to_low += [hfield[n - 1] for n in h_sets[2]]
            to_high += [hfield[n - 1] for n in h_sets[3]]
        x_low_tiles = [src[n, 0:8] for n in lam_sets[0]]
        x_high_tiles = [src[n, top:rows] for n in lam_sets[1]]
        if step == 0:
            x_low_tiles += [hfield[n - 1, 0:8] for n in h_sets[0]]
            x_high_tiles += [hfield[n - 1, top:rows] for n in h_sets[1]]
        count_lo = (len(x_low_tiles) + 1) // 2
        count_hi = (len(x_high_tiles) + 1) // 2
        xpack_lo[step, pl.ds(0, 8 * count_lo)] = pack_rows(x_low_tiles, True)
        xpack_hi[step, pl.ds(0, 8 * count_hi)] = pack_rows(x_high_tiles, False)
        copies += start_copies(
            [
                (xpack_lo.at[step, pl.ds(0, 8 * count_lo)], xhi.at[step, pl.ds(0, 8 * count_lo)], (dn_x, me_y)),
                (xpack_hi.at[step, pl.ds(0, 8 * count_hi)], xlo.at[step, pl.ds(0, 8 * count_hi)], (up_x, me_y)),
            ],
            xsend.at[step],
            xrecv.at[step],
        )
        ypack[step, 0] = pack_edge(to_low, 0, rows)
        ypack[step, 1] = pack_edge(to_high, 127, rows)
        copies += start_copies(
            [(ypack.at[step, 0], yhi.at[step], (me_x, dn_y)), (ypack.at[step, 1], ylo.at[step], (me_x, up_y))],
            ysend.at[step],
            yrecv.at[step],
        )
        if step == STEPS - 1:
            for copy in h_copies:
                copy.wait_recv()
            sent += h_copies
            total = drag_acc
            for number in range(1, 19):
                gathered = shifted(hfield[number - 1], h_speeds[number], number, h_sets, h_bufs, rows)
                total = total + jnp.sum((src[number] * gathered).reshape(rows // 8, 8, 128), axis=0)
            for number in range(1, 19):
                cx = lattice_speeds[number][0]
                weight = drag_weight(number, last_flow, fluid_all)
                bounced = jnp.where(blk_ref[number - 1] == 1, src[opposite_of(number)] + 2.0 * cx, 0.0)
                total = total + jnp.sum((weight * bounced).reshape(rows // 8, 8, 128), axis=0)
            part[...] = jnp.broadcast_to(jnp.sum(total), (8, 128))
            row_copies = []
            for k in range(1, ny):
                copy = pltpu.make_async_remote_copy(
                    src_ref=part, dst_ref=row_buf.at[me_y], send_sem=sum_send_a.at[k],
                    recv_sem=sum_recv_a.at[k], device_id=(me_x, lax.rem(me_y + k, ny)),
                    device_id_type=MESH)
                copy.start()
                row_copies.append(copy)
            row_buf[me_y] = part[...]
        for copy in copies:
            copy.wait_recv()
        sent += copies

        moved[0] = src[0]
        for number in range(1, 19):
            source = shifted(src[number], lam_speeds[number], number, lam_sets, bufs, rows)
            bounced = src[opposite_of(number)] + 2.0 * lam_speeds[number][0]
            moved[number] = jnp.where(blk_ref[number - 1] == 1, bounced, source)

        if step == STEPS - 1:
            for copy in row_copies:
                copy.wait_recv()
            sent += row_copies
            total = row_buf[0]
            for j in range(1, ny):
                total = total + row_buf[j]
            row_sum[...] = total
            col_copies = []
            for k in range(1, nx):
                copy = pltpu.make_async_remote_copy(
                    src_ref=row_sum, dst_ref=col_buf.at[me_x], send_sem=sum_send_b.at[k],
                    recv_sem=sum_recv_b.at[k], device_id=(lax.rem(me_x + k, nx), me_y),
                    device_id_type=MESH)
                copy.start()
                col_copies.append(copy)
            col_buf[me_x] = total

        dest = out_ref if step == STEPS - 1 else state

        def chunk(c, acc):
            at = pl.ds(pl.multiple_of(c * 8, 8), 8)
            flow = [vel_ref[step, axis, at] for axis in range(3)]
            mu = [moved[number, at] for number in range(19)]
            fresh, drag = collide(mu, flow, fluid_ref[at])
            for number in range(19):
                dest[number, at] = fresh[number]
            return acc + drag

        if step < STEPS - 1:
            drag_acc = lax.fori_loop(0, rows // 8, chunk, drag_acc)
        else:
            lax.fori_loop(0, rows // 8, chunk, drag_acc)

    for copy in col_copies:
        copy.wait_recv()
    sent += col_copies
    total = col_buf[0]
    for j in range(1, nx):
        total = total + col_buf[j]
    drag_ref[0] = -scale * total[0, 0]
    for copy in sent:
        copy.wait_send()


def per_device(adjoint_in, velocity, solid_tiles, link_blocked):
    nx = lax.axis_size("gx")
    ny = lax.axis_size("gy")
    q, rows_x, levels, rows_y = adjoint_in.shape
    rows = rows_x * levels
    lam = adjoint_in.reshape(q, rows, rows_y)
    flow = velocity.reshape(STEPS, 3, rows, rows_y)
    blocked = link_blocked.reshape(q - 1, rows, rows_y)
    cell_count = rows_x * nx * rows_y * ny * levels
    scale = drag_factor / math.sqrt(cell_count)
    vmem = pl.BlockSpec(memory_space=pltpu.VMEM)
    x_tiles = max(
        (len(crossing(MOVING)[face]) + len(crossing(REVERSED)[face]) + 1) // 2 for face in (0, 1)
    )
    state, drag = pl.pallas_call(
        functools.partial(lbm_kernel, nx, ny, rows, scale),
        out_shape=(
            jax.ShapeDtypeStruct((q, rows, rows_y), jnp.float32),
            jax.ShapeDtypeStruct((1,), jnp.float32),
        ),
        in_specs=[pl.BlockSpec(memory_space=pl.ANY)] * 3,
        out_specs=(vmem, pl.BlockSpec(memory_space=pltpu.SMEM)),
        scratch_shapes=[
            pltpu.VMEM((q, rows, rows_y), jnp.float32),
            pltpu.VMEM((STEPS, 3, rows, rows_y), velocity.dtype),
            pltpu.VMEM((q - 1, rows, rows_y), link_blocked.dtype),
            pltpu.SemaphoreType.DMA((3,)),
            pltpu.VMEM((STEPS, 3, rows, rows_y), jnp.float32),
            pltpu.VMEM((rows, rows_y), jnp.float32),
            pltpu.VMEM((q, rows, rows_y), jnp.float32),
            pltpu.VMEM((q, rows, rows_y), jnp.float32),
            pltpu.VMEM((q - 1, rows, rows_y), jnp.float32),
        ]
        + [pltpu.VMEM((STEPS, 8 * x_tiles, rows_y), jnp.float32)] * 2
        + [pltpu.VMEM((STEPS, rows, rows_y), jnp.float32)] * 2
        + [pltpu.VMEM((STEPS, len(crossing(MOVING)[4]), 8, rows_y), jnp.float32)]
        + [pltpu.VMEM((len(crossing(REVERSED)[4]), 8, rows_y), jnp.float32)]
        + [
            pltpu.VMEM((STEPS, 2, rows, rows_y), jnp.float32),
            pltpu.SemaphoreType.DMA((STEPS, 2)),
            pltpu.SemaphoreType.DMA((STEPS, 2)),
            pltpu.VMEM((STEPS, 8 * x_tiles, rows_y), jnp.float32),
            pltpu.VMEM((STEPS, 8 * x_tiles, rows_y), jnp.float32),
            pltpu.SemaphoreType.DMA((STEPS, 2)),
            pltpu.SemaphoreType.DMA((STEPS, 2)),
        ]
        + [
            pltpu.VMEM((8, 128), jnp.float32),
            pltpu.VMEM((ny, 8, 128), jnp.float32),
            pltpu.VMEM((nx, 8, 128), jnp.float32),
            pltpu.VMEM((8, 128), jnp.float32),
            pltpu.SemaphoreType.DMA((STEPS, N_COPIES)),
            pltpu.SemaphoreType.DMA((STEPS, N_COPIES)),
            pltpu.SemaphoreType.DMA((N_COPIES,)),
            pltpu.SemaphoreType.DMA((N_COPIES,)),
            pltpu.SemaphoreType.DMA((ny,)),
            pltpu.SemaphoreType.DMA((ny,)),
            pltpu.SemaphoreType.DMA((nx,)),
            pltpu.SemaphoreType.DMA((nx,)),
        ],
        compiler_params=pltpu.CompilerParams(collective_id=0, has_side_effects=True),
    )(lam, flow, blocked)
    return (state.reshape(q, rows_x, levels, rows_y), drag)


def solution(mesh):
    placed = (
        P(None, "gx", None, "gy"),
        P(None, None, "gx", None, "gy"),
        P("gx", None, "gy"),
        P(None, "gx", None, "gy"),
    )
    return jax.shard_map(
        per_device,
        mesh=mesh,
        in_specs=placed,
        out_specs=(P(None, "gx", None, "gy"), P()),
        check_vma=False,
    )
```

```python
import functools
import math

import jax
import jax.numpy as jnp
from jax import lax
from jax.experimental import pallas as pl
from jax.experimental.pallas import tpu as pltpu
from jax.sharding import PartitionSpec as P

MESH = pl.DeviceIdType.MESH
TILE = 4
STEPS = 2

lattice_speeds = (
    (0, 0, 0),
    (1, 0, 0),
    (-1, 0, 0),
    (0, 1, 0),
    (0, -1, 0),
    (0, 0, 1),
    (0, 0, -1),
    (1, 1, 0),
    (-1, -1, 0),
    (1, -1, 0),
    (-1, 1, 0),
    (1, 0, 1),
    (-1, 0, -1),
    (1, 0, -1),
    (-1, 0, 1),
    (0, 1, 1),
    (0, -1, -1),
    (0, 1, -1),
    (0, -1, 1),
)
lattice_weights = (1.0 / 3.0,) + (1.0 / 18.0,) * 6 + (1.0 / 36.0,) * 12
relax_rate = 1.6
drag_factor = 20.0


def crossing(speeds):
    return (
        tuple(n for n, c in speeds if c[0] == 1),
        tuple(n for n, c in speeds if c[0] == -1),
        tuple(n for n, c in speeds if c[1] == 1),
        tuple(n for n, c in speeds if c[1] == -1),
        tuple(n for n, c in speeds if c[0] != 0 and c[1] != 0),
    )


MOVING = tuple((n, lattice_speeds[n]) for n in range(1, 19))
REVERSED = tuple((n, tuple(-v for v in lattice_speeds[n])) for n in range(1, 19))
N_COPIES = len(crossing(MOVING)[4])


def opposite_of(number):
    return number + 1 if number % 2 == 1 else number - 1


def along_of(speed, flow):
    along = None
    for axis in range(3):
        if speed[axis] == 0:
            continue
        term = flow[axis] if speed[axis] == 1 else -flow[axis]
        along = term if along is None else along + term
    return along


def collide(moved, flow, fluid):
    speed_sq = flow[0] * flow[0] + flow[1] * flow[1] + flow[2] * flow[2]
    scalar_part = None
    vector_part = [None, None, None]
    drag_local = None
    for number in range(19):
        speed = lattice_speeds[number]
        weighted = lattice_weights[number] * moved[number]
        along = along_of(speed, flow)
        if along is None:
            scalar_term = weighted * (1.0 - 1.5 * speed_sq)
        else:
            scalar_term = weighted * (1.0 + 3.0 * along + 4.5 * along * along - 1.5 * speed_sq)
            drag_term = 3.0 * weighted * along
            drag_local = drag_term if drag_local is None else drag_local + drag_term
        scalar_part = scalar_term if scalar_part is None else scalar_part + scalar_term
        for axis in range(3):
            if speed[axis] == 0:
                term = weighted * (-3.0 * flow[axis])
            else:
                term = weighted * (3.0 * speed[axis] + 9.0 * along * speed[axis] - 3.0 * flow[axis])
            vector_part[axis] = term if vector_part[axis] is None else vector_part[axis] + term
    results = []
    for number in range(19):
        speed = lattice_speeds[number]
        projected = scalar_part
        for axis in range(3):
            projected = projected + vector_part[axis] * (speed[axis] - flow[axis])
        results.append(fluid * ((1.0 - relax_rate) * moved[number] + relax_rate * projected))
    return results, fluid * drag_local


def send_plan(sets, speeds, field, bufs, top, near):
    up_x, dn_x, up_y, dn_y, me_x, me_y = near
    x_high, x_low, _, _, corners = sets
    xhi, xlo, _, _, corner = bufs
    plan = []
    for j, n in enumerate(corners):
        cx, cy, _ = speeds[n]
        rows_at = pl.ds(0, 8) if cx == 1 else pl.ds(top, 8)
        dev_x = dn_x if cx == 1 else up_x
        dev_y = dn_y if cy == 1 else up_y
        plan.append((field(n).at[rows_at], corner.at[j], (dev_x, dev_y)))
    return plan


def start_copies(plan, send_sems, recv_sems):
    copies = []
    for k, (from_ref, to_ref, dev) in enumerate(plan):
        copy = pltpu.make_async_remote_copy(
            src_ref=from_ref, dst_ref=to_ref, send_sem=send_sems.at[k],
            recv_sem=recv_sems.at[k], device_id=dev, device_id_type=MESH)
        copy.start()
        copies.append(copy)
    return copies


def shifted(own, speed, n, sets, bufs, rows):
    x_high, x_low, y_high, y_low, corners = sets
    xhi, xlo, yhi, ylo, corner = bufs
    cx, cy, cz = speed
    top = rows - 8
    row8 = lax.broadcasted_iota(jnp.int32, (8, 128), 0)
    lane = lax.broadcasted_iota(jnp.int32, (rows, 128), 1)
    level = lax.rem(lax.broadcasted_iota(jnp.int32, (rows, 128), 0), 4)

    def patch_x(block, tile):
        if cx == 1:
            head = jnp.where(row8 < 4, tile, block[0:8])
            return jnp.concatenate([head, block[8:]], axis=0)
        tail = jnp.where(row8 >= 4, tile, block[top:])
        return jnp.concatenate([block[:top], tail], axis=0)

    if cx == 1:
        own = patch_x(own, xhi(n))
    elif cx == -1:
        own = patch_x(own, xlo(n))
    if cy != 0:
        side = yhi(n) if cy == 1 else ylo(n)
        if cx != 0:
            side = patch_x(side, corner[corners.index(n)])
        edge = 0 if cy == 1 else 127
        own = jnp.where(lane == edge, side, own)
    shift = 4 * cx + cz
    if shift % rows:
        own = pltpu.roll(own, (-shift) % rows, 0)
    if cy != 0:
        own = pltpu.roll(own, (-cy) % 128, 1)
    if cz == 1:
        own = jnp.where(level == 3, 0.0, own)
    elif cz == -1:
        own = jnp.where(level == 0, 0.0, own)
    return own


def pack_edge(fields, from_lane, rows):
    lane = lax.broadcasted_iota(jnp.int32, (rows, 128), 1)
    packed = jnp.zeros((rows, 128), jnp.float32)
    for k, field in enumerate(fields):
        moved = field if k == from_lane else pltpu.roll(field, (k - from_lane) % 128, 1)
        packed = jnp.where(lane == k, moved, packed)
    return packed


def pack_rows(tiles, low_half):
    row8 = lax.broadcasted_iota(jnp.int32, (8, 128), 0)
    if len(tiles) % 2:
        tiles = tiles + [jnp.zeros((8, 128), jnp.float32)]
    packed = []
    for a, b in zip(tiles[0::2], tiles[1::2]):
        if low_half:
            packed.append(jnp.where(row8 < 4, a, pltpu.roll(b, 4, 0)))
        else:
            packed.append(jnp.where(row8 >= 4, b, pltpu.roll(a, 4, 0)))
    return jnp.concatenate(packed, axis=0)


def unpack_rows(packed_ref, k, low_half):
    tile = packed_ref[pl.ds(8 * (k // 2), 8)]
    if (k % 2 == 0) == low_half:
        return tile
    return pltpu.roll(tile, 4, 0)


def unpack_edge(packed_ref, k, to_lane):
    packed = packed_ref[...]
    return packed if k == to_lane else pltpu.roll(packed, (to_lane - k) % 128, 1)


def drag_weight(number, flow, fluid):
    return (3.0 * lattice_weights[number]) * along_of(lattice_speeds[number], flow) * fluid


def lbm_kernel(nx, ny, rows, scale, lam_hbm, vel_hbm, blk_hbm, out_ref, drag_ref,
               lam_ref, vel_in, blk_ref, load_sem, vel_ref, fluid_ref, moved, state, hfield, xhi, xlo, yhi, ylo, corner, hcorner, ypack, ysend, yrecv,
               xpack_lo, xpack_hi, xsend, xrecv,
               part, row_buf, col_buf, row_sum,
               ssem, rsem, hsend, hrecv, sum_send_a, sum_recv_a, sum_send_b, sum_recv_b):
    me_x = lax.axis_index("gx")
    me_y = lax.axis_index("gy")
    up_x = lax.rem(me_x + 1, nx)
    dn_x = lax.rem(me_x + nx - 1, nx)
    up_y = lax.rem(me_y + 1, ny)
    dn_y = lax.rem(me_y + ny - 1, ny)
    near = (up_x, dn_x, up_y, dn_y, me_x, me_y)
    top = rows - 8

    loads = [
        pltpu.make_async_copy(hbm, vmem, load_sem.at[k])
        for k, (hbm, vmem) in enumerate(((lam_hbm, lam_ref), (vel_hbm, vel_in), (blk_hbm, blk_ref)))
    ]
    for load in loads:
        load.start()

    half = nx // 2
    my_half = me_x // half
    in_half = lax.rem(me_x, half)
    a_peers = []
    for dz in range(2):
        for k in range(ny):
            if dz == 0 and k == 0:
                continue
            a_peers.append((k + dz * ny, (in_half + lax.rem(my_half + dz, 2) * half, lax.rem(me_y + k, ny))))
    b_peers = [(k, (my_half * half + lax.rem(in_half + k, half), me_y)) for k in range(1, half)]

    barrier = pltpu.get_barrier_semaphore()
    for _, dev in a_peers + b_peers:
        pl.semaphore_signal(barrier, inc=1, device_id=dev, device_id_type=MESH)
    for dev in ((up_x, up_y), (up_x, dn_y), (dn_x, up_y), (dn_x, dn_y), (up_x, me_y), (dn_x, me_y)):
        pl.semaphore_signal(barrier, inc=1, device_id=dev, device_id_type=MESH)

    loads[1].wait()
    loads[2].wait()
    for step in range(STEPS):
        for axis in range(3):
            vel_ref[step, axis] = vel_in[step, axis].astype(jnp.float32)
    level = lax.rem(lax.broadcasted_iota(jnp.int32, (rows, 128), 0), 4)
    from_below = pltpu.roll(blk_ref[4], 1, 0)
    from_above = pltpu.roll(blk_ref[5], rows - 1, 0)
    solid = jnp.where(level == 3, from_below, from_above)
    fluid_ref[...] = 1.0 - solid.astype(jnp.float32)

    last_flow = [vel_ref[STEPS - 1, axis] for axis in range(3)]
    fluid_all = fluid_ref[...]
    for number in range(1, 19):
        weight = drag_weight(number, last_flow, fluid_all)
        hfield[number - 1] = jnp.where(blk_ref[number - 1] == 1, 0.0, weight)

    pl.semaphore_wait(barrier, len(a_peers) + len(b_peers) + 6)

    lam_sets = crossing(MOVING)
    h_sets = crossing(REVERSED)
    h_speeds = dict(REVERSED)
    lam_speeds = dict(MOVING)
    n_hi = len(lam_sets[2])
    n_lo = len(lam_sets[3])
    nx_hi = len(lam_sets[0])
    nx_lo = len(lam_sets[1])
    h_bufs = (
        lambda n: unpack_rows(xhi.at[0], nx_hi + h_sets[0].index(n), True),
        lambda n: unpack_rows(xlo.at[0], nx_lo + h_sets[1].index(n), False),
        lambda n: unpack_edge(yhi.at[0], n_hi + h_sets[2].index(n), 0),
        lambda n: unpack_edge(ylo.at[0], n_lo + h_sets[3].index(n), 127),
        hcorner,
    )
    h_copies = None
    sent = []
    drag_acc = jnp.zeros((8, 128), jnp.float32)

    for step in range(STEPS):
        src = lam_ref if step == 0 else state
        origin = lam_hbm if step == 0 else state
        bufs = (
            lambda n, s=step: unpack_rows(xhi.at[s], lam_sets[0].index(n), True),
            lambda n, s=step: unpack_rows(xlo.at[s], lam_sets[1].index(n), False),
            lambda n, s=step: unpack_edge(yhi.at[s], lam_sets[2].index(n), 0),
            lambda n, s=step: unpack_edge(ylo.at[s], lam_sets[3].index(n), 127),
            corner.at[step],
        )
        plan = send_plan(lam_sets, lam_speeds, lambda n: origin.at[n], bufs, top, near)
        copies = start_copies(plan, ssem.at[step], rsem.at[step])
        if step == 0:
            h_plan = send_plan(h_sets, h_speeds, lambda n: hfield.at[n - 1], h_bufs, top, near)
            h_copies = start_copies(h_plan, hsend, hrecv)
            loads[0].wait()
        to_low = [src[n] for n in lam_sets[2]]
        to_high = [src[n] for n in lam_sets[3]]
        if step == 0:
            to_low += [hfield[n - 1] for n in h_sets[2]]
            to_high += [hfield[n - 1] for n in h_sets[3]]
        x_low_tiles = [src[n, 0:8] for n in lam_sets[0]]
        x_high_tiles = [src[n, top:rows] for n in lam_sets[1]]
        if step == 0:
            x_low_tiles += [hfield[n - 1, 0:8] for n in h_sets[0]]
            x_high_tiles += [hfield[n - 1, top:rows] for n in h_sets[1]]
        count_lo = (len(x_low_tiles) + 1) // 2
        count_hi = (len(x_high_tiles) + 1) // 2
        xpack_lo[step, pl.ds(0, 8 * count_lo)] = pack_rows(x_low_tiles, True)
        xpack_hi[step, pl.ds(0, 8 * count_hi)] = pack_rows(x_high_tiles, False)
        copies += start_copies(
            [
                (xpack_lo.at[step, pl.ds(0, 8 * count_lo)], xhi.at[step, pl.ds(0, 8 * count_lo)], (dn_x, me_y)),
                (xpack_hi.at[step, pl.ds(0, 8 * count_hi)], xlo.at[step, pl.ds(0, 8 * count_hi)], (up_x, me_y)),
            ],
            xsend.at[step],
            xrecv.at[step],
        )
        ypack[step, 0] = pack_edge(to_low, 0, rows)
        ypack[step, 1] = pack_edge(to_high, 127, rows)
        copies += start_copies(
            [(ypack.at[step, 0], yhi.at[step], (me_x, dn_y)), (ypack.at[step, 1], ylo.at[step], (me_x, up_y))],
            ysend.at[step],
            yrecv.at[step],
        )
        if step == STEPS - 1:
            for copy in h_copies:
                copy.wait_recv()
            sent += h_copies
            total = drag_acc
            for number in range(1, 19):
                gathered = shifted(hfield[number - 1], h_speeds[number], number, h_sets, h_bufs, rows)
                total = total + jnp.sum((src[number] * gathered).reshape(rows // 8, 8, 128), axis=0)
            for number in range(1, 19):
                cx = lattice_speeds[number][0]
                weight = drag_weight(number, last_flow, fluid_all)
                bounced = jnp.where(blk_ref[number - 1] == 1, src[opposite_of(number)] + 2.0 * cx, 0.0)
                total = total + jnp.sum((weight * bounced).reshape(rows // 8, 8, 128), axis=0)
            part[...] = jnp.broadcast_to(jnp.sum(total), (8, 128))
            a_slot = my_half * ny + me_y
            row_copies = []
            for k, dev in a_peers:
                copy = pltpu.make_async_remote_copy(
                    src_ref=part, dst_ref=row_buf.at[a_slot], send_sem=sum_send_a.at[k],
                    recv_sem=sum_recv_a.at[k], device_id=dev, device_id_type=MESH)
                copy.start()
                row_copies.append(copy)
            row_buf[a_slot] = part[...]
        for copy in copies:
            copy.wait_recv()
        sent += copies

        moved[0] = src[0]
        for number in range(1, 19):
            source = shifted(src[number], lam_speeds[number], number, lam_sets, bufs, rows)
            bounced = src[opposite_of(number)] + 2.0 * lam_speeds[number][0]
            moved[number] = jnp.where(blk_ref[number - 1] == 1, bounced, source)

        if step == STEPS - 1:
            for copy in row_copies:
                copy.wait_recv()
            sent += row_copies
            total = row_buf[0]
            for j in range(1, 2 * ny):
                total = total + row_buf[j]
            row_sum[...] = total
            col_copies = []
            for k, dev in b_peers:
                copy = pltpu.make_async_remote_copy(
                    src_ref=row_sum, dst_ref=col_buf.at[in_half], send_sem=sum_send_b.at[k],
                    recv_sem=sum_recv_b.at[k], device_id=dev, device_id_type=MESH)
                copy.start()
                col_copies.append(copy)
            col_buf[in_half] = total

        dest = out_ref if step == STEPS - 1 else state

        def chunk(c, acc):
            at = pl.ds(pl.multiple_of(c * 8, 8), 8)
            flow = [vel_ref[step, axis, at] for axis in range(3)]
            mu = [moved[number, at] for number in range(19)]
            fresh, drag = collide(mu, flow, fluid_ref[at])
            for number in range(19):
                dest[number, at] = fresh[number]
            return acc + drag

        if step < STEPS - 1:
            drag_acc = lax.fori_loop(0, rows // 8, chunk, drag_acc)
        else:
            lax.fori_loop(0, rows // 8, chunk, drag_acc)

    for copy in col_copies:
        copy.wait_recv()
    sent += col_copies
    total = col_buf[0]
    for j in range(1, nx // 2):
        total = total + col_buf[j]
    drag_ref[0] = -scale * total[0, 0]
    for copy in sent:
        copy.wait_send()


def per_device(adjoint_in, velocity, solid_tiles, link_blocked):
    nx = lax.axis_size("gx")
    ny = lax.axis_size("gy")
    q, rows_x, levels, rows_y = adjoint_in.shape
    rows = rows_x * levels
    lam = adjoint_in.reshape(q, rows, rows_y)
    flow = velocity.reshape(STEPS, 3, rows, rows_y)
    blocked = link_blocked.reshape(q - 1, rows, rows_y)
    cell_count = rows_x * nx * rows_y * ny * levels
    scale = drag_factor / math.sqrt(cell_count)
    vmem = pl.BlockSpec(memory_space=pltpu.VMEM)
    x_tiles = max(
        (len(crossing(MOVING)[face]) + len(crossing(REVERSED)[face]) + 1) // 2 for face in (0, 1)
    )
    state, drag = pl.pallas_call(
        functools.partial(lbm_kernel, nx, ny, rows, scale),
        out_shape=(
            jax.ShapeDtypeStruct((q, rows, rows_y), jnp.float32),
            jax.ShapeDtypeStruct((1,), jnp.float32),
        ),
        in_specs=[pl.BlockSpec(memory_space=pl.ANY)] * 3,
        out_specs=(vmem, pl.BlockSpec(memory_space=pltpu.SMEM)),
        scratch_shapes=[
            pltpu.VMEM((q, rows, rows_y), jnp.float32),
            pltpu.VMEM((STEPS, 3, rows, rows_y), velocity.dtype),
            pltpu.VMEM((q - 1, rows, rows_y), link_blocked.dtype),
            pltpu.SemaphoreType.DMA((3,)),
            pltpu.VMEM((STEPS, 3, rows, rows_y), jnp.float32),
            pltpu.VMEM((rows, rows_y), jnp.float32),
            pltpu.VMEM((q, rows, rows_y), jnp.float32),
            pltpu.VMEM((q, rows, rows_y), jnp.float32),
            pltpu.VMEM((q - 1, rows, rows_y), jnp.float32),
        ]
        + [pltpu.VMEM((STEPS, 8 * x_tiles, rows_y), jnp.float32)] * 2
        + [pltpu.VMEM((STEPS, rows, rows_y), jnp.float32)] * 2
        + [pltpu.VMEM((STEPS, len(crossing(MOVING)[4]), 8, rows_y), jnp.float32)]
        + [pltpu.VMEM((len(crossing(REVERSED)[4]), 8, rows_y), jnp.float32)]
        + [
            pltpu.VMEM((STEPS, 2, rows, rows_y), jnp.float32),
            pltpu.SemaphoreType.DMA((STEPS, 2)),
            pltpu.SemaphoreType.DMA((STEPS, 2)),
            pltpu.VMEM((STEPS, 8 * x_tiles, rows_y), jnp.float32),
            pltpu.VMEM((STEPS, 8 * x_tiles, rows_y), jnp.float32),
            pltpu.SemaphoreType.DMA((STEPS, 2)),
            pltpu.SemaphoreType.DMA((STEPS, 2)),
        ]
        + [
            pltpu.VMEM((8, 128), jnp.float32),
            pltpu.VMEM((2 * ny, 8, 128), jnp.float32),
            pltpu.VMEM((nx // 2, 8, 128), jnp.float32),
            pltpu.VMEM((8, 128), jnp.float32),
            pltpu.SemaphoreType.DMA((STEPS, N_COPIES)),
            pltpu.SemaphoreType.DMA((STEPS, N_COPIES)),
            pltpu.SemaphoreType.DMA((N_COPIES,)),
            pltpu.SemaphoreType.DMA((N_COPIES,)),
            pltpu.SemaphoreType.DMA((2 * ny,)),
            pltpu.SemaphoreType.DMA((2 * ny,)),
            pltpu.SemaphoreType.DMA((nx // 2,)),
            pltpu.SemaphoreType.DMA((nx // 2,)),
        ],
        compiler_params=pltpu.CompilerParams(collective_id=0, has_side_effects=True),
    )(lam, flow, blocked)
    return (state.reshape(q, rows_x, levels, rows_y), drag)


def solution(mesh):
    placed = (
        P(None, "gx", None, "gy"),
        P(None, None, "gx", None, "gy"),
        P("gx", None, "gy"),
        P(None, "gx", None, "gy"),
    )
    return jax.shard_map(
        per_device,
        mesh=mesh,
        in_specs=placed,
        out_specs=(P(None, "gx", None, "gy"), P()),
        check_vma=False,
    )
```

```python
import functools
import math

import jax
import jax.numpy as jnp
from jax import lax
from jax.experimental import pallas as pl
from jax.experimental.pallas import tpu as pltpu
from jax.sharding import PartitionSpec as P

MESH = pl.DeviceIdType.MESH
TILE = 4
STEPS = 2

lattice_speeds = (
    (0, 0, 0),
    (1, 0, 0),
    (-1, 0, 0),
    (0, 1, 0),
    (0, -1, 0),
    (0, 0, 1),
    (0, 0, -1),
    (1, 1, 0),
    (-1, -1, 0),
    (1, -1, 0),
    (-1, 1, 0),
    (1, 0, 1),
    (-1, 0, -1),
    (1, 0, -1),
    (-1, 0, 1),
    (0, 1, 1),
    (0, -1, -1),
    (0, 1, -1),
    (0, -1, 1),
)
lattice_weights = (1.0 / 3.0,) + (1.0 / 18.0,) * 6 + (1.0 / 36.0,) * 12
relax_rate = 1.6
drag_factor = 20.0


def crossing(speeds):
    return (
        tuple(n for n, c in speeds if c[0] == 1),
        tuple(n for n, c in speeds if c[0] == -1),
        tuple(n for n, c in speeds if c[1] == 1),
        tuple(n for n, c in speeds if c[1] == -1),
        tuple(n for n, c in speeds if c[0] != 0 and c[1] != 0),
    )


MOVING = tuple((n, lattice_speeds[n]) for n in range(1, 19))
REVERSED = tuple((n, tuple(-v for v in lattice_speeds[n])) for n in range(1, 19))
N_COPIES = len(crossing(MOVING)[4])


def opposite_of(number):
    return number + 1 if number % 2 == 1 else number - 1


def along_of(speed, flow):
    along = None
    for axis in range(3):
        if speed[axis] == 0:
            continue
        term = flow[axis] if speed[axis] == 1 else -flow[axis]
        along = term if along is None else along + term
    return along


def collide(moved, flow, fluid):
    speed_sq = flow[0] * flow[0] + flow[1] * flow[1] + flow[2] * flow[2]
    scalar_part = None
    vector_part = [None, None, None]
    drag_local = None
    for number in range(19):
        speed = lattice_speeds[number]
        weighted = lattice_weights[number] * moved[number]
        along = along_of(speed, flow)
        if along is None:
            scalar_term = weighted * (1.0 - 1.5 * speed_sq)
        else:
            scalar_term = weighted * (1.0 + 3.0 * along + 4.5 * along * along - 1.5 * speed_sq)
            drag_term = 3.0 * weighted * along
            drag_local = drag_term if drag_local is None else drag_local + drag_term
        scalar_part = scalar_term if scalar_part is None else scalar_part + scalar_term
        for axis in range(3):
            if speed[axis] == 0:
                term = weighted * (-3.0 * flow[axis])
            else:
                term = weighted * (3.0 * speed[axis] + 9.0 * along * speed[axis] - 3.0 * flow[axis])
            vector_part[axis] = term if vector_part[axis] is None else vector_part[axis] + term
    results = []
    for number in range(19):
        speed = lattice_speeds[number]
        projected = scalar_part
        for axis in range(3):
            projected = projected + vector_part[axis] * (speed[axis] - flow[axis])
        results.append(fluid * ((1.0 - relax_rate) * moved[number] + relax_rate * projected))
    return results, fluid * drag_local


def send_plan(sets, speeds, field, bufs, top, near):
    up_x, dn_x, up_y, dn_y, me_x, me_y = near
    x_high, x_low, _, _, corners = sets
    xhi, xlo, _, _, corner = bufs
    plan = []
    for j, n in enumerate(corners):
        cx, cy, _ = speeds[n]
        rows_at = pl.ds(0, 8) if cx == 1 else pl.ds(top, 8)
        dev_x = dn_x if cx == 1 else up_x
        dev_y = dn_y if cy == 1 else up_y
        plan.append((field(n).at[rows_at], corner.at[j], (dev_x, dev_y)))
    return plan


def start_copies(plan, send_sems, recv_sems):
    copies = []
    for k, (from_ref, to_ref, dev) in enumerate(plan):
        copy = pltpu.make_async_remote_copy(
            src_ref=from_ref, dst_ref=to_ref, send_sem=send_sems.at[k],
            recv_sem=recv_sems.at[k], device_id=dev, device_id_type=MESH)
        copy.start()
        copies.append(copy)
    return copies


def shifted(own, speed, n, sets, bufs, rows):
    x_high, x_low, y_high, y_low, corners = sets
    xhi, xlo, yhi, ylo, corner = bufs
    cx, cy, cz = speed
    top = rows - 8
    row8 = lax.broadcasted_iota(jnp.int32, (8, 128), 0)
    lane = lax.broadcasted_iota(jnp.int32, (rows, 128), 1)
    level = lax.rem(lax.broadcasted_iota(jnp.int32, (rows, 128), 0), 4)

    def patch_x(block, tile):
        if cx == 1:
            head = jnp.where(row8 < 4, tile, block[0:8])
            return jnp.concatenate([head, block[8:]], axis=0)
        tail = jnp.where(row8 >= 4, tile, block[top:])
        return jnp.concatenate([block[:top], tail], axis=0)

    if cx == 1:
        own = patch_x(own, xhi(n))
    elif cx == -1:
        own = patch_x(own, xlo(n))
    if cy != 0:
        side = yhi(n) if cy == 1 else ylo(n)
        if cx != 0:
            side = patch_x(side, corner[corners.index(n)])
        edge = 0 if cy == 1 else 127
        own = jnp.where(lane == edge, side, own)
    shift = 4 * cx + cz
    if shift % rows:
        own = pltpu.roll(own, (-shift) % rows, 0)
    if cy != 0:
        own = pltpu.roll(own, (-cy) % 128, 1)
    if cz == 1:
        own = jnp.where(level == 3, 0.0, own)
    elif cz == -1:
        own = jnp.where(level == 0, 0.0, own)
    return own


def pack_edge(fields, from_lane, rows):
    lane = lax.broadcasted_iota(jnp.int32, (rows, 128), 1)
    packed = jnp.zeros((rows, 128), jnp.float32)
    for k, field in enumerate(fields):
        moved = field if k == from_lane else pltpu.roll(field, (k - from_lane) % 128, 1)
        packed = jnp.where(lane == k, moved, packed)
    return packed


def pack_rows(tiles, low_half):
    row8 = lax.broadcasted_iota(jnp.int32, (8, 128), 0)
    if len(tiles) % 2:
        tiles = tiles + [jnp.zeros((8, 128), jnp.float32)]
    packed = []
    for a, b in zip(tiles[0::2], tiles[1::2]):
        if low_half:
            packed.append(jnp.where(row8 < 4, a, pltpu.roll(b, 4, 0)))
        else:
            packed.append(jnp.where(row8 >= 4, b, pltpu.roll(a, 4, 0)))
    return jnp.concatenate(packed, axis=0)


def unpack_rows(packed_ref, k, low_half):
    tile = packed_ref[pl.ds(8 * (k // 2), 8)]
    if (k % 2 == 0) == low_half:
        return tile
    return pltpu.roll(tile, 4, 0)


def unpack_edge(packed_ref, k, to_lane):
    packed = packed_ref[...]
    return packed if k == to_lane else pltpu.roll(packed, (to_lane - k) % 128, 1)


def drag_weight(number, flow, fluid):
    return (3.0 * lattice_weights[number]) * along_of(lattice_speeds[number], flow) * fluid


def lbm_kernel(nx, ny, rows, scale, lam_hbm, vel_hbm, blk_hbm, out_ref, drag_ref,
               lam_ref, vel_in, blk_ref, load_sem, vel_ref, fluid_ref, moved, state, hfield, xhi, xlo, yhi, ylo, corner, hcorner, ypack, ysend, yrecv,
               xpack_lo, xpack_hi, xsend, xrecv,
               part, row_buf, col_buf, row_sum,
               ssem, rsem, hsend, hrecv, sum_send_a, sum_recv_a, sum_send_b, sum_recv_b):
    me_x = lax.axis_index("gx")
    me_y = lax.axis_index("gy")
    up_x = lax.rem(me_x + 1, nx)
    dn_x = lax.rem(me_x + nx - 1, nx)
    up_y = lax.rem(me_y + 1, ny)
    dn_y = lax.rem(me_y + ny - 1, ny)
    near = (up_x, dn_x, up_y, dn_y, me_x, me_y)
    top = rows - 8

    loads = [
        pltpu.make_async_copy(hbm, vmem, load_sem.at[k])
        for k, (hbm, vmem) in enumerate(((lam_hbm, lam_ref), (vel_hbm, vel_in), (blk_hbm, blk_ref)))
    ]
    for load in loads:
        load.start()

    barrier = pltpu.get_barrier_semaphore()
    for k in range(1, ny):
        pl.semaphore_signal(barrier, inc=1, device_id=(me_x, lax.rem(me_y + k, ny)), device_id_type=MESH)
    for k in range(1, nx):
        pl.semaphore_signal(barrier, inc=1, device_id=(lax.rem(me_x + k, nx), me_y), device_id_type=MESH)
    for dev in ((up_x, up_y), (up_x, dn_y), (dn_x, up_y), (dn_x, dn_y)):
        pl.semaphore_signal(barrier, inc=1, device_id=dev, device_id_type=MESH)

    loads[1].wait()
    loads[2].wait()
    for step in range(STEPS):
        for axis in range(3):
            vel_ref[step, axis] = vel_in[step, axis].astype(jnp.float32)
    level = lax.rem(lax.broadcasted_iota(jnp.int32, (rows, 128), 0), 4)
    from_below = pltpu.roll(blk_ref[4], 1, 0)
    from_above = pltpu.roll(blk_ref[5], rows - 1, 0)
    solid = jnp.where(level == 3, from_below, from_above)
    fluid_ref[...] = 1.0 - solid.astype(jnp.float32)

    last_flow = [vel_ref[STEPS - 1, axis] for axis in range(3)]
    fluid_all = fluid_ref[...]
    for number in range(1, 19):
        weight = drag_weight(number, last_flow, fluid_all)
        hfield[number - 1] = jnp.where(blk_ref[number - 1] == 1, 0.0, weight)

    pl.semaphore_wait(barrier, nx + ny + 2)

    lam_sets = crossing(MOVING)
    h_sets = crossing(REVERSED)
    h_speeds = dict(REVERSED)
    lam_speeds = dict(MOVING)
    n_hi = len(lam_sets[2])
    n_lo = len(lam_sets[3])
    nx_hi = len(lam_sets[0])
    nx_lo = len(lam_sets[1])
    h_bufs = (
        lambda n: unpack_rows(xhi.at[0], nx_hi + h_sets[0].index(n), True),
        lambda n: unpack_rows(xlo.at[0], nx_lo + h_sets[1].index(n), False),
        lambda n: unpack_edge(yhi.at[0], n_hi + h_sets[2].index(n), 0),
        lambda n: unpack_edge(ylo.at[0], n_lo + h_sets[3].index(n), 127),
        hcorner,
    )
    h_copies = None
    sent = []
    drag_acc = jnp.zeros((8, 128), jnp.float32)

    for step in range(STEPS):
        src = lam_ref if step == 0 else state
        origin = lam_hbm if step == 0 else state
        bufs = (
            lambda n, s=step: unpack_rows(xhi.at[s], lam_sets[0].index(n), True),
            lambda n, s=step: unpack_rows(xlo.at[s], lam_sets[1].index(n), False),
            lambda n, s=step: unpack_edge(yhi.at[s], lam_sets[2].index(n), 0),
            lambda n, s=step: unpack_edge(ylo.at[s], lam_sets[3].index(n), 127),
            corner.at[step],
        )
        plan = send_plan(lam_sets, lam_speeds, lambda n: origin.at[n], bufs, top, near)
        copies = start_copies(plan, ssem.at[step], rsem.at[step])
        if step == 0:
            h_plan = send_plan(h_sets, h_speeds, lambda n: hfield.at[n - 1], h_bufs, top, near)
            h_copies = start_copies(h_plan, hsend, hrecv)
            loads[0].wait()
        to_low = [src[n] for n in lam_sets[2]]
        to_high = [src[n] for n in lam_sets[3]]
        if step == 0:
            to_low += [hfield[n - 1] for n in h_sets[2]]
            to_high += [hfield[n - 1] for n in h_sets[3]]
        x_low_tiles = [src[n, 0:8] for n in lam_sets[0]]
        x_high_tiles = [src[n, top:rows] for n in lam_sets[1]]
        if step == 0:
            x_low_tiles += [hfield[n - 1, 0:8] for n in h_sets[0]]
            x_high_tiles += [hfield[n - 1, top:rows] for n in h_sets[1]]
        count_lo = (len(x_low_tiles) + 1) // 2
        count_hi = (len(x_high_tiles) + 1) // 2
        xpack_lo[step, pl.ds(0, 8 * count_lo)] = pack_rows(x_low_tiles, True)
        xpack_hi[step, pl.ds(0, 8 * count_hi)] = pack_rows(x_high_tiles, False)
        copies += start_copies(
            [
                (xpack_lo.at[step, pl.ds(0, 8 * count_lo)], xhi.at[step, pl.ds(0, 8 * count_lo)], (dn_x, me_y)),
                (xpack_hi.at[step, pl.ds(0, 8 * count_hi)], xlo.at[step, pl.ds(0, 8 * count_hi)], (up_x, me_y)),
            ],
            xsend.at[step],
            xrecv.at[step],
        )
        ypack[step, 0] = pack_edge(to_low, 0, rows)
        ypack[step, 1] = pack_edge(to_high, 127, rows)
        copies += start_copies(
            [(ypack.at[step, 0], yhi.at[step], (me_x, dn_y)), (ypack.at[step, 1], ylo.at[step], (me_x, up_y))],
            ysend.at[step],
            yrecv.at[step],
        )
        if step == STEPS - 1:
            for copy in h_copies:
                copy.wait_recv()
            sent += h_copies
            total = drag_acc
            for number in range(1, 19):
                gathered = shifted(hfield[number - 1], h_speeds[number], number, h_sets, h_bufs, rows)
                total = total + jnp.sum((src[number] * gathered).reshape(rows // 8, 8, 128), axis=0)
            for number in range(1, 19):
                cx = lattice_speeds[number][0]
                weight = drag_weight(number, last_flow, fluid_all)
                bounced = jnp.where(blk_ref[number - 1] == 1, src[opposite_of(number)] + 2.0 * cx, 0.0)
                total = total + jnp.sum((weight * bounced).reshape(rows // 8, 8, 128), axis=0)
            part[...] = jnp.broadcast_to(jnp.sum(total), (8, 128))
            row_copies = []
            for k in range(1, ny):
                copy = pltpu.make_async_remote_copy(
                    src_ref=part, dst_ref=row_buf.at[me_y], send_sem=sum_send_a.at[k],
                    recv_sem=sum_recv_a.at[k], device_id=(me_x, lax.rem(me_y + k, ny)),
                    device_id_type=MESH)
                copy.start()
                row_copies.append(copy)
            row_buf[me_y] = part[...]
            for copy in row_copies:
                copy.wait_recv()
            sent += row_copies
            total = row_buf[0]
            for j in range(1, ny):
                total = total + row_buf[j]
            row_sum[...] = total
            col_copies = []
            for k in range(1, nx):
                copy = pltpu.make_async_remote_copy(
                    src_ref=row_sum, dst_ref=col_buf.at[me_x], send_sem=sum_send_b.at[k],
                    recv_sem=sum_recv_b.at[k], device_id=(lax.rem(me_x + k, nx), me_y),
                    device_id_type=MESH)
                copy.start()
                col_copies.append(copy)
            col_buf[me_x] = total
        for copy in copies:
            copy.wait_recv()
        sent += copies

        moved[0] = src[0]
        for number in range(1, 19):
            source = shifted(src[number], lam_speeds[number], number, lam_sets, bufs, rows)
            bounced = src[opposite_of(number)] + 2.0 * lam_speeds[number][0]
            moved[number] = jnp.where(blk_ref[number - 1] == 1, bounced, source)


        dest = out_ref if step == STEPS - 1 else state

        def chunk(c, acc):
            at = pl.ds(pl.multiple_of(c * 8, 8), 8)
            flow = [vel_ref[step, axis, at] for axis in range(3)]
            mu = [moved[number, at] for number in range(19)]
            fresh, drag = collide(mu, flow, fluid_ref[at])
            for number in range(19):
                dest[number, at] = fresh[number]
            return acc + drag

        if step < STEPS - 1:
            drag_acc = lax.fori_loop(0, rows // 8, chunk, drag_acc)
        else:
            lax.fori_loop(0, rows // 8, chunk, drag_acc)

    for copy in col_copies:
        copy.wait_recv()
    sent += col_copies
    total = col_buf[0]
    for j in range(1, nx):
        total = total + col_buf[j]
    drag_ref[0] = -scale * total[0, 0]
    for copy in sent:
        copy.wait_send()


def per_device(adjoint_in, velocity, solid_tiles, link_blocked):
    nx = lax.axis_size("gx")
    ny = lax.axis_size("gy")
    q, rows_x, levels, rows_y = adjoint_in.shape
    rows = rows_x * levels
    lam = adjoint_in.reshape(q, rows, rows_y)
    flow = velocity.reshape(STEPS, 3, rows, rows_y)
    blocked = link_blocked.reshape(q - 1, rows, rows_y)
    cell_count = rows_x * nx * rows_y * ny * levels
    scale = drag_factor / math.sqrt(cell_count)
    vmem = pl.BlockSpec(memory_space=pltpu.VMEM)
    x_tiles = max(
        (len(crossing(MOVING)[face]) + len(crossing(REVERSED)[face]) + 1) // 2 for face in (0, 1)
    )
    state, drag = pl.pallas_call(
        functools.partial(lbm_kernel, nx, ny, rows, scale),
        out_shape=(
            jax.ShapeDtypeStruct((q, rows, rows_y), jnp.float32),
            jax.ShapeDtypeStruct((1,), jnp.float32),
        ),
        in_specs=[pl.BlockSpec(memory_space=pl.ANY)] * 3,
        out_specs=(vmem, pl.BlockSpec(memory_space=pltpu.SMEM)),
        scratch_shapes=[
            pltpu.VMEM((q, rows, rows_y), jnp.float32),
            pltpu.VMEM((STEPS, 3, rows, rows_y), velocity.dtype),
            pltpu.VMEM((q - 1, rows, rows_y), link_blocked.dtype),
            pltpu.SemaphoreType.DMA((3,)),
            pltpu.VMEM((STEPS, 3, rows, rows_y), jnp.float32),
            pltpu.VMEM((rows, rows_y), jnp.float32),
            pltpu.VMEM((q, rows, rows_y), jnp.float32),
            pltpu.VMEM((q, rows, rows_y), jnp.float32),
            pltpu.VMEM((q - 1, rows, rows_y), jnp.float32),
        ]
        + [pltpu.VMEM((STEPS, 8 * x_tiles, rows_y), jnp.float32)] * 2
        + [pltpu.VMEM((STEPS, rows, rows_y), jnp.float32)] * 2
        + [pltpu.VMEM((STEPS, len(crossing(MOVING)[4]), 8, rows_y), jnp.float32)]
        + [pltpu.VMEM((len(crossing(REVERSED)[4]), 8, rows_y), jnp.float32)]
        + [
            pltpu.VMEM((STEPS, 2, rows, rows_y), jnp.float32),
            pltpu.SemaphoreType.DMA((STEPS, 2)),
            pltpu.SemaphoreType.DMA((STEPS, 2)),
            pltpu.VMEM((STEPS, 8 * x_tiles, rows_y), jnp.float32),
            pltpu.VMEM((STEPS, 8 * x_tiles, rows_y), jnp.float32),
            pltpu.SemaphoreType.DMA((STEPS, 2)),
            pltpu.SemaphoreType.DMA((STEPS, 2)),
        ]
        + [
            pltpu.VMEM((8, 128), jnp.float32),
            pltpu.VMEM((ny, 8, 128), jnp.float32),
            pltpu.VMEM((nx, 8, 128), jnp.float32),
            pltpu.VMEM((8, 128), jnp.float32),
            pltpu.SemaphoreType.DMA((STEPS, N_COPIES)),
            pltpu.SemaphoreType.DMA((STEPS, N_COPIES)),
            pltpu.SemaphoreType.DMA((N_COPIES,)),
            pltpu.SemaphoreType.DMA((N_COPIES,)),
            pltpu.SemaphoreType.DMA((ny,)),
            pltpu.SemaphoreType.DMA((ny,)),
            pltpu.SemaphoreType.DMA((nx,)),
            pltpu.SemaphoreType.DMA((nx,)),
        ],
        compiler_params=pltpu.CompilerParams(collective_id=0, has_side_effects=True),
    )(lam, flow, blocked)
    return (state.reshape(q, rows_x, levels, rows_y), drag)


def solution(mesh):
    placed = (
        P(None, "gx", None, "gy"),
        P(None, None, "gx", None, "gy"),
        P("gx", None, "gy"),
        P(None, "gx", None, "gy"),
    )
    return jax.shard_map(
        per_device,
        mesh=mesh,
        in_specs=placed,
        out_specs=(P(None, "gx", None, "gy"), P()),
        check_vma=False,
    )
```

```python
import functools
import math

import jax
import jax.numpy as jnp
from jax import lax
from jax.experimental import pallas as pl
from jax.experimental.pallas import tpu as pltpu
from jax.sharding import PartitionSpec as P

MESH = pl.DeviceIdType.MESH
SPAN_X = 4
TILE = 4
STEPS = 2

lattice_speeds = (
    (0, 0, 0),
    (1, 0, 0),
    (-1, 0, 0),
    (0, 1, 0),
    (0, -1, 0),
    (0, 0, 1),
    (0, 0, -1),
    (1, 1, 0),
    (-1, -1, 0),
    (1, -1, 0),
    (-1, 1, 0),
    (1, 0, 1),
    (-1, 0, -1),
    (1, 0, -1),
    (-1, 0, 1),
    (0, 1, 1),
    (0, -1, -1),
    (0, 1, -1),
    (0, -1, 1),
)
lattice_weights = (1.0 / 3.0,) + (1.0 / 18.0,) * 6 + (1.0 / 36.0,) * 12
relax_rate = 1.6
drag_factor = 20.0


def crossing(speeds):
    return (
        tuple(n for n, c in speeds if c[0] == 1),
        tuple(n for n, c in speeds if c[0] == -1),
        tuple(n for n, c in speeds if c[1] == 1),
        tuple(n for n, c in speeds if c[1] == -1),
        tuple(n for n, c in speeds if c[0] != 0 and c[1] != 0),
    )


MOVING = tuple((n, lattice_speeds[n]) for n in range(1, 19))
REVERSED = tuple((n, tuple(-v for v in lattice_speeds[n])) for n in range(1, 19))
N_COPIES = len(crossing(MOVING)[4])


def opposite_of(number):
    return number + 1 if number % 2 == 1 else number - 1


def along_of(speed, flow):
    along = None
    for axis in range(3):
        if speed[axis] == 0:
            continue
        term = flow[axis] if speed[axis] == 1 else -flow[axis]
        along = term if along is None else along + term
    return along


def collide(moved, flow, fluid):
    speed_sq = flow[0] * flow[0] + flow[1] * flow[1] + flow[2] * flow[2]
    scalar_part = None
    vector_part = [None, None, None]
    drag_local = None
    for number in range(19):
        speed = lattice_speeds[number]
        weighted = lattice_weights[number] * moved[number]
        along = along_of(speed, flow)
        if along is None:
            scalar_term = weighted * (1.0 - 1.5 * speed_sq)
        else:
            scalar_term = weighted * (1.0 + 3.0 * along + 4.5 * along * along - 1.5 * speed_sq)
            drag_term = 3.0 * weighted * along
            drag_local = drag_term if drag_local is None else drag_local + drag_term
        scalar_part = scalar_term if scalar_part is None else scalar_part + scalar_term
        for axis in range(3):
            if speed[axis] == 0:
                term = weighted * (-3.0 * flow[axis])
            else:
                term = weighted * (3.0 * speed[axis] + 9.0 * along * speed[axis] - 3.0 * flow[axis])
            vector_part[axis] = term if vector_part[axis] is None else vector_part[axis] + term
    results = []
    for number in range(19):
        speed = lattice_speeds[number]
        projected = scalar_part
        for axis in range(3):
            projected = projected + vector_part[axis] * (speed[axis] - flow[axis])
        results.append(fluid * ((1.0 - relax_rate) * moved[number] + relax_rate * projected))
    return results, fluid * drag_local


def send_plan(sets, speeds, field, bufs, top, near):
    up_x, dn_x, up_y, dn_y, me_x, me_y = near
    x_high, x_low, _, _, corners = sets
    xhi, xlo, _, _, corner = bufs
    plan = []
    for j, n in enumerate(corners):
        cx, cy, _ = speeds[n]
        rows_at = pl.ds(0, 8) if cx == 1 else pl.ds(top, 8)
        dev_x = dn_x if cx == 1 else up_x
        dev_y = dn_y if cy == 1 else up_y
        plan.append((field(n).at[rows_at], corner.at[j], (dev_x, dev_y)))
    return plan


def start_copies(plan, send_sems, recv_sems):
    copies = []
    for k, (from_ref, to_ref, dev) in enumerate(plan):
        copy = pltpu.make_async_remote_copy(
            src_ref=from_ref, dst_ref=to_ref, send_sem=send_sems.at[k],
            recv_sem=recv_sems.at[k], device_id=dev, device_id_type=MESH)
        copy.start()
        copies.append(copy)
    return copies


def shifted(own, speed, n, sets, bufs, rows):
    x_high, x_low, y_high, y_low, corners = sets
    xhi, xlo, yhi, ylo, corner = bufs
    cx, cy, cz = speed
    top = rows - 8
    row8 = lax.broadcasted_iota(jnp.int32, (8, 128), 0)
    lane = lax.broadcasted_iota(jnp.int32, (rows, 128), 1)
    level = lax.rem(lax.broadcasted_iota(jnp.int32, (rows, 128), 0), 4)

    def patch_x(block, tile):
        if cx == 1:
            head = jnp.where(row8 < 4, tile, block[0:8])
            return jnp.concatenate([head, block[8:]], axis=0)
        tail = jnp.where(row8 >= 4, tile, block[top:])
        return jnp.concatenate([block[:top], tail], axis=0)

    if cx == 1:
        own = patch_x(own, xhi(n))
    elif cx == -1:
        own = patch_x(own, xlo(n))
    if cy != 0:
        side = yhi(n) if cy == 1 else ylo(n)
        if cx != 0:
            side = patch_x(side, corner[corners.index(n)])
        edge = 0 if cy == 1 else 127
        own = jnp.where(lane == edge, side, own)
    shift = 4 * cx + cz
    if shift % rows:
        own = pltpu.roll(own, (-shift) % rows, 0)
    if cy != 0:
        own = pltpu.roll(own, (-cy) % 128, 1)
    if cz == 1:
        own = jnp.where(level == 3, 0.0, own)
    elif cz == -1:
        own = jnp.where(level == 0, 0.0, own)
    return own


def pack_edge(fields, from_lane, rows):
    lane = lax.broadcasted_iota(jnp.int32, (rows, 128), 1)
    packed = jnp.zeros((rows, 128), jnp.float32)
    for k, field in enumerate(fields):
        moved = field if k == from_lane else pltpu.roll(field, (k - from_lane) % 128, 1)
        packed = jnp.where(lane == k, moved, packed)
    return packed


def pack_rows(tiles, low_half):
    row8 = lax.broadcasted_iota(jnp.int32, (8, 128), 0)
    if len(tiles) % 2:
        tiles = tiles + [jnp.zeros((8, 128), jnp.float32)]
    packed = []
    for a, b in zip(tiles[0::2], tiles[1::2]):
        if low_half:
            packed.append(jnp.where(row8 < 4, a, pltpu.roll(b, 4, 0)))
        else:
            packed.append(jnp.where(row8 >= 4, b, pltpu.roll(a, 4, 0)))
    return jnp.concatenate(packed, axis=0)


def unpack_rows(packed_ref, k, low_half):
    tile = packed_ref[pl.ds(8 * (k // 2), 8)]
    if (k % 2 == 0) == low_half:
        return tile
    return pltpu.roll(tile, 4, 0)


def unpack_edge(packed_ref, k, to_lane):
    packed = packed_ref[...]
    return packed if k == to_lane else pltpu.roll(packed, (to_lane - k) % 128, 1)


def drag_weight(number, flow, fluid):
    return (3.0 * lattice_weights[number]) * along_of(lattice_speeds[number], flow) * fluid


def start_gather(value_ref, buf, slot, peers, send_sems, recv_sems):
    copies = []
    for k, dev in peers:
        copy = pltpu.make_async_remote_copy(
            src_ref=value_ref, dst_ref=buf.at[slot], send_sem=send_sems.at[k],
            recv_sem=recv_sems.at[k], device_id=dev, device_id_type=MESH)
        copy.start()
        copies.append(copy)
    return copies


def gather_sum(value_ref, buf, slot, peers, send_sems, recv_sems, sent):
    copies = start_gather(value_ref, buf, slot, peers, send_sems, recv_sems)
    buf[slot] = value_ref[...]
    for copy in copies:
        copy.wait_recv()
    sent += copies
    total = buf[0]
    for j in range(1, len(peers) + 1):
        total = total + buf[j]
    return total


def lbm_kernel(nx, ny, rows, scale, lam_hbm, vel_hbm, blk_hbm, out_ref, drag_ref,
               lam_ref, vel_in, blk_ref, load_sem, vel_ref, fluid_ref, moved, state, hfield, xhi, xlo, yhi, ylo, corner, hcorner, ypack, ysend, yrecv,
               xpack_lo, xpack_hi, xsend, xrecv,
               part, g1_buf, g2_buf, g3_buf, g1_sum, g2_sum,
               ssem, rsem, hsend, hrecv, g1_send, g1_recv, g2_send, g2_recv, g3_send, g3_recv):
    me_x = lax.axis_index("gx")
    me_y = lax.axis_index("gy")
    up_x = lax.rem(me_x + 1, nx)
    dn_x = lax.rem(me_x + nx - 1, nx)
    up_y = lax.rem(me_y + 1, ny)
    dn_y = lax.rem(me_y + ny - 1, ny)
    near = (up_x, dn_x, up_y, dn_y, me_x, me_y)
    top = rows - 8

    loads = [
        pltpu.make_async_copy(hbm, vmem, load_sem.at[k])
        for k, (hbm, vmem) in enumerate(((lam_hbm, lam_ref), (vel_hbm, vel_in), (blk_hbm, blk_ref)))
    ]
    for load in loads:
        load.start()

    b1, b2 = nx // 2, SPAN_X
    n3 = 2 * (ny // b2)
    slot1 = lax.rem(me_x, b1)
    slot2 = lax.rem(me_y, b2)
    slot3 = (me_x // b1) * (ny // b2) + me_y // b2
    peers1 = [(k, ((me_x // b1) * b1 + lax.rem(slot1 + k, b1), me_y)) for k in range(1, b1)]
    peers2 = [(k, (me_x, (me_y // b2) * b2 + lax.rem(slot2 + k, b2))) for k in range(1, b2)]
    peers3 = []
    for k in range(1, n3):
        t = lax.rem(slot3 + k, n3)
        peers3.append((k, ((t // (ny // b2)) * b1 + slot1, lax.rem(t, ny // b2) * b2 + slot2)))

    barrier = pltpu.get_barrier_semaphore()
    for _, dev in peers1 + peers2 + peers3:
        pl.semaphore_signal(barrier, inc=1, device_id=dev, device_id_type=MESH)
    for dev in ((up_x, up_y), (up_x, dn_y), (dn_x, up_y), (dn_x, dn_y), (up_x, me_y), (dn_x, me_y), (me_x, up_y), (me_x, dn_y)):
        pl.semaphore_signal(barrier, inc=1, device_id=dev, device_id_type=MESH)

    loads[1].wait()
    loads[2].wait()
    for step in range(STEPS):
        for axis in range(3):
            vel_ref[step, axis] = vel_in[step, axis].astype(jnp.float32)
    level = lax.rem(lax.broadcasted_iota(jnp.int32, (rows, 128), 0), 4)
    from_below = pltpu.roll(blk_ref[4], 1, 0)
    from_above = pltpu.roll(blk_ref[5], rows - 1, 0)
    solid = jnp.where(level == 3, from_below, from_above)
    fluid_ref[...] = 1.0 - solid.astype(jnp.float32)

    last_flow = [vel_ref[STEPS - 1, axis] for axis in range(3)]
    fluid_all = fluid_ref[...]
    for number in range(1, 19):
        weight = drag_weight(number, last_flow, fluid_all)
        hfield[number - 1] = jnp.where(blk_ref[number - 1] == 1, 0.0, weight)

    pl.semaphore_wait(barrier, len(peers1) + len(peers2) + len(peers3) + 8)

    lam_sets = crossing(MOVING)
    h_sets = crossing(REVERSED)
    h_speeds = dict(REVERSED)
    lam_speeds = dict(MOVING)
    n_hi = len(lam_sets[2])
    n_lo = len(lam_sets[3])
    nx_hi = len(lam_sets[0])
    nx_lo = len(lam_sets[1])
    h_bufs = (
        lambda n: unpack_rows(xhi.at[0], nx_hi + h_sets[0].index(n), True),
        lambda n: unpack_rows(xlo.at[0], nx_lo + h_sets[1].index(n), False),
        lambda n: unpack_edge(yhi.at[0], n_hi + h_sets[2].index(n), 0),
        lambda n: unpack_edge(ylo.at[0], n_lo + h_sets[3].index(n), 127),
        hcorner,
    )
    h_copies = None
    sent = []
    drag_acc = jnp.zeros((8, 128), jnp.float32)

    for step in range(STEPS):
        src = lam_ref if step == 0 else state
        origin = lam_hbm if step == 0 else state
        bufs = (
            lambda n, s=step: unpack_rows(xhi.at[s], lam_sets[0].index(n), True),
            lambda n, s=step: unpack_rows(xlo.at[s], lam_sets[1].index(n), False),
            lambda n, s=step: unpack_edge(yhi.at[s], lam_sets[2].index(n), 0),
            lambda n, s=step: unpack_edge(ylo.at[s], lam_sets[3].index(n), 127),
            corner.at[step],
        )
        plan = send_plan(lam_sets, lam_speeds, lambda n: origin.at[n], bufs, top, near)
        copies = start_copies(plan, ssem.at[step], rsem.at[step])
        if step == 0:
            h_plan = send_plan(h_sets, h_speeds, lambda n: hfield.at[n - 1], h_bufs, top, near)
            h_copies = start_copies(h_plan, hsend, hrecv)
            loads[0].wait()
        to_low = [src[n] for n in lam_sets[2]]
        to_high = [src[n] for n in lam_sets[3]]
        if step == 0:
            to_low += [hfield[n - 1] for n in h_sets[2]]
            to_high += [hfield[n - 1] for n in h_sets[3]]
        x_low_tiles = [src[n, 0:8] for n in lam_sets[0]]
        x_high_tiles = [src[n, top:rows] for n in lam_sets[1]]
        if step == 0:
            x_low_tiles += [hfield[n - 1, 0:8] for n in h_sets[0]]
            x_high_tiles += [hfield[n - 1, top:rows] for n in h_sets[1]]
        count_lo = (len(x_low_tiles) + 1) // 2
        count_hi = (len(x_high_tiles) + 1) // 2
        xpack_lo[step, pl.ds(0, 8 * count_lo)] = pack_rows(x_low_tiles, True)
        xpack_hi[step, pl.ds(0, 8 * count_hi)] = pack_rows(x_high_tiles, False)
        copies += start_copies(
            [
                (xpack_lo.at[step, pl.ds(0, 8 * count_lo)], xhi.at[step, pl.ds(0, 8 * count_lo)], (dn_x, me_y)),
                (xpack_hi.at[step, pl.ds(0, 8 * count_hi)], xlo.at[step, pl.ds(0, 8 * count_hi)], (up_x, me_y)),
            ],
            xsend.at[step],
            xrecv.at[step],
        )
        ypack[step, 0] = pack_edge(to_low, 0, rows)
        ypack[step, 1] = pack_edge(to_high, 127, rows)
        copies += start_copies(
            [(ypack.at[step, 0], yhi.at[step], (me_x, dn_y)), (ypack.at[step, 1], ylo.at[step], (me_x, up_y))],
            ysend.at[step],
            yrecv.at[step],
        )
        if step == STEPS - 1:
            for copy in h_copies:
                copy.wait_recv()
            sent += h_copies
            total = drag_acc
            for number in range(1, 19):
                gathered = shifted(hfield[number - 1], h_speeds[number], number, h_sets, h_bufs, rows)
                total = total + jnp.sum((src[number] * gathered).reshape(rows // 8, 8, 128), axis=0)
            for number in range(1, 19):
                cx = lattice_speeds[number][0]
                weight = drag_weight(number, last_flow, fluid_all)
                bounced = jnp.where(blk_ref[number - 1] == 1, src[opposite_of(number)] + 2.0 * cx, 0.0)
                total = total + jnp.sum((weight * bounced).reshape(rows // 8, 8, 128), axis=0)
            part[...] = jnp.broadcast_to(jnp.sum(total), (8, 128))
            total = gather_sum(part, g1_buf, slot1, peers1, g1_send, g1_recv, sent)
            g1_sum[...] = total
            total = gather_sum(g1_sum, g2_buf, slot2, peers2, g2_send, g2_recv, sent)
            g2_sum[...] = total
            g3_copies = start_gather(g2_sum, g3_buf, slot3, peers3, g3_send, g3_recv)
            g3_buf[slot3] = total
        for copy in copies:
            copy.wait_recv()
        sent += copies

        moved[0] = src[0]
        for number in range(1, 19):
            source = shifted(src[number], lam_speeds[number], number, lam_sets, bufs, rows)
            bounced = src[opposite_of(number)] + 2.0 * lam_speeds[number][0]
            moved[number] = jnp.where(blk_ref[number - 1] == 1, bounced, source)


        dest = out_ref if step == STEPS - 1 else state

        def chunk(c, acc):
            at = pl.ds(pl.multiple_of(c * 8, 8), 8)
            flow = [vel_ref[step, axis, at] for axis in range(3)]
            mu = [moved[number, at] for number in range(19)]
            fresh, drag = collide(mu, flow, fluid_ref[at])
            for number in range(19):
                dest[number, at] = fresh[number]
            return acc + drag

        if step < STEPS - 1:
            drag_acc = lax.fori_loop(0, rows // 8, chunk, drag_acc)
        else:
            lax.fori_loop(0, rows // 8, chunk, drag_acc)

    for copy in g3_copies:
        copy.wait_recv()
    sent += g3_copies
    total = g3_buf[0]
    for j in range(1, n3):
        total = total + g3_buf[j]
    drag_ref[0] = -scale * total[0, 0]
    for copy in sent:
        copy.wait_send()


def per_device(adjoint_in, velocity, solid_tiles, link_blocked):
    nx = lax.axis_size("gx")
    ny = lax.axis_size("gy")
    q, rows_x, levels, rows_y = adjoint_in.shape
    rows = rows_x * levels
    lam = adjoint_in.reshape(q, rows, rows_y)
    flow = velocity.reshape(STEPS, 3, rows, rows_y)
    blocked = link_blocked.reshape(q - 1, rows, rows_y)
    cell_count = rows_x * nx * rows_y * ny * levels
    scale = drag_factor / math.sqrt(cell_count)
    vmem = pl.BlockSpec(memory_space=pltpu.VMEM)
    x_tiles = max(
        (len(crossing(MOVING)[face]) + len(crossing(REVERSED)[face]) + 1) // 2 for face in (0, 1)
    )
    state, drag = pl.pallas_call(
        functools.partial(lbm_kernel, nx, ny, rows, scale),
        out_shape=(
            jax.ShapeDtypeStruct((q, rows, rows_y), jnp.float32),
            jax.ShapeDtypeStruct((1,), jnp.float32),
        ),
        in_specs=[pl.BlockSpec(memory_space=pl.ANY)] * 3,
        out_specs=(vmem, pl.BlockSpec(memory_space=pltpu.SMEM)),
        scratch_shapes=[
            pltpu.VMEM((q, rows, rows_y), jnp.float32),
            pltpu.VMEM((STEPS, 3, rows, rows_y), velocity.dtype),
            pltpu.VMEM((q - 1, rows, rows_y), link_blocked.dtype),
            pltpu.SemaphoreType.DMA((3,)),
            pltpu.VMEM((STEPS, 3, rows, rows_y), jnp.float32),
            pltpu.VMEM((rows, rows_y), jnp.float32),
            pltpu.VMEM((q, rows, rows_y), jnp.float32),
            pltpu.VMEM((q, rows, rows_y), jnp.float32),
            pltpu.VMEM((q - 1, rows, rows_y), jnp.float32),
        ]
        + [pltpu.VMEM((STEPS, 8 * x_tiles, rows_y), jnp.float32)] * 2
        + [pltpu.VMEM((STEPS, rows, rows_y), jnp.float32)] * 2
        + [pltpu.VMEM((STEPS, len(crossing(MOVING)[4]), 8, rows_y), jnp.float32)]
        + [pltpu.VMEM((len(crossing(REVERSED)[4]), 8, rows_y), jnp.float32)]
        + [
            pltpu.VMEM((STEPS, 2, rows, rows_y), jnp.float32),
            pltpu.SemaphoreType.DMA((STEPS, 2)),
            pltpu.SemaphoreType.DMA((STEPS, 2)),
            pltpu.VMEM((STEPS, 8 * x_tiles, rows_y), jnp.float32),
            pltpu.VMEM((STEPS, 8 * x_tiles, rows_y), jnp.float32),
            pltpu.SemaphoreType.DMA((STEPS, 2)),
            pltpu.SemaphoreType.DMA((STEPS, 2)),
        ]
        + [
            pltpu.VMEM((8, 128), jnp.float32),
            pltpu.VMEM((nx // 2, 8, 128), jnp.float32),
            pltpu.VMEM((SPAN_X, 8, 128), jnp.float32),
            pltpu.VMEM((2 * ny // SPAN_X, 8, 128), jnp.float32),
            pltpu.VMEM((8, 128), jnp.float32),
            pltpu.VMEM((8, 128), jnp.float32),
            pltpu.SemaphoreType.DMA((STEPS, N_COPIES)),
            pltpu.SemaphoreType.DMA((STEPS, N_COPIES)),
            pltpu.SemaphoreType.DMA((N_COPIES,)),
            pltpu.SemaphoreType.DMA((N_COPIES,)),
            pltpu.SemaphoreType.DMA((nx // 2,)),
            pltpu.SemaphoreType.DMA((nx // 2,)),
            pltpu.SemaphoreType.DMA((SPAN_X,)),
            pltpu.SemaphoreType.DMA((SPAN_X,)),
            pltpu.SemaphoreType.DMA((2 * ny // SPAN_X,)),
            pltpu.SemaphoreType.DMA((2 * ny // SPAN_X,)),
        ],
        compiler_params=pltpu.CompilerParams(collective_id=0, has_side_effects=True),
    )(lam, flow, blocked)
    return (state.reshape(q, rows_x, levels, rows_y), drag)


def solution(mesh):
    placed = (
        P(None, "gx", None, "gy"),
        P(None, None, "gx", None, "gy"),
        P("gx", None, "gy"),
        P(None, "gx", None, "gy"),
    )
    return jax.shard_map(
        per_device,
        mesh=mesh,
        in_specs=placed,
        out_specs=(P(None, "gx", None, "gy"), P()),
        check_vma=False,
    )
```

```python
import functools
import math

import jax
import jax.numpy as jnp
from jax import lax
from jax.experimental import pallas as pl
from jax.experimental.pallas import tpu as pltpu
from jax.sharding import PartitionSpec as P

MESH = pl.DeviceIdType.MESH
SPAN_X = 4
TILE = 4
STEPS = 2

lattice_speeds = (
    (0, 0, 0),
    (1, 0, 0),
    (-1, 0, 0),
    (0, 1, 0),
    (0, -1, 0),
    (0, 0, 1),
    (0, 0, -1),
    (1, 1, 0),
    (-1, -1, 0),
    (1, -1, 0),
    (-1, 1, 0),
    (1, 0, 1),
    (-1, 0, -1),
    (1, 0, -1),
    (-1, 0, 1),
    (0, 1, 1),
    (0, -1, -1),
    (0, 1, -1),
    (0, -1, 1),
)
lattice_weights = (1.0 / 3.0,) + (1.0 / 18.0,) * 6 + (1.0 / 36.0,) * 12
relax_rate = 1.6
drag_factor = 20.0


def crossing(speeds):
    return (
        tuple(n for n, c in speeds if c[0] == 1),
        tuple(n for n, c in speeds if c[0] == -1),
        tuple(n for n, c in speeds if c[1] == 1),
        tuple(n for n, c in speeds if c[1] == -1),
        tuple(n for n, c in speeds if c[0] != 0 and c[1] != 0),
    )


MOVING = tuple((n, lattice_speeds[n]) for n in range(1, 19))
REVERSED = tuple((n, tuple(-v for v in lattice_speeds[n])) for n in range(1, 19))
N_COPIES = len(crossing(MOVING)[4])


def opposite_of(number):
    return number + 1 if number % 2 == 1 else number - 1


def along_of(speed, flow):
    along = None
    for axis in range(3):
        if speed[axis] == 0:
            continue
        term = flow[axis] if speed[axis] == 1 else -flow[axis]
        along = term if along is None else along + term
    return along


def collide(moved, flow, fluid):
    speed_sq = flow[0] * flow[0] + flow[1] * flow[1] + flow[2] * flow[2]
    scalar_part = None
    vector_part = [None, None, None]
    drag_local = None
    for number in range(19):
        speed = lattice_speeds[number]
        weighted = lattice_weights[number] * moved[number]
        along = along_of(speed, flow)
        if along is None:
            scalar_term = weighted * (1.0 - 1.5 * speed_sq)
        else:
            scalar_term = weighted * (1.0 + 3.0 * along + 4.5 * along * along - 1.5 * speed_sq)
            drag_term = 3.0 * weighted * along
            drag_local = drag_term if drag_local is None else drag_local + drag_term
        scalar_part = scalar_term if scalar_part is None else scalar_part + scalar_term
        for axis in range(3):
            if speed[axis] == 0:
                term = weighted * (-3.0 * flow[axis])
            else:
                term = weighted * (3.0 * speed[axis] + 9.0 * along * speed[axis] - 3.0 * flow[axis])
            vector_part[axis] = term if vector_part[axis] is None else vector_part[axis] + term
    results = []
    for number in range(19):
        speed = lattice_speeds[number]
        projected = scalar_part
        for axis in range(3):
            projected = projected + vector_part[axis] * (speed[axis] - flow[axis])
        results.append(fluid * ((1.0 - relax_rate) * moved[number] + relax_rate * projected))
    return results, fluid * drag_local


def send_plan(sets, speeds, field, bufs, top, near):
    up_x, dn_x, up_y, dn_y, me_x, me_y = near
    x_high, x_low, _, _, corners = sets
    xhi, xlo, _, _, corner = bufs
    plan = []
    for j, n in enumerate(corners):
        cx, cy, _ = speeds[n]
        rows_at = pl.ds(0, 8) if cx == 1 else pl.ds(top, 8)
        dev_x = dn_x if cx == 1 else up_x
        dev_y = dn_y if cy == 1 else up_y
        plan.append((field(n).at[rows_at], corner.at[j], (dev_x, dev_y)))
    return plan


def start_copies(plan, send_sems, recv_sems):
    copies = []
    for k, (from_ref, to_ref, dev) in enumerate(plan):
        copy = pltpu.make_async_remote_copy(
            src_ref=from_ref, dst_ref=to_ref, send_sem=send_sems.at[k],
            recv_sem=recv_sems.at[k], device_id=dev, device_id_type=MESH)
        copy.start()
        copies.append(copy)
    return copies


def shifted(own, speed, n, sets, bufs, rows):
    x_high, x_low, y_high, y_low, corners = sets
    xhi, xlo, yhi, ylo, corner = bufs
    cx, cy, cz = speed
    top = rows - 8
    row8 = lax.broadcasted_iota(jnp.int32, (8, 128), 0)
    lane = lax.broadcasted_iota(jnp.int32, (rows, 128), 1)
    level = lax.rem(lax.broadcasted_iota(jnp.int32, (rows, 128), 0), 4)

    def patch_x(block, tile):
        if cx == 1:
            head = jnp.where(row8 < 4, tile, block[0:8])
            return jnp.concatenate([head, block[8:]], axis=0)
        tail = jnp.where(row8 >= 4, tile, block[top:])
        return jnp.concatenate([block[:top], tail], axis=0)

    if cx == 1:
        own = patch_x(own, xhi(n))
    elif cx == -1:
        own = patch_x(own, xlo(n))
    if cy != 0:
        side = yhi(n) if cy == 1 else ylo(n)
        if cx != 0:
            side = patch_x(side, corner[corners.index(n)])
        edge = 0 if cy == 1 else 127
        own = jnp.where(lane == edge, side, own)
    shift = 4 * cx + cz
    if shift % rows:
        own = pltpu.roll(own, (-shift) % rows, 0)
    if cy != 0:
        own = pltpu.roll(own, (-cy) % 128, 1)
    if cz == 1:
        own = jnp.where(level == 3, 0.0, own)
    elif cz == -1:
        own = jnp.where(level == 0, 0.0, own)
    return own


def pack_edge(fields, from_lane, rows):
    lane = lax.broadcasted_iota(jnp.int32, (rows, 128), 1)
    packed = jnp.zeros((rows, 128), jnp.float32)
    for k, field in enumerate(fields):
        moved = field if k == from_lane else pltpu.roll(field, (k - from_lane) % 128, 1)
        packed = jnp.where(lane == k, moved, packed)
    return packed


def pack_rows(tiles, low_half):
    row8 = lax.broadcasted_iota(jnp.int32, (8, 128), 0)
    if len(tiles) % 2:
        tiles = tiles + [jnp.zeros((8, 128), jnp.float32)]
    packed = []
    for a, b in zip(tiles[0::2], tiles[1::2]):
        if low_half:
            packed.append(jnp.where(row8 < 4, a, pltpu.roll(b, 4, 0)))
        else:
            packed.append(jnp.where(row8 >= 4, b, pltpu.roll(a, 4, 0)))
    return jnp.concatenate(packed, axis=0)


def unpack_rows(packed_ref, k, low_half):
    tile = packed_ref[pl.ds(8 * (k // 2), 8)]
    if (k % 2 == 0) == low_half:
        return tile
    return pltpu.roll(tile, 4, 0)


def unpack_edge(packed_ref, k, to_lane):
    packed = packed_ref[...]
    return packed if k == to_lane else pltpu.roll(packed, (to_lane - k) % 128, 1)


def drag_weight(number, flow, fluid):
    return (3.0 * lattice_weights[number]) * along_of(lattice_speeds[number], flow) * fluid


def start_gather(value_ref, buf, slot, peers, send_sems, recv_sems):
    copies = []
    for k, dev in peers:
        copy = pltpu.make_async_remote_copy(
            src_ref=value_ref, dst_ref=buf.at[slot], send_sem=send_sems.at[k],
            recv_sem=recv_sems.at[k], device_id=dev, device_id_type=MESH)
        copy.start()
        copies.append(copy)
    return copies


def gather_sum(value_ref, buf, slot, peers, send_sems, recv_sems, sent):
    copies = start_gather(value_ref, buf, slot, peers, send_sems, recv_sems)
    buf[slot] = value_ref[...]
    for copy in copies:
        copy.wait_recv()
    sent += copies
    total = buf[0]
    for j in range(1, len(peers) + 1):
        total = total + buf[j]
    return total


def lbm_kernel(nx, ny, rows, scale, lam_hbm, vel_hbm, blk_hbm, out_ref, drag_ref,
               lam_ref, vel_in, blk_ref, load_sem, vel_ref, fluid_ref, moved, state, hfield, xhi, xlo, yhi, ylo, corner, hcorner, ypack, ysend, yrecv,
               xpack_lo, xpack_hi, xsend, xrecv,
               part, g1_buf, g2_buf, g3_buf, g4_buf, g1_sum, g2_sum, g3_sum,
               ssem, rsem, hsend, hrecv, g1_send, g1_recv, g2_send, g2_recv, g3_send, g3_recv, g4_send, g4_recv):
    me_x = lax.axis_index("gx")
    me_y = lax.axis_index("gy")
    up_x = lax.rem(me_x + 1, nx)
    dn_x = lax.rem(me_x + nx - 1, nx)
    up_y = lax.rem(me_y + 1, ny)
    dn_y = lax.rem(me_y + ny - 1, ny)
    near = (up_x, dn_x, up_y, dn_y, me_x, me_y)
    top = rows - 8

    loads = [
        pltpu.make_async_copy(hbm, vmem, load_sem.at[k])
        for k, (hbm, vmem) in enumerate(((lam_hbm, lam_ref), (vel_hbm, vel_in), (blk_hbm, blk_ref)))
    ]
    for load in loads:
        load.start()

    b1, b2 = nx // 2, SPAN_X
    n3 = 2 * (ny // b2)
    slot1 = lax.rem(me_x, b1)
    slot2 = lax.rem(me_y, b2)
    slot3 = (me_x // b1) * (ny // b2) + me_y // b2
    peers1 = [(k, ((me_x // b1) * b1 + lax.rem(slot1 + k, b1), me_y)) for k in range(1, b1)]
    peers2 = [(k, (me_x, (me_y // b2) * b2 + lax.rem(slot2 + k, b2))) for k in range(1, b2)]
    near_z = min(4, n3)
    far_z = n3 // near_z

    def z_device(t):
        return ((t // (ny // b2)) * b1 + slot1, lax.rem(t, ny // b2) * b2 + slot2)

    slot3_all = slot3
    slot3 = lax.rem(slot3_all, near_z)
    slot4 = slot3_all // near_z
    peers3 = [(k, z_device(slot4 * near_z + lax.rem(slot3 + k, near_z))) for k in range(1, near_z)]
    peers4 = [(k, z_device(lax.rem(slot4 + k, far_z) * near_z + slot3)) for k in range(1, far_z)]

    barrier = pltpu.get_barrier_semaphore()
    for _, dev in peers1 + peers2 + peers3 + peers4:
        pl.semaphore_signal(barrier, inc=1, device_id=dev, device_id_type=MESH)
    for dev in ((up_x, up_y), (up_x, dn_y), (dn_x, up_y), (dn_x, dn_y), (up_x, me_y), (dn_x, me_y), (me_x, up_y), (me_x, dn_y)):
        pl.semaphore_signal(barrier, inc=1, device_id=dev, device_id_type=MESH)

    loads[1].wait()
    loads[2].wait()
    for step in range(STEPS):
        for axis in range(3):
            vel_ref[step, axis] = vel_in[step, axis].astype(jnp.float32)
    level = lax.rem(lax.broadcasted_iota(jnp.int32, (rows, 128), 0), 4)
    from_below = pltpu.roll(blk_ref[4], 1, 0)
    from_above = pltpu.roll(blk_ref[5], rows - 1, 0)
    solid = jnp.where(level == 3, from_below, from_above)
    fluid_ref[...] = 1.0 - solid.astype(jnp.float32)

    last_flow = [vel_ref[STEPS - 1, axis] for axis in range(3)]
    fluid_all = fluid_ref[...]
    for number in range(1, 19):
        weight = drag_weight(number, last_flow, fluid_all)
        hfield[number - 1] = jnp.where(blk_ref[number - 1] == 1, 0.0, weight)

    pl.semaphore_wait(barrier, len(peers1) + len(peers2) + len(peers3) + len(peers4) + 8)

    lam_sets = crossing(MOVING)
    h_sets = crossing(REVERSED)
    h_speeds = dict(REVERSED)
    lam_speeds = dict(MOVING)
    n_hi = len(lam_sets[2])
    n_lo = len(lam_sets[3])
    nx_hi = len(lam_sets[0])
    nx_lo = len(lam_sets[1])
    h_bufs = (
        lambda n: unpack_rows(xhi.at[0], nx_hi + h_sets[0].index(n), True),
        lambda n: unpack_rows(xlo.at[0], nx_lo + h_sets[1].index(n), False),
        lambda n: unpack_edge(yhi.at[0], n_hi + h_sets[2].index(n), 0),
        lambda n: unpack_edge(ylo.at[0], n_lo + h_sets[3].index(n), 127),
        hcorner,
    )
    h_copies = None
    sent = []
    drag_acc = jnp.zeros((8, 128), jnp.float32)

    for step in range(STEPS):
        src = lam_ref if step == 0 else state
        origin = lam_hbm if step == 0 else state
        bufs = (
            lambda n, s=step: unpack_rows(xhi.at[s], lam_sets[0].index(n), True),
            lambda n, s=step: unpack_rows(xlo.at[s], lam_sets[1].index(n), False),
            lambda n, s=step: unpack_edge(yhi.at[s], lam_sets[2].index(n), 0),
            lambda n, s=step: unpack_edge(ylo.at[s], lam_sets[3].index(n), 127),
            corner.at[step],
        )
        plan = send_plan(lam_sets, lam_speeds, lambda n: origin.at[n], bufs, top, near)
        copies = start_copies(plan, ssem.at[step], rsem.at[step])
        if step == 0:
            h_plan = send_plan(h_sets, h_speeds, lambda n: hfield.at[n - 1], h_bufs, top, near)
            h_copies = start_copies(h_plan, hsend, hrecv)
            loads[0].wait()
        to_low = [src[n] for n in lam_sets[2]]
        to_high = [src[n] for n in lam_sets[3]]
        if step == 0:
            to_low += [hfield[n - 1] for n in h_sets[2]]
            to_high += [hfield[n - 1] for n in h_sets[3]]
        x_low_tiles = [src[n, 0:8] for n in lam_sets[0]]
        x_high_tiles = [src[n, top:rows] for n in lam_sets[1]]
        if step == 0:
            x_low_tiles += [hfield[n - 1, 0:8] for n in h_sets[0]]
            x_high_tiles += [hfield[n - 1, top:rows] for n in h_sets[1]]
        count_lo = (len(x_low_tiles) + 1) // 2
        count_hi = (len(x_high_tiles) + 1) // 2
        xpack_lo[step, pl.ds(0, 8 * count_lo)] = pack_rows(x_low_tiles, True)
        xpack_hi[step, pl.ds(0, 8 * count_hi)] = pack_rows(x_high_tiles, False)
        copies += start_copies(
            [
                (xpack_lo.at[step, pl.ds(0, 8 * count_lo)], xhi.at[step, pl.ds(0, 8 * count_lo)], (dn_x, me_y)),
                (xpack_hi.at[step, pl.ds(0, 8 * count_hi)], xlo.at[step, pl.ds(0, 8 * count_hi)], (up_x, me_y)),
            ],
            xsend.at[step],
            xrecv.at[step],
        )
        ypack[step, 0] = pack_edge(to_low, 0, rows)
        ypack[step, 1] = pack_edge(to_high, 127, rows)
        copies += start_copies(
            [(ypack.at[step, 0], yhi.at[step], (me_x, dn_y)), (ypack.at[step, 1], ylo.at[step], (me_x, up_y))],
            ysend.at[step],
            yrecv.at[step],
        )
        if step == STEPS - 1:
            for copy in h_copies:
                copy.wait_recv()
            sent += h_copies
            total = drag_acc
            for number in range(1, 19):
                gathered = shifted(hfield[number - 1], h_speeds[number], number, h_sets, h_bufs, rows)
                total = total + jnp.sum((src[number] * gathered).reshape(rows // 8, 8, 128), axis=0)
            for number in range(1, 19):
                cx = lattice_speeds[number][0]
                weight = drag_weight(number, last_flow, fluid_all)
                bounced = jnp.where(blk_ref[number - 1] == 1, src[opposite_of(number)] + 2.0 * cx, 0.0)
                total = total + jnp.sum((weight * bounced).reshape(rows // 8, 8, 128), axis=0)
            part[...] = jnp.broadcast_to(jnp.sum(total), (8, 128))
            total = gather_sum(part, g1_buf, slot1, peers1, g1_send, g1_recv, sent)
            g1_sum[...] = total
            total = gather_sum(g1_sum, g2_buf, slot2, peers2, g2_send, g2_recv, sent)
            g2_sum[...] = total
            total = gather_sum(g2_sum, g3_buf, slot3, peers3, g3_send, g3_recv, sent)
            g3_sum[...] = total
            g4_copies = start_gather(g3_sum, g4_buf, slot4, peers4, g4_send, g4_recv)
            g4_buf[slot4] = total
        for copy in copies:
            copy.wait_recv()
        sent += copies

        moved[0] = src[0]
        for number in range(1, 19):
            source = shifted(src[number], lam_speeds[number], number, lam_sets, bufs, rows)
            bounced = src[opposite_of(number)] + 2.0 * lam_speeds[number][0]
            moved[number] = jnp.where(blk_ref[number - 1] == 1, bounced, source)


        dest = out_ref if step == STEPS - 1 else state

        def chunk(c, acc):
            at = pl.ds(pl.multiple_of(c * 8, 8), 8)
            flow = [vel_ref[step, axis, at] for axis in range(3)]
            mu = [moved[number, at] for number in range(19)]
            fresh, drag = collide(mu, flow, fluid_ref[at])
            for number in range(19):
                dest[number, at] = fresh[number]
            return acc + drag

        if step < STEPS - 1:
            drag_acc = lax.fori_loop(0, rows // 8, chunk, drag_acc)
        else:
            lax.fori_loop(0, rows // 8, chunk, drag_acc)

    for copy in g4_copies:
        copy.wait_recv()
    sent += g4_copies
    total = g4_buf[0]
    for j in range(1, far_z):
        total = total + g4_buf[j]
    drag_ref[0] = -scale * total[0, 0]
    for copy in sent:
        copy.wait_send()


def per_device(adjoint_in, velocity, solid_tiles, link_blocked):
    nx = lax.axis_size("gx")
    ny = lax.axis_size("gy")
    q, rows_x, levels, rows_y = adjoint_in.shape
    rows = rows_x * levels
    lam = adjoint_in.reshape(q, rows, rows_y)
    flow = velocity.reshape(STEPS, 3, rows, rows_y)
    blocked = link_blocked.reshape(q - 1, rows, rows_y)
    cell_count = rows_x * nx * rows_y * ny * levels
    scale = drag_factor / math.sqrt(cell_count)
    vmem = pl.BlockSpec(memory_space=pltpu.VMEM)
    NEAR_Z = min(4, 2 * ny // SPAN_X)
    x_tiles = max(
        (len(crossing(MOVING)[face]) + len(crossing(REVERSED)[face]) + 1) // 2 for face in (0, 1)
    )
    state, drag = pl.pallas_call(
        functools.partial(lbm_kernel, nx, ny, rows, scale),
        out_shape=(
            jax.ShapeDtypeStruct((q, rows, rows_y), jnp.float32),
            jax.ShapeDtypeStruct((1,), jnp.float32),
        ),
        in_specs=[pl.BlockSpec(memory_space=pl.ANY)] * 3,
        out_specs=(vmem, pl.BlockSpec(memory_space=pltpu.SMEM)),
        scratch_shapes=[
            pltpu.VMEM((q, rows, rows_y), jnp.float32),
            pltpu.VMEM((STEPS, 3, rows, rows_y), velocity.dtype),
            pltpu.VMEM((q - 1, rows, rows_y), link_blocked.dtype),
            pltpu.SemaphoreType.DMA((3,)),
            pltpu.VMEM((STEPS, 3, rows, rows_y), jnp.float32),
            pltpu.VMEM((rows, rows_y), jnp.float32),
            pltpu.VMEM((q, rows, rows_y), jnp.float32),
            pltpu.VMEM((q, rows, rows_y), jnp.float32),
            pltpu.VMEM((q - 1, rows, rows_y), jnp.float32),
        ]
        + [pltpu.VMEM((STEPS, 8 * x_tiles, rows_y), jnp.float32)] * 2
        + [pltpu.VMEM((STEPS, rows, rows_y), jnp.float32)] * 2
        + [pltpu.VMEM((STEPS, len(crossing(MOVING)[4]), 8, rows_y), jnp.float32)]
        + [pltpu.VMEM((len(crossing(REVERSED)[4]), 8, rows_y), jnp.float32)]
        + [
            pltpu.VMEM((STEPS, 2, rows, rows_y), jnp.float32),
            pltpu.SemaphoreType.DMA((STEPS, 2)),
            pltpu.SemaphoreType.DMA((STEPS, 2)),
            pltpu.VMEM((STEPS, 8 * x_tiles, rows_y), jnp.float32),
            pltpu.VMEM((STEPS, 8 * x_tiles, rows_y), jnp.float32),
            pltpu.SemaphoreType.DMA((STEPS, 2)),
            pltpu.SemaphoreType.DMA((STEPS, 2)),
        ]
        + [
            pltpu.VMEM((8, 128), jnp.float32),
            pltpu.VMEM((nx // 2, 8, 128), jnp.float32),
            pltpu.VMEM((SPAN_X, 8, 128), jnp.float32),
            pltpu.VMEM((NEAR_Z, 8, 128), jnp.float32),
            pltpu.VMEM((2 * ny // SPAN_X // NEAR_Z, 8, 128), jnp.float32),
            pltpu.VMEM((8, 128), jnp.float32),
            pltpu.VMEM((8, 128), jnp.float32),
            pltpu.VMEM((8, 128), jnp.float32),
            pltpu.SemaphoreType.DMA((STEPS, N_COPIES)),
            pltpu.SemaphoreType.DMA((STEPS, N_COPIES)),
            pltpu.SemaphoreType.DMA((N_COPIES,)),
            pltpu.SemaphoreType.DMA((N_COPIES,)),
            pltpu.SemaphoreType.DMA((nx // 2,)),
            pltpu.SemaphoreType.DMA((nx // 2,)),
            pltpu.SemaphoreType.DMA((SPAN_X,)),
            pltpu.SemaphoreType.DMA((SPAN_X,)),
            pltpu.SemaphoreType.DMA((NEAR_Z,)),
            pltpu.SemaphoreType.DMA((NEAR_Z,)),
            pltpu.SemaphoreType.DMA((2 * ny // SPAN_X // NEAR_Z,)),
            pltpu.SemaphoreType.DMA((2 * ny // SPAN_X // NEAR_Z,)),
        ],
        compiler_params=pltpu.CompilerParams(collective_id=0, has_side_effects=True),
    )(lam, flow, blocked)
    return (state.reshape(q, rows_x, levels, rows_y), drag)


def solution(mesh):
    placed = (
        P(None, "gx", None, "gy"),
        P(None, None, "gx", None, "gy"),
        P("gx", None, "gy"),
        P(None, "gx", None, "gy"),
    )
    return jax.shard_map(
        per_device,
        mesh=mesh,
        in_specs=placed,
        out_specs=(P(None, "gx", None, "gy"), P()),
        check_vma=False,
    )
```

```python
import functools
import math

import jax
import jax.numpy as jnp
from jax import lax
from jax.experimental import pallas as pl
from jax.experimental.pallas import tpu as pltpu
from jax.sharding import PartitionSpec as P

MESH = pl.DeviceIdType.MESH
SPAN_X = 4
TILE = 4
STEPS = 2

lattice_speeds = (
    (0, 0, 0),
    (1, 0, 0),
    (-1, 0, 0),
    (0, 1, 0),
    (0, -1, 0),
    (0, 0, 1),
    (0, 0, -1),
    (1, 1, 0),
    (-1, -1, 0),
    (1, -1, 0),
    (-1, 1, 0),
    (1, 0, 1),
    (-1, 0, -1),
    (1, 0, -1),
    (-1, 0, 1),
    (0, 1, 1),
    (0, -1, -1),
    (0, 1, -1),
    (0, -1, 1),
)
lattice_weights = (1.0 / 3.0,) + (1.0 / 18.0,) * 6 + (1.0 / 36.0,) * 12
relax_rate = 1.6
drag_factor = 20.0


def crossing(speeds):
    return (
        tuple(n for n, c in speeds if c[0] == 1),
        tuple(n for n, c in speeds if c[0] == -1),
        tuple(n for n, c in speeds if c[1] == 1),
        tuple(n for n, c in speeds if c[1] == -1),
        tuple(n for n, c in speeds if c[0] != 0 and c[1] != 0),
    )


MOVING = tuple((n, lattice_speeds[n]) for n in range(1, 19))
REVERSED = tuple((n, tuple(-v for v in lattice_speeds[n])) for n in range(1, 19))
N_COPIES = len(crossing(MOVING)[4])


def opposite_of(number):
    return number + 1 if number % 2 == 1 else number - 1


def along_of(speed, flow):
    along = None
    for axis in range(3):
        if speed[axis] == 0:
            continue
        term = flow[axis] if speed[axis] == 1 else -flow[axis]
        along = term if along is None else along + term
    return along


def collide(moved, flow, fluid):
    speed_sq = flow[0] * flow[0] + flow[1] * flow[1] + flow[2] * flow[2]
    scalar_part = None
    vector_part = [None, None, None]
    drag_local = None
    for number in range(19):
        speed = lattice_speeds[number]
        weighted = lattice_weights[number] * moved[number]
        along = along_of(speed, flow)
        if along is None:
            scalar_term = weighted * (1.0 - 1.5 * speed_sq)
        else:
            scalar_term = weighted * (1.0 + 3.0 * along + 4.5 * along * along - 1.5 * speed_sq)
            drag_term = 3.0 * weighted * along
            drag_local = drag_term if drag_local is None else drag_local + drag_term
        scalar_part = scalar_term if scalar_part is None else scalar_part + scalar_term
        for axis in range(3):
            if speed[axis] == 0:
                term = weighted * (-3.0 * flow[axis])
            else:
                term = weighted * (3.0 * speed[axis] + 9.0 * along * speed[axis] - 3.0 * flow[axis])
            vector_part[axis] = term if vector_part[axis] is None else vector_part[axis] + term
    results = []
    for number in range(19):
        speed = lattice_speeds[number]
        projected = scalar_part
        for axis in range(3):
            projected = projected + vector_part[axis] * (speed[axis] - flow[axis])
        results.append(fluid * ((1.0 - relax_rate) * moved[number] + relax_rate * projected))
    return results, fluid * drag_local


def send_plan(sets, speeds, field, bufs, top, near):
    up_x, dn_x, up_y, dn_y, me_x, me_y = near
    x_high, x_low, _, _, corners = sets
    xhi, xlo, _, _, corner = bufs
    plan = []
    for j, n in enumerate(corners):
        cx, cy, _ = speeds[n]
        rows_at = pl.ds(0, 8) if cx == 1 else pl.ds(top, 8)
        dev_x = dn_x if cx == 1 else up_x
        dev_y = dn_y if cy == 1 else up_y
        plan.append((field(n).at[rows_at], corner.at[j], (dev_x, dev_y)))
    return plan


def start_copies(plan, send_sems, recv_sems):
    copies = []
    for k, (from_ref, to_ref, dev) in enumerate(plan):
        copy = pltpu.make_async_remote_copy(
            src_ref=from_ref, dst_ref=to_ref, send_sem=send_sems.at[k],
            recv_sem=recv_sems.at[k], device_id=dev, device_id_type=MESH)
        copy.start()
        copies.append(copy)
    return copies


def shifted(own, speed, n, sets, bufs, rows):
    x_high, x_low, y_high, y_low, corners = sets
    xhi, xlo, yhi, ylo, corner = bufs
    cx, cy, cz = speed
    top = rows - 8
    row8 = lax.broadcasted_iota(jnp.int32, (8, 128), 0)
    lane = lax.broadcasted_iota(jnp.int32, (rows, 128), 1)
    level = lax.rem(lax.broadcasted_iota(jnp.int32, (rows, 128), 0), 4)

    def patch_x(block, tile):
        if cx == 1:
            head = jnp.where(row8 < 4, tile, block[0:8])
            return jnp.concatenate([head, block[8:]], axis=0)
        tail = jnp.where(row8 >= 4, tile, block[top:])
        return jnp.concatenate([block[:top], tail], axis=0)

    if cx == 1:
        own = patch_x(own, xhi(n))
    elif cx == -1:
        own = patch_x(own, xlo(n))
    if cy != 0:
        side = yhi(n) if cy == 1 else ylo(n)
        if cx != 0:
            side = patch_x(side, corner[corners.index(n)])
        edge = 0 if cy == 1 else 127
        own = jnp.where(lane == edge, side, own)
    shift = 4 * cx + cz
    if shift % rows:
        own = pltpu.roll(own, (-shift) % rows, 0)
    if cy != 0:
        own = pltpu.roll(own, (-cy) % 128, 1)
    if cz == 1:
        own = jnp.where(level == 3, 0.0, own)
    elif cz == -1:
        own = jnp.where(level == 0, 0.0, own)
    return own


def pack_edge(fields, from_lane, rows):
    lane = lax.broadcasted_iota(jnp.int32, (rows, 128), 1)
    packed = jnp.zeros((rows, 128), jnp.float32)
    for k, field in enumerate(fields):
        moved = field if k == from_lane else pltpu.roll(field, (k - from_lane) % 128, 1)
        packed = jnp.where(lane == k, moved, packed)
    return packed


def pack_rows(tiles, low_half):
    row8 = lax.broadcasted_iota(jnp.int32, (8, 128), 0)
    if len(tiles) % 2:
        tiles = tiles + [jnp.zeros((8, 128), jnp.float32)]
    packed = []
    for a, b in zip(tiles[0::2], tiles[1::2]):
        if low_half:
            packed.append(jnp.where(row8 < 4, a, pltpu.roll(b, 4, 0)))
        else:
            packed.append(jnp.where(row8 >= 4, b, pltpu.roll(a, 4, 0)))
    return jnp.concatenate(packed, axis=0)


def unpack_rows(packed_ref, k, low_half):
    tile = packed_ref[pl.ds(8 * (k // 2), 8)]
    if (k % 2 == 0) == low_half:
        return tile
    return pltpu.roll(tile, 4, 0)


def unpack_edge(packed_ref, k, to_lane):
    packed = packed_ref[...]
    return packed if k == to_lane else pltpu.roll(packed, (to_lane - k) % 128, 1)


def drag_weight(number, flow, fluid):
    return (3.0 * lattice_weights[number]) * along_of(lattice_speeds[number], flow) * fluid


def start_gather(value_ref, buf, slot, peers, send_sems, recv_sems):
    copies = []
    for k, dev in peers:
        copy = pltpu.make_async_remote_copy(
            src_ref=value_ref, dst_ref=buf.at[slot], send_sem=send_sems.at[k],
            recv_sem=recv_sems.at[k], device_id=dev, device_id_type=MESH)
        copy.start()
        copies.append(copy)
    return copies


def gather_sum(value_ref, buf, slot, peers, send_sems, recv_sems, sent):
    copies = start_gather(value_ref, buf, slot, peers, send_sems, recv_sems)
    buf[slot] = value_ref[...]
    for copy in copies:
        copy.wait_recv()
    sent += copies
    total = buf[0]
    for j in range(1, len(peers) + 1):
        total = total + buf[j]
    return total


def lbm_kernel(nx, ny, rows, scale, lam_hbm, vel_hbm, blk_hbm, out_ref, drag_ref,
               lam_ref, vel_in, blk_ref, load_sem, vel_ref, fluid_ref, moved, state, hfield, xhi, xlo, yhi, ylo, corner, hcorner, ypack, ysend, yrecv,
               xpack_lo, xpack_hi, xsend, xrecv,
               part, g1_buf, g2_buf, g3_buf, g1_sum, g2_sum,
               ssem, rsem, hsend, hrecv, g1_send, g1_recv, g2_send, g2_recv, g3_send, g3_recv):
    me_x = lax.axis_index("gx")
    me_y = lax.axis_index("gy")
    up_x = lax.rem(me_x + 1, nx)
    dn_x = lax.rem(me_x + nx - 1, nx)
    up_y = lax.rem(me_y + 1, ny)
    dn_y = lax.rem(me_y + ny - 1, ny)
    near = (up_x, dn_x, up_y, dn_y, me_x, me_y)
    top = rows - 8

    loads = [
        pltpu.make_async_copy(hbm, vmem, load_sem.at[k])
        for k, (hbm, vmem) in enumerate(((lam_hbm, lam_ref), (vel_hbm, vel_in), (blk_hbm, blk_ref)))
    ]
    for load in loads:
        load.start()

    b1, b2 = nx // 2, SPAN_X
    n3 = 2 * (ny // b2)
    slot1 = lax.rem(me_x, b1)
    slot2 = lax.rem(me_y, b2)
    slot3 = (me_x // b1) * (ny // b2) + me_y // b2
    slot12 = slot1 * b2 + slot2
    peers12 = []
    for k in range(1, b1 * b2):
        t = lax.rem(slot12 + k, b1 * b2)
        peers12.append((k, ((me_x // b1) * b1 + t // b2, (me_y // b2) * b2 + lax.rem(t, b2))))
    peers3 = []
    for k in range(1, n3):
        t = lax.rem(slot3 + k, n3)
        peers3.append((k, ((t // (ny // b2)) * b1 + slot1, lax.rem(t, ny // b2) * b2 + slot2)))

    barrier = pltpu.get_barrier_semaphore()
    for _, dev in peers12 + peers3:
        pl.semaphore_signal(barrier, inc=1, device_id=dev, device_id_type=MESH)
    for dev in ((up_x, up_y), (up_x, dn_y), (dn_x, up_y), (dn_x, dn_y), (up_x, me_y), (dn_x, me_y), (me_x, up_y), (me_x, dn_y)):
        pl.semaphore_signal(barrier, inc=1, device_id=dev, device_id_type=MESH)

    loads[1].wait()
    loads[2].wait()
    for step in range(STEPS):
        for axis in range(3):
            vel_ref[step, axis] = vel_in[step, axis].astype(jnp.float32)
    level = lax.rem(lax.broadcasted_iota(jnp.int32, (rows, 128), 0), 4)
    from_below = pltpu.roll(blk_ref[4], 1, 0)
    from_above = pltpu.roll(blk_ref[5], rows - 1, 0)
    solid = jnp.where(level == 3, from_below, from_above)
    fluid_ref[...] = 1.0 - solid.astype(jnp.float32)

    last_flow = [vel_ref[STEPS - 1, axis] for axis in range(3)]
    fluid_all = fluid_ref[...]
    for number in range(1, 19):
        weight = drag_weight(number, last_flow, fluid_all)
        hfield[number - 1] = jnp.where(blk_ref[number - 1] == 1, 0.0, weight)

    pl.semaphore_wait(barrier, len(peers12) + len(peers3) + 8)

    lam_sets = crossing(MOVING)
    h_sets = crossing(REVERSED)
    h_speeds = dict(REVERSED)
    lam_speeds = dict(MOVING)
    n_hi = len(lam_sets[2])
    n_lo = len(lam_sets[3])
    nx_hi = len(lam_sets[0])
    nx_lo = len(lam_sets[1])
    h_bufs = (
        lambda n: unpack_rows(xhi.at[0], nx_hi + h_sets[0].index(n), True),
        lambda n: unpack_rows(xlo.at[0], nx_lo + h_sets[1].index(n), False),
        lambda n: unpack_edge(yhi.at[0], n_hi + h_sets[2].index(n), 0),
        lambda n: unpack_edge(ylo.at[0], n_lo + h_sets[3].index(n), 127),
        hcorner,
    )
    h_copies = None
    sent = []
    drag_acc = jnp.zeros((8, 128), jnp.float32)

    for step in range(STEPS):
        src = lam_ref if step == 0 else state
        origin = lam_hbm if step == 0 else state
        bufs = (
            lambda n, s=step: unpack_rows(xhi.at[s], lam_sets[0].index(n), True),
            lambda n, s=step: unpack_rows(xlo.at[s], lam_sets[1].index(n), False),
            lambda n, s=step: unpack_edge(yhi.at[s], lam_sets[2].index(n), 0),
            lambda n, s=step: unpack_edge(ylo.at[s], lam_sets[3].index(n), 127),
            corner.at[step],
        )
        plan = send_plan(lam_sets, lam_speeds, lambda n: origin.at[n], bufs, top, near)
        copies = start_copies(plan, ssem.at[step], rsem.at[step])
        if step == 0:
            h_plan = send_plan(h_sets, h_speeds, lambda n: hfield.at[n - 1], h_bufs, top, near)
            h_copies = start_copies(h_plan, hsend, hrecv)
            loads[0].wait()
        to_low = [src[n] for n in lam_sets[2]]
        to_high = [src[n] for n in lam_sets[3]]
        if step == 0:
            to_low += [hfield[n - 1] for n in h_sets[2]]
            to_high += [hfield[n - 1] for n in h_sets[3]]
        x_low_tiles = [src[n, 0:8] for n in lam_sets[0]]
        x_high_tiles = [src[n, top:rows] for n in lam_sets[1]]
        if step == 0:
            x_low_tiles += [hfield[n - 1, 0:8] for n in h_sets[0]]
            x_high_tiles += [hfield[n - 1, top:rows] for n in h_sets[1]]
        count_lo = (len(x_low_tiles) + 1) // 2
        count_hi = (len(x_high_tiles) + 1) // 2
        xpack_lo[step, pl.ds(0, 8 * count_lo)] = pack_rows(x_low_tiles, True)
        xpack_hi[step, pl.ds(0, 8 * count_hi)] = pack_rows(x_high_tiles, False)
        copies += start_copies(
            [
                (xpack_lo.at[step, pl.ds(0, 8 * count_lo)], xhi.at[step, pl.ds(0, 8 * count_lo)], (dn_x, me_y)),
                (xpack_hi.at[step, pl.ds(0, 8 * count_hi)], xlo.at[step, pl.ds(0, 8 * count_hi)], (up_x, me_y)),
            ],
            xsend.at[step],
            xrecv.at[step],
        )
        ypack[step, 0] = pack_edge(to_low, 0, rows)
        ypack[step, 1] = pack_edge(to_high, 127, rows)
        copies += start_copies(
            [(ypack.at[step, 0], yhi.at[step], (me_x, dn_y)), (ypack.at[step, 1], ylo.at[step], (me_x, up_y))],
            ysend.at[step],
            yrecv.at[step],
        )
        if step == STEPS - 1:
            for copy in h_copies:
                copy.wait_recv()
            sent += h_copies
            total = drag_acc
            for number in range(1, 19):
                gathered = shifted(hfield[number - 1], h_speeds[number], number, h_sets, h_bufs, rows)
                total = total + jnp.sum((src[number] * gathered).reshape(rows // 8, 8, 128), axis=0)
            for number in range(1, 19):
                cx = lattice_speeds[number][0]
                weight = drag_weight(number, last_flow, fluid_all)
                bounced = jnp.where(blk_ref[number - 1] == 1, src[opposite_of(number)] + 2.0 * cx, 0.0)
                total = total + jnp.sum((weight * bounced).reshape(rows // 8, 8, 128), axis=0)
            part[...] = jnp.broadcast_to(jnp.sum(total), (8, 128))
            total = gather_sum(part, g1_buf, slot12, peers12, g1_send, g1_recv, sent)
            g2_sum[...] = total
            g3_copies = start_gather(g2_sum, g3_buf, slot3, peers3, g3_send, g3_recv)
            g3_buf[slot3] = total
        for copy in copies:
            copy.wait_recv()
        sent += copies

        moved[0] = src[0]
        for number in range(1, 19):
            source = shifted(src[number], lam_speeds[number], number, lam_sets, bufs, rows)
            bounced = src[opposite_of(number)] + 2.0 * lam_speeds[number][0]
            moved[number] = jnp.where(blk_ref[number - 1] == 1, bounced, source)


        dest = out_ref if step == STEPS - 1 else state

        def chunk(c, acc):
            at = pl.ds(pl.multiple_of(c * 8, 8), 8)
            flow = [vel_ref[step, axis, at] for axis in range(3)]
            mu = [moved[number, at] for number in range(19)]
            fresh, drag = collide(mu, flow, fluid_ref[at])
            for number in range(19):
                dest[number, at] = fresh[number]
            return acc + drag

        if step < STEPS - 1:
            drag_acc = lax.fori_loop(0, rows // 8, chunk, drag_acc)
        else:
            lax.fori_loop(0, rows // 8, chunk, drag_acc)

    for copy in g3_copies:
        copy.wait_recv()
    sent += g3_copies
    total = g3_buf[0]
    for j in range(1, n3):
        total = total + g3_buf[j]
    drag_ref[0] = -scale * total[0, 0]
    for copy in sent:
        copy.wait_send()


def per_device(adjoint_in, velocity, solid_tiles, link_blocked):
    nx = lax.axis_size("gx")
    ny = lax.axis_size("gy")
    q, rows_x, levels, rows_y = adjoint_in.shape
    rows = rows_x * levels
    lam = adjoint_in.reshape(q, rows, rows_y)
    flow = velocity.reshape(STEPS, 3, rows, rows_y)
    blocked = link_blocked.reshape(q - 1, rows, rows_y)
    cell_count = rows_x * nx * rows_y * ny * levels
    scale = drag_factor / math.sqrt(cell_count)
    vmem = pl.BlockSpec(memory_space=pltpu.VMEM)
    x_tiles = max(
        (len(crossing(MOVING)[face]) + len(crossing(REVERSED)[face]) + 1) // 2 for face in (0, 1)
    )
    state, drag = pl.pallas_call(
        functools.partial(lbm_kernel, nx, ny, rows, scale),
        out_shape=(
            jax.ShapeDtypeStruct((q, rows, rows_y), jnp.float32),
            jax.ShapeDtypeStruct((1,), jnp.float32),
        ),
        in_specs=[pl.BlockSpec(memory_space=pl.ANY)] * 3,
        out_specs=(vmem, pl.BlockSpec(memory_space=pltpu.SMEM)),
        scratch_shapes=[
            pltpu.VMEM((q, rows, rows_y), jnp.float32),
            pltpu.VMEM((STEPS, 3, rows, rows_y), velocity.dtype),
            pltpu.VMEM((q - 1, rows, rows_y), link_blocked.dtype),
            pltpu.SemaphoreType.DMA((3,)),
            pltpu.VMEM((STEPS, 3, rows, rows_y), jnp.float32),
            pltpu.VMEM((rows, rows_y), jnp.float32),
            pltpu.VMEM((q, rows, rows_y), jnp.float32),
            pltpu.VMEM((q, rows, rows_y), jnp.float32),
            pltpu.VMEM((q - 1, rows, rows_y), jnp.float32),
        ]
        + [pltpu.VMEM((STEPS, 8 * x_tiles, rows_y), jnp.float32)] * 2
        + [pltpu.VMEM((STEPS, rows, rows_y), jnp.float32)] * 2
        + [pltpu.VMEM((STEPS, len(crossing(MOVING)[4]), 8, rows_y), jnp.float32)]
        + [pltpu.VMEM((len(crossing(REVERSED)[4]), 8, rows_y), jnp.float32)]
        + [
            pltpu.VMEM((STEPS, 2, rows, rows_y), jnp.float32),
            pltpu.SemaphoreType.DMA((STEPS, 2)),
            pltpu.SemaphoreType.DMA((STEPS, 2)),
            pltpu.VMEM((STEPS, 8 * x_tiles, rows_y), jnp.float32),
            pltpu.VMEM((STEPS, 8 * x_tiles, rows_y), jnp.float32),
            pltpu.SemaphoreType.DMA((STEPS, 2)),
            pltpu.SemaphoreType.DMA((STEPS, 2)),
        ]
        + [
            pltpu.VMEM((8, 128), jnp.float32),
            pltpu.VMEM((nx // 2 * SPAN_X, 8, 128), jnp.float32),
            pltpu.VMEM((SPAN_X, 8, 128), jnp.float32),
            pltpu.VMEM((2 * ny // SPAN_X, 8, 128), jnp.float32),
            pltpu.VMEM((8, 128), jnp.float32),
            pltpu.VMEM((8, 128), jnp.float32),
            pltpu.SemaphoreType.DMA((STEPS, N_COPIES)),
            pltpu.SemaphoreType.DMA((STEPS, N_COPIES)),
            pltpu.SemaphoreType.DMA((N_COPIES,)),
            pltpu.SemaphoreType.DMA((N_COPIES,)),
            pltpu.SemaphoreType.DMA((nx // 2 * SPAN_X,)),
            pltpu.SemaphoreType.DMA((nx // 2 * SPAN_X,)),
            pltpu.SemaphoreType.DMA((SPAN_X,)),
            pltpu.SemaphoreType.DMA((SPAN_X,)),
            pltpu.SemaphoreType.DMA((2 * ny // SPAN_X,)),
            pltpu.SemaphoreType.DMA((2 * ny // SPAN_X,)),
        ],
        compiler_params=pltpu.CompilerParams(collective_id=0, has_side_effects=True),
    )(lam, flow, blocked)
    return (state.reshape(q, rows_x, levels, rows_y), drag)


def solution(mesh):
    placed = (
        P(None, "gx", None, "gy"),
        P(None, None, "gx", None, "gy"),
        P("gx", None, "gy"),
        P(None, "gx", None, "gy"),
    )
    return jax.shard_map(
        per_device,
        mesh=mesh,
        in_specs=placed,
        out_specs=(P(None, "gx", None, "gy"), P()),
        check_vma=False,
    )
```

```python
import functools
import math

import jax
import jax.numpy as jnp
from jax import lax
from jax.experimental import pallas as pl
from jax.experimental.pallas import tpu as pltpu
from jax.sharding import PartitionSpec as P

MESH = pl.DeviceIdType.MESH
SPAN_X = 4
TILE = 4
STEPS = 2

lattice_speeds = (
    (0, 0, 0),
    (1, 0, 0),
    (-1, 0, 0),
    (0, 1, 0),
    (0, -1, 0),
    (0, 0, 1),
    (0, 0, -1),
    (1, 1, 0),
    (-1, -1, 0),
    (1, -1, 0),
    (-1, 1, 0),
    (1, 0, 1),
    (-1, 0, -1),
    (1, 0, -1),
    (-1, 0, 1),
    (0, 1, 1),
    (0, -1, -1),
    (0, 1, -1),
    (0, -1, 1),
)
lattice_weights = (1.0 / 3.0,) + (1.0 / 18.0,) * 6 + (1.0 / 36.0,) * 12
relax_rate = 1.6
drag_factor = 20.0


def crossing(speeds):
    return (
        tuple(n for n, c in speeds if c[0] == 1),
        tuple(n for n, c in speeds if c[0] == -1),
        tuple(n for n, c in speeds if c[1] == 1),
        tuple(n for n, c in speeds if c[1] == -1),
        tuple(n for n, c in speeds if c[0] != 0 and c[1] != 0),
    )


MOVING = tuple((n, lattice_speeds[n]) for n in range(1, 19))
REVERSED = tuple((n, tuple(-v for v in lattice_speeds[n])) for n in range(1, 19))
N_COPIES = len(crossing(MOVING)[4])


def opposite_of(number):
    return number + 1 if number % 2 == 1 else number - 1


def along_of(speed, flow):
    along = None
    for axis in range(3):
        if speed[axis] == 0:
            continue
        term = flow[axis] if speed[axis] == 1 else -flow[axis]
        along = term if along is None else along + term
    return along


def collide(moved, flow, fluid):
    speed_sq = flow[0] * flow[0] + flow[1] * flow[1] + flow[2] * flow[2]
    scalar_part = None
    vector_part = [None, None, None]
    drag_local = None
    for number in range(19):
        speed = lattice_speeds[number]
        weighted = lattice_weights[number] * moved[number]
        along = along_of(speed, flow)
        if along is None:
            scalar_term = weighted * (1.0 - 1.5 * speed_sq)
        else:
            scalar_term = weighted * (1.0 + 3.0 * along + 4.5 * along * along - 1.5 * speed_sq)
            drag_term = 3.0 * weighted * along
            drag_local = drag_term if drag_local is None else drag_local + drag_term
        scalar_part = scalar_term if scalar_part is None else scalar_part + scalar_term
        for axis in range(3):
            if speed[axis] == 0:
                term = weighted * (-3.0 * flow[axis])
            else:
                term = weighted * (3.0 * speed[axis] + 9.0 * along * speed[axis] - 3.0 * flow[axis])
            vector_part[axis] = term if vector_part[axis] is None else vector_part[axis] + term
    results = []
    for number in range(19):
        speed = lattice_speeds[number]
        projected = scalar_part
        for axis in range(3):
            projected = projected + vector_part[axis] * (speed[axis] - flow[axis])
        results.append(fluid * ((1.0 - relax_rate) * moved[number] + relax_rate * projected))
    return results, fluid * drag_local


def send_plan(sets, speeds, field, bufs, top, near):
    up_x, dn_x, up_y, dn_y, me_x, me_y = near
    x_high, x_low, _, _, corners = sets
    xhi, xlo, _, _, corner = bufs
    plan = []
    for j, n in enumerate(corners):
        cx, cy, _ = speeds[n]
        rows_at = pl.ds(0, 8) if cx == 1 else pl.ds(top, 8)
        dev_x = dn_x if cx == 1 else up_x
        dev_y = dn_y if cy == 1 else up_y
        plan.append((field(n).at[rows_at], corner.at[j], (dev_x, dev_y)))
    return plan


def start_copies(plan, send_sems, recv_sems):
    copies = []
    for k, (from_ref, to_ref, dev) in enumerate(plan):
        copy = pltpu.make_async_remote_copy(
            src_ref=from_ref, dst_ref=to_ref, send_sem=send_sems.at[k],
            recv_sem=recv_sems.at[k], device_id=dev, device_id_type=MESH)
        copy.start()
        copies.append(copy)
    return copies


def shifted(own, speed, n, sets, bufs, rows):
    x_high, x_low, y_high, y_low, corners = sets
    xhi, xlo, yhi, ylo, corner = bufs
    cx, cy, cz = speed
    top = rows - 8
    row8 = lax.broadcasted_iota(jnp.int32, (8, 128), 0)
    lane = lax.broadcasted_iota(jnp.int32, (rows, 128), 1)
    level = lax.rem(lax.broadcasted_iota(jnp.int32, (rows, 128), 0), 4)

    def patch_x(block, tile):
        if cx == 1:
            head = jnp.where(row8 < 4, tile, block[0:8])
            return jnp.concatenate([head, block[8:]], axis=0)
        tail = jnp.where(row8 >= 4, tile, block[top:])
        return jnp.concatenate([block[:top], tail], axis=0)

    if cx == 1:
        own = patch_x(own, xhi(n))
    elif cx == -1:
        own = patch_x(own, xlo(n))
    if cy != 0:
        side = yhi(n) if cy == 1 else ylo(n)
        if cx != 0:
            side = patch_x(side, corner[corners.index(n)])
        edge = 0 if cy == 1 else 127
        own = jnp.where(lane == edge, side, own)
    shift = 4 * cx + cz
    if shift % rows:
        own = pltpu.roll(own, (-shift) % rows, 0)
    if cy != 0:
        own = pltpu.roll(own, (-cy) % 128, 1)
    if cz == 1:
        own = jnp.where(level == 3, 0.0, own)
    elif cz == -1:
        own = jnp.where(level == 0, 0.0, own)
    return own


def pack_edge(fields, from_lane, rows):
    lane = lax.broadcasted_iota(jnp.int32, (rows, 128), 1)
    packed = jnp.zeros((rows, 128), jnp.float32)
    for k, field in enumerate(fields):
        moved = field if k == from_lane else pltpu.roll(field, (k - from_lane) % 128, 1)
        packed = jnp.where(lane == k, moved, packed)
    return packed


def pack_rows(tiles, low_half):
    row8 = lax.broadcasted_iota(jnp.int32, (8, 128), 0)
    if len(tiles) % 2:
        tiles = tiles + [jnp.zeros((8, 128), jnp.float32)]
    packed = []
    for a, b in zip(tiles[0::2], tiles[1::2]):
        if low_half:
            packed.append(jnp.where(row8 < 4, a, pltpu.roll(b, 4, 0)))
        else:
            packed.append(jnp.where(row8 >= 4, b, pltpu.roll(a, 4, 0)))
    return jnp.concatenate(packed, axis=0)


def unpack_rows(packed_ref, k, low_half):
    tile = packed_ref[pl.ds(8 * (k // 2), 8)]
    if (k % 2 == 0) == low_half:
        return tile
    return pltpu.roll(tile, 4, 0)


def unpack_edge(packed_ref, k, to_lane):
    packed = packed_ref[...]
    return packed if k == to_lane else pltpu.roll(packed, (to_lane - k) % 128, 1)


def drag_weight(number, flow, fluid):
    return (3.0 * lattice_weights[number]) * along_of(lattice_speeds[number], flow) * fluid


def start_gather(value_ref, buf, slot, peers, send_sems, recv_sems):
    copies = []
    for k, dev in peers:
        copy = pltpu.make_async_remote_copy(
            src_ref=value_ref, dst_ref=buf.at[slot], send_sem=send_sems.at[k],
            recv_sem=recv_sems.at[k], device_id=dev, device_id_type=MESH)
        copy.start()
        copies.append(copy)
    return copies


def gather_sum(value_ref, buf, slot, peers, send_sems, recv_sems, sent):
    copies = start_gather(value_ref, buf, slot, peers, send_sems, recv_sems)
    buf[slot] = value_ref[...]
    for copy in copies:
        copy.wait_recv()
    sent += copies
    total = buf[0]
    for j in range(1, len(peers) + 1):
        total = total + buf[j]
    return total


def lbm_kernel(nx, ny, rows, scale, lam_hbm, vel_hbm, blk_hbm, out_ref, drag_ref,
               lam_ref, vel_in, blk_ref, load_sem, vel_ref, fluid_ref, moved, state, hfield, xhi, xlo, yhi, ylo, corner, hcorner, ypack, ysend, yrecv,
               xpack_lo, xpack_hi, xsend, xrecv,
               part, g1_buf, g2_buf, g3_buf, g1_sum, g2_sum,
               ssem, rsem, hsend, hrecv, g1_send, g1_recv, g2_send, g2_recv, g3_send, g3_recv):
    me_x = lax.axis_index("gx")
    me_y = lax.axis_index("gy")
    up_x = lax.rem(me_x + 1, nx)
    dn_x = lax.rem(me_x + nx - 1, nx)
    up_y = lax.rem(me_y + 1, ny)
    dn_y = lax.rem(me_y + ny - 1, ny)
    near = (up_x, dn_x, up_y, dn_y, me_x, me_y)
    top = rows - 8

    loads = [
        pltpu.make_async_copy(hbm, vmem, load_sem.at[k])
        for k, (hbm, vmem) in enumerate(((lam_hbm, lam_ref), (vel_hbm, vel_in), (blk_hbm, blk_ref)))
    ]
    for load in loads:
        load.start()

    b1, b2 = nx // 2, SPAN_X
    n3 = 2 * (ny // b2)
    slot1 = lax.rem(me_x, b1)
    slot2 = lax.rem(me_y, b2)
    slot3 = (me_x // b1) * (ny // b2) + me_y // b2
    slot12 = slot1 * b2 + slot2
    peers12 = []
    for k in range(1, b1 * b2):
        t = lax.rem(slot12 + k, b1 * b2)
        peers12.append((k, ((me_x // b1) * b1 + t // b2, (me_y // b2) * b2 + lax.rem(t, b2))))
    peers3 = []
    for k in range(1, n3):
        t = lax.rem(slot3 + k, n3)
        peers3.append((k, ((t // (ny // b2)) * b1 + slot1, lax.rem(t, ny // b2) * b2 + slot2)))

    barrier = pltpu.get_barrier_semaphore()
    for _, dev in peers12 + peers3:
        pl.semaphore_signal(barrier, inc=1, device_id=dev, device_id_type=MESH)
    for dev in ((up_x, up_y), (up_x, dn_y), (dn_x, up_y), (dn_x, dn_y), (up_x, me_y), (dn_x, me_y), (me_x, up_y), (me_x, dn_y)):
        pl.semaphore_signal(barrier, inc=1, device_id=dev, device_id_type=MESH)

    loads[1].wait()
    loads[2].wait()
    for step in range(STEPS):
        for axis in range(3):
            vel_ref[step, axis] = vel_in[step, axis].astype(jnp.float32)
    level = lax.rem(lax.broadcasted_iota(jnp.int32, (rows, 128), 0), 4)
    from_below = pltpu.roll(blk_ref[4], 1, 0)
    from_above = pltpu.roll(blk_ref[5], rows - 1, 0)
    solid = jnp.where(level == 3, from_below, from_above)
    fluid_ref[...] = 1.0 - solid.astype(jnp.float32)

    last_flow = [vel_ref[STEPS - 1, axis] for axis in range(3)]
    fluid_all = fluid_ref[...]
    for number in range(1, 19):
        weight = drag_weight(number, last_flow, fluid_all)
        hfield[number - 1] = jnp.where(blk_ref[number - 1] == 1, 0.0, weight)

    pl.semaphore_wait(barrier, len(peers12) + len(peers3) + 8)

    lam_sets = crossing(MOVING)
    h_sets = crossing(REVERSED)
    h_speeds = dict(REVERSED)
    lam_speeds = dict(MOVING)
    n_hi = len(lam_sets[2])
    n_lo = len(lam_sets[3])
    nx_hi = len(lam_sets[0])
    nx_lo = len(lam_sets[1])
    h_bufs = (
        lambda n: unpack_rows(xhi.at[0], nx_hi + h_sets[0].index(n), True),
        lambda n: unpack_rows(xlo.at[0], nx_lo + h_sets[1].index(n), False),
        lambda n: unpack_edge(yhi.at[0], n_hi + h_sets[2].index(n), 0),
        lambda n: unpack_edge(ylo.at[0], n_lo + h_sets[3].index(n), 127),
        hcorner,
    )
    h_copies = None
    sent = []
    drag_acc = jnp.zeros((8, 128), jnp.float32)

    for step in range(STEPS):
        src = lam_ref if step == 0 else state
        origin = lam_hbm if step == 0 else state
        bufs = (
            lambda n, s=step: unpack_rows(xhi.at[s], lam_sets[0].index(n), True),
            lambda n, s=step: unpack_rows(xlo.at[s], lam_sets[1].index(n), False),
            lambda n, s=step: unpack_edge(yhi.at[s], lam_sets[2].index(n), 0),
            lambda n, s=step: unpack_edge(ylo.at[s], lam_sets[3].index(n), 127),
            corner.at[step],
        )
        plan = send_plan(lam_sets, lam_speeds, lambda n: origin.at[n], bufs, top, near)
        copies = start_copies(plan, ssem.at[step], rsem.at[step])
        if step == 0:
            h_plan = send_plan(h_sets, h_speeds, lambda n: hfield.at[n - 1], h_bufs, top, near)
            h_copies = start_copies(h_plan, hsend, hrecv)
            loads[0].wait()
        to_low = [src[n] for n in lam_sets[2]]
        to_high = [src[n] for n in lam_sets[3]]
        if step == 0:
            to_low += [hfield[n - 1] for n in h_sets[2]]
            to_high += [hfield[n - 1] for n in h_sets[3]]
        x_low_tiles = [src[n, 0:8] for n in lam_sets[0]]
        x_high_tiles = [src[n, top:rows] for n in lam_sets[1]]
        if step == 0:
            x_low_tiles += [hfield[n - 1, 0:8] for n in h_sets[0]]
            x_high_tiles += [hfield[n - 1, top:rows] for n in h_sets[1]]
        count_lo = (len(x_low_tiles) + 1) // 2
        count_hi = (len(x_high_tiles) + 1) // 2
        xpack_lo[step, pl.ds(0, 8 * count_lo)] = pack_rows(x_low_tiles, True)
        xpack_hi[step, pl.ds(0, 8 * count_hi)] = pack_rows(x_high_tiles, False)
        copies += start_copies(
            [
                (xpack_lo.at[step, pl.ds(0, 8 * count_lo)], xhi.at[step, pl.ds(0, 8 * count_lo)], (dn_x, me_y)),
                (xpack_hi.at[step, pl.ds(0, 8 * count_hi)], xlo.at[step, pl.ds(0, 8 * count_hi)], (up_x, me_y)),
            ],
            xsend.at[step],
            xrecv.at[step],
        )
        ypack[step, 0] = pack_edge(to_low, 0, rows)
        ypack[step, 1] = pack_edge(to_high, 127, rows)
        copies += start_copies(
            [(ypack.at[step, 0], yhi.at[step], (me_x, dn_y)), (ypack.at[step, 1], ylo.at[step], (me_x, up_y))],
            ysend.at[step],
            yrecv.at[step],
        )
        if step == STEPS - 1:
            for copy in h_copies:
                copy.wait_recv()
            sent += h_copies
            total = drag_acc
            for number in range(1, 19):
                gathered = shifted(hfield[number - 1], h_speeds[number], number, h_sets, h_bufs, rows)
                total = total + jnp.sum((src[number] * gathered).reshape(rows // 8, 8, 128), axis=0)
            for number in range(1, 19):
                cx = lattice_speeds[number][0]
                weight = drag_weight(number, last_flow, fluid_all)
                bounced = jnp.where(blk_ref[number - 1] == 1, src[opposite_of(number)] + 2.0 * cx, 0.0)
                total = total + jnp.sum((weight * bounced).reshape(rows // 8, 8, 128), axis=0)
            part[...] = jnp.broadcast_to(jnp.sum(total), (8, 128))
            g1_copies = start_gather(part, g1_buf, slot12, peers12, g1_send, g1_recv)
            g1_buf[slot12] = part[...]
        for copy in copies:
            copy.wait_recv()
        sent += copies

        moved[0] = src[0]
        for number in range(1, 19):
            source = shifted(src[number], lam_speeds[number], number, lam_sets, bufs, rows)
            bounced = src[opposite_of(number)] + 2.0 * lam_speeds[number][0]
            moved[number] = jnp.where(blk_ref[number - 1] == 1, bounced, source)


        if step == STEPS - 1:
            for copy in g1_copies:
                copy.wait_recv()
            sent += g1_copies
            total = g1_buf[0]
            for j in range(1, len(peers12) + 1):
                total = total + g1_buf[j]
            g2_sum[...] = total
            g3_copies = start_gather(g2_sum, g3_buf, slot3, peers3, g3_send, g3_recv)
            g3_buf[slot3] = total

        dest = out_ref if step == STEPS - 1 else state

        def chunk(c, acc):
            at = pl.ds(pl.multiple_of(c * 8, 8), 8)
            flow = [vel_ref[step, axis, at] for axis in range(3)]
            mu = [moved[number, at] for number in range(19)]
            fresh, drag = collide(mu, flow, fluid_ref[at])
            for number in range(19):
                dest[number, at] = fresh[number]
            return acc + drag

        if step < STEPS - 1:
            drag_acc = lax.fori_loop(0, rows // 8, chunk, drag_acc)
        else:
            lax.fori_loop(0, rows // 8, chunk, drag_acc)

    for copy in g3_copies:
        copy.wait_recv()
    sent += g3_copies
    total = g3_buf[0]
    for j in range(1, n3):
        total = total + g3_buf[j]
    drag_ref[0] = -scale * total[0, 0]
    for copy in sent:
        copy.wait_send()


def per_device(adjoint_in, velocity, solid_tiles, link_blocked):
    nx = lax.axis_size("gx")
    ny = lax.axis_size("gy")
    q, rows_x, levels, rows_y = adjoint_in.shape
    rows = rows_x * levels
    lam = adjoint_in.reshape(q, rows, rows_y)
    flow = velocity.reshape(STEPS, 3, rows, rows_y)
    blocked = link_blocked.reshape(q - 1, rows, rows_y)
    cell_count = rows_x * nx * rows_y * ny * levels
    scale = drag_factor / math.sqrt(cell_count)
    vmem = pl.BlockSpec(memory_space=pltpu.VMEM)
    x_tiles = max(
        (len(crossing(MOVING)[face]) + len(crossing(REVERSED)[face]) + 1) // 2 for face in (0, 1)
    )
    state, drag = pl.pallas_call(
        functools.partial(lbm_kernel, nx, ny, rows, scale),
        out_shape=(
            jax.ShapeDtypeStruct((q, rows, rows_y), jnp.float32),
            jax.ShapeDtypeStruct((1,), jnp.float32),
        ),
        in_specs=[pl.BlockSpec(memory_space=pl.ANY)] * 3,
        out_specs=(vmem, pl.BlockSpec(memory_space=pltpu.SMEM)),
        scratch_shapes=[
            pltpu.VMEM((q, rows, rows_y), jnp.float32),
            pltpu.VMEM((STEPS, 3, rows, rows_y), velocity.dtype),
            pltpu.VMEM((q - 1, rows, rows_y), link_blocked.dtype),
            pltpu.SemaphoreType.DMA((3,)),
            pltpu.VMEM((STEPS, 3, rows, rows_y), jnp.float32),
            pltpu.VMEM((rows, rows_y), jnp.float32),
            pltpu.VMEM((q, rows, rows_y), jnp.float32),
            pltpu.VMEM((q, rows, rows_y), jnp.float32),
            pltpu.VMEM((q - 1, rows, rows_y), jnp.float32),
        ]
        + [pltpu.VMEM((STEPS, 8 * x_tiles, rows_y), jnp.float32)] * 2
        + [pltpu.VMEM((STEPS, rows, rows_y), jnp.float32)] * 2
        + [pltpu.VMEM((STEPS, len(crossing(MOVING)[4]), 8, rows_y), jnp.float32)]
        + [pltpu.VMEM((len(crossing(REVERSED)[4]), 8, rows_y), jnp.float32)]
        + [
            pltpu.VMEM((STEPS, 2, rows, rows_y), jnp.float32),
            pltpu.SemaphoreType.DMA((STEPS, 2)),
            pltpu.SemaphoreType.DMA((STEPS, 2)),
            pltpu.VMEM((STEPS, 8 * x_tiles, rows_y), jnp.float32),
            pltpu.VMEM((STEPS, 8 * x_tiles, rows_y), jnp.float32),
            pltpu.SemaphoreType.DMA((STEPS, 2)),
            pltpu.SemaphoreType.DMA((STEPS, 2)),
        ]
        + [
            pltpu.VMEM((8, 128), jnp.float32),
            pltpu.VMEM((nx // 2 * SPAN_X, 8, 128), jnp.float32),
            pltpu.VMEM((SPAN_X, 8, 128), jnp.float32),
            pltpu.VMEM((2 * ny // SPAN_X, 8, 128), jnp.float32),
            pltpu.VMEM((8, 128), jnp.float32),
            pltpu.VMEM((8, 128), jnp.float32),
            pltpu.SemaphoreType.DMA((STEPS, N_COPIES)),
            pltpu.SemaphoreType.DMA((STEPS, N_COPIES)),
            pltpu.SemaphoreType.DMA((N_COPIES,)),
            pltpu.SemaphoreType.DMA((N_COPIES,)),
            pltpu.SemaphoreType.DMA((nx // 2 * SPAN_X,)),
            pltpu.SemaphoreType.DMA((nx // 2 * SPAN_X,)),
            pltpu.SemaphoreType.DMA((SPAN_X,)),
            pltpu.SemaphoreType.DMA((SPAN_X,)),
            pltpu.SemaphoreType.DMA((2 * ny // SPAN_X,)),
            pltpu.SemaphoreType.DMA((2 * ny // SPAN_X,)),
        ],
        compiler_params=pltpu.CompilerParams(collective_id=0, has_side_effects=True),
    )(lam, flow, blocked)
    return (state.reshape(q, rows_x, levels, rows_y), drag)


def solution(mesh):
    placed = (
        P(None, "gx", None, "gy"),
        P(None, None, "gx", None, "gy"),
        P("gx", None, "gy"),
        P(None, "gx", None, "gy"),
    )
    return jax.shard_map(
        per_device,
        mesh=mesh,
        in_specs=placed,
        out_specs=(P(None, "gx", None, "gy"), P()),
        check_vma=False,
    )
```

```python
import functools
import math

import jax
import jax.numpy as jnp
from jax import lax
from jax.experimental import pallas as pl
from jax.experimental.pallas import tpu as pltpu
from jax.sharding import PartitionSpec as P

MESH = pl.DeviceIdType.MESH
SPAN_X = 4
TILE = 4
STEPS = 2

lattice_speeds = (
    (0, 0, 0),
    (1, 0, 0),
    (-1, 0, 0),
    (0, 1, 0),
    (0, -1, 0),
    (0, 0, 1),
    (0, 0, -1),
    (1, 1, 0),
    (-1, -1, 0),
    (1, -1, 0),
    (-1, 1, 0),
    (1, 0, 1),
    (-1, 0, -1),
    (1, 0, -1),
    (-1, 0, 1),
    (0, 1, 1),
    (0, -1, -1),
    (0, 1, -1),
    (0, -1, 1),
)
lattice_weights = (1.0 / 3.0,) + (1.0 / 18.0,) * 6 + (1.0 / 36.0,) * 12
relax_rate = 1.6
drag_factor = 20.0


def crossing(speeds):
    return (
        tuple(n for n, c in speeds if c[0] == 1),
        tuple(n for n, c in speeds if c[0] == -1),
        tuple(n for n, c in speeds if c[1] == 1),
        tuple(n for n, c in speeds if c[1] == -1),
        tuple(n for n, c in speeds if c[0] != 0 and c[1] != 0),
    )


MOVING = tuple((n, lattice_speeds[n]) for n in range(1, 19))
REVERSED = tuple((n, tuple(-v for v in lattice_speeds[n])) for n in range(1, 19))
N_COPIES = len(crossing(MOVING)[4])


def opposite_of(number):
    return number + 1 if number % 2 == 1 else number - 1


def along_of(speed, flow):
    along = None
    for axis in range(3):
        if speed[axis] == 0:
            continue
        term = flow[axis] if speed[axis] == 1 else -flow[axis]
        along = term if along is None else along + term
    return along


def collide(moved, flow, fluid):
    speed_sq = flow[0] * flow[0] + flow[1] * flow[1] + flow[2] * flow[2]
    scalar_part = None
    vector_part = [None, None, None]
    drag_local = None
    for number in range(19):
        speed = lattice_speeds[number]
        weighted = lattice_weights[number] * moved[number]
        along = along_of(speed, flow)
        if along is None:
            scalar_term = weighted * (1.0 - 1.5 * speed_sq)
        else:
            scalar_term = weighted * (1.0 + 3.0 * along + 4.5 * along * along - 1.5 * speed_sq)
            drag_term = 3.0 * weighted * along
            drag_local = drag_term if drag_local is None else drag_local + drag_term
        scalar_part = scalar_term if scalar_part is None else scalar_part + scalar_term
        for axis in range(3):
            if speed[axis] == 0:
                term = weighted * (-3.0 * flow[axis])
            else:
                term = weighted * (3.0 * speed[axis] + 9.0 * along * speed[axis] - 3.0 * flow[axis])
            vector_part[axis] = term if vector_part[axis] is None else vector_part[axis] + term
    results = []
    for number in range(19):
        speed = lattice_speeds[number]
        projected = scalar_part
        for axis in range(3):
            projected = projected + vector_part[axis] * (speed[axis] - flow[axis])
        results.append(fluid * ((1.0 - relax_rate) * moved[number] + relax_rate * projected))
    return results, fluid * drag_local


def send_plan(sets, speeds, field, bufs, top, near):
    up_x, dn_x, up_y, dn_y, me_x, me_y = near
    x_high, x_low, _, _, corners = sets
    xhi, xlo, _, _, corner = bufs
    plan = []
    for j, n in enumerate(()):
        cx, cy, _ = speeds[n]
        rows_at = pl.ds(0, 8) if cx == 1 else pl.ds(top, 8)
        dev_x = dn_x if cx == 1 else up_x
        dev_y = dn_y if cy == 1 else up_y
        plan.append((field(n).at[rows_at], corner.at[j], (dev_x, dev_y)))
    return plan


def start_copies(plan, send_sems, recv_sems):
    copies = []
    for k, (from_ref, to_ref, dev) in enumerate(plan):
        copy = pltpu.make_async_remote_copy(
            src_ref=from_ref, dst_ref=to_ref, send_sem=send_sems.at[k],
            recv_sem=recv_sems.at[k], device_id=dev, device_id_type=MESH)
        copy.start()
        copies.append(copy)
    return copies


def shifted(own, speed, n, sets, bufs, rows):
    x_high, x_low, y_high, y_low, corners = sets
    xhi, xlo, yhi, ylo, corner = bufs
    cx, cy, cz = speed
    top = rows - 8
    row8 = lax.broadcasted_iota(jnp.int32, (8, 128), 0)
    lane = lax.broadcasted_iota(jnp.int32, (rows, 128), 1)
    level = lax.rem(lax.broadcasted_iota(jnp.int32, (rows, 128), 0), 4)

    def patch_x(block, tile):
        if cx == 1:
            head = jnp.where(row8 < 4, tile, block[0:8])
            return jnp.concatenate([head, block[8:]], axis=0)
        tail = jnp.where(row8 >= 4, tile, block[top:])
        return jnp.concatenate([block[:top], tail], axis=0)

    if cx == 1:
        own = patch_x(own, xhi(n))
    elif cx == -1:
        own = patch_x(own, xlo(n))
    if cy != 0:
        side = yhi(n) if cy == 1 else ylo(n)
        if cx != 0:
            side = patch_x(side, corner(n))
        edge = 0 if cy == 1 else 127
        own = jnp.where(lane == edge, side, own)
    shift = 4 * cx + cz
    if shift % rows:
        own = pltpu.roll(own, (-shift) % rows, 0)
    if cy != 0:
        own = pltpu.roll(own, (-cy) % 128, 1)
    if cz == 1:
        own = jnp.where(level == 3, 0.0, own)
    elif cz == -1:
        own = jnp.where(level == 0, 0.0, own)
    return own


def pack_edge(fields, from_lane, rows):
    lane = lax.broadcasted_iota(jnp.int32, (rows, 128), 1)
    packed = jnp.zeros((rows, 128), jnp.float32)
    for k, field in enumerate(fields):
        moved = field if k == from_lane else pltpu.roll(field, (k - from_lane) % 128, 1)
        packed = jnp.where(lane == k, moved, packed)
    return packed


def pack_rows(tiles, low_half):
    row8 = lax.broadcasted_iota(jnp.int32, (8, 128), 0)
    if len(tiles) % 2:
        tiles = tiles + [jnp.zeros((8, 128), jnp.float32)]
    packed = []
    for a, b in zip(tiles[0::2], tiles[1::2]):
        if low_half:
            packed.append(jnp.where(row8 < 4, a, pltpu.roll(b, 4, 0)))
        else:
            packed.append(jnp.where(row8 >= 4, b, pltpu.roll(a, 4, 0)))
    return jnp.concatenate(packed, axis=0)


def unpack_rows(packed_ref, k, low_half):
    tile = packed_ref[pl.ds(8 * (k // 2), 8)]
    if (k % 2 == 0) == low_half:
        return tile
    return pltpu.roll(tile, 4, 0)


def unpack_edge(packed_ref, k, to_lane):
    packed = packed_ref[...]
    return packed if k == to_lane else pltpu.roll(packed, (to_lane - k) % 128, 1)


def drag_weight(number, flow, fluid):
    return (3.0 * lattice_weights[number]) * along_of(lattice_speeds[number], flow) * fluid


def start_gather(value_ref, buf, slot, peers, send_sems, recv_sems):
    copies = []
    for k, dev in peers:
        copy = pltpu.make_async_remote_copy(
            src_ref=value_ref, dst_ref=buf.at[slot], send_sem=send_sems.at[k],
            recv_sem=recv_sems.at[k], device_id=dev, device_id_type=MESH)
        copy.start()
        copies.append(copy)
    return copies


def gather_sum(value_ref, buf, slot, peers, send_sems, recv_sems, sent):
    copies = start_gather(value_ref, buf, slot, peers, send_sems, recv_sems)
    buf[slot] = value_ref[...]
    for copy in copies:
        copy.wait_recv()
    sent += copies
    total = buf[0]
    for j in range(1, len(peers) + 1):
        total = total + buf[j]
    return total


def lbm_kernel(nx, ny, rows, scale, lam_hbm, vel_hbm, blk_hbm, out_ref, drag_ref,
               lam_ref, vel_in, blk_ref, load_sem, vel_ref, fluid_ref, moved, state, hfield, xhi, xlo, yhi, ylo, corner, hcorner, ypack, ysend, yrecv,
               xpack_lo, xpack_hi, xsend, xrecv,
               part, g1_buf, g2_buf, g3_buf, g1_sum, g2_sum,
               ssem, rsem, hsend, hrecv, g1_send, g1_recv, g2_send, g2_recv, g3_send, g3_recv):
    me_x = lax.axis_index("gx")
    me_y = lax.axis_index("gy")
    up_x = lax.rem(me_x + 1, nx)
    dn_x = lax.rem(me_x + nx - 1, nx)
    up_y = lax.rem(me_y + 1, ny)
    dn_y = lax.rem(me_y + ny - 1, ny)
    near = (up_x, dn_x, up_y, dn_y, me_x, me_y)
    top = rows - 8

    loads = [
        pltpu.make_async_copy(hbm, vmem, load_sem.at[k])
        for k, (hbm, vmem) in enumerate(((lam_hbm, lam_ref), (vel_hbm, vel_in), (blk_hbm, blk_ref)))
    ]
    for load in loads:
        load.start()

    b1, b2 = nx // 2, SPAN_X
    n3 = 2 * (ny // b2)
    slot1 = lax.rem(me_x, b1)
    slot2 = lax.rem(me_y, b2)
    slot3 = (me_x // b1) * (ny // b2) + me_y // b2
    slot12 = slot1 * b2 + slot2
    peers12 = []
    for k in range(1, b1 * b2):
        t = lax.rem(slot12 + k, b1 * b2)
        peers12.append((k, ((me_x // b1) * b1 + t // b2, (me_y // b2) * b2 + lax.rem(t, b2))))
    peers3 = []
    for k in range(1, n3):
        t = lax.rem(slot3 + k, n3)
        peers3.append((k, ((t // (ny // b2)) * b1 + slot1, lax.rem(t, ny // b2) * b2 + slot2)))

    barrier = pltpu.get_barrier_semaphore()
    for _, dev in peers12 + peers3:
        pl.semaphore_signal(barrier, inc=1, device_id=dev, device_id_type=MESH)
    for dev in ((up_x, up_y), (up_x, dn_y), (dn_x, up_y), (dn_x, dn_y), (up_x, me_y), (dn_x, me_y), (me_x, up_y), (me_x, dn_y)):
        pl.semaphore_signal(barrier, inc=1, device_id=dev, device_id_type=MESH)

    loads[1].wait()
    loads[2].wait()
    for step in range(STEPS):
        for axis in range(3):
            vel_ref[step, axis] = vel_in[step, axis].astype(jnp.float32)
    level = lax.rem(lax.broadcasted_iota(jnp.int32, (rows, 128), 0), 4)
    from_below = pltpu.roll(blk_ref[4], 1, 0)
    from_above = pltpu.roll(blk_ref[5], rows - 1, 0)
    solid = jnp.where(level == 3, from_below, from_above)
    fluid_ref[...] = 1.0 - solid.astype(jnp.float32)

    last_flow = [vel_ref[STEPS - 1, axis] for axis in range(3)]
    fluid_all = fluid_ref[...]
    for number in range(1, 19):
        weight = drag_weight(number, last_flow, fluid_all)
        hfield[number - 1] = jnp.where(blk_ref[number - 1] == 1, 0.0, weight)

    pl.semaphore_wait(barrier, len(peers12) + len(peers3) + 8)

    lam_sets = crossing(MOVING)
    h_sets = crossing(REVERSED)
    h_speeds = dict(REVERSED)
    lam_speeds = dict(MOVING)
    n_hi = len(lam_sets[2])
    n_lo = len(lam_sets[3])
    nx_hi = len(lam_sets[0])
    nx_lo = len(lam_sets[1])
    h_bufs = (
        lambda n: unpack_rows(xhi.at[0], nx_hi + h_sets[0].index(n), True),
        lambda n: unpack_rows(xlo.at[0], nx_lo + h_sets[1].index(n), False),
        lambda n: unpack_edge(yhi.at[0], n_hi + h_sets[2].index(n), 0),
        lambda n: unpack_edge(ylo.at[0], n_lo + h_sets[3].index(n), 127),
        lambda n: unpack_rows(corner.at[0], 2 * lam_sets[4].index(opposite_of(n)) + 1, h_speeds[n][0] == 1),
    )
    h_copies = None
    sent = []
    drag_acc = jnp.zeros((8, 128), jnp.float32)

    for step in range(STEPS):
        src = lam_ref if step == 0 else state
        origin = lam_hbm if step == 0 else state
        bufs = (
            lambda n, s=step: unpack_rows(xhi.at[s], lam_sets[0].index(n), True),
            lambda n, s=step: unpack_rows(xlo.at[s], lam_sets[1].index(n), False),
            lambda n, s=step: unpack_edge(yhi.at[s], lam_sets[2].index(n), 0),
            lambda n, s=step: unpack_edge(ylo.at[s], lam_sets[3].index(n), 127),
            lambda n, s=step: unpack_rows(corner.at[s], 2 * lam_sets[4].index(n), lam_speeds[n][0] == 1),
        )
        plan = send_plan(lam_sets, lam_speeds, lambda n: origin.at[n], bufs, top, near)
        copies = start_copies(plan, ssem.at[step], rsem.at[step])
        if step == 0:
            h_plan = send_plan(h_sets, h_speeds, lambda n: hfield.at[n - 1], h_bufs, top, near)
            h_copies = start_copies(h_plan, hsend, hrecv)
            loads[0].wait()
        corner_plan = []
        for d, n in enumerate(lam_sets[4]):
            cx, cy, _ = lam_speeds[n]
            rows_at = slice(0, 8) if cx == 1 else slice(top, rows)
            tiles = [src[n, rows_at]]
            if step == 0:
                tiles.append(hfield[opposite_of(n) - 1, rows_at])
            hcorner[step, pl.ds(8 * d, 8)] = pack_rows(tiles, cx == 1)
            dev = (dn_x if cx == 1 else up_x, dn_y if cy == 1 else up_y)
            corner_plan.append((hcorner.at[step, pl.ds(8 * d, 8)], corner.at[step, pl.ds(8 * d, 8)], dev))
        copies += start_copies(corner_plan, ssem.at[step], rsem.at[step])
        to_low = [src[n] for n in lam_sets[2]]
        to_high = [src[n] for n in lam_sets[3]]
        if step == 0:
            to_low += [hfield[n - 1] for n in h_sets[2]]
            to_high += [hfield[n - 1] for n in h_sets[3]]
        x_low_tiles = [src[n, 0:8] for n in lam_sets[0]]
        x_high_tiles = [src[n, top:rows] for n in lam_sets[1]]
        if step == 0:
            x_low_tiles += [hfield[n - 1, 0:8] for n in h_sets[0]]
            x_high_tiles += [hfield[n - 1, top:rows] for n in h_sets[1]]
        count_lo = (len(x_low_tiles) + 1) // 2
        count_hi = (len(x_high_tiles) + 1) // 2
        xpack_lo[step, pl.ds(0, 8 * count_lo)] = pack_rows(x_low_tiles, True)
        xpack_hi[step, pl.ds(0, 8 * count_hi)] = pack_rows(x_high_tiles, False)
        copies += start_copies(
            [
                (xpack_lo.at[step, pl.ds(0, 8 * count_lo)], xhi.at[step, pl.ds(0, 8 * count_lo)], (dn_x, me_y)),
                (xpack_hi.at[step, pl.ds(0, 8 * count_hi)], xlo.at[step, pl.ds(0, 8 * count_hi)], (up_x, me_y)),
            ],
            xsend.at[step],
            xrecv.at[step],
        )
        ypack[step, 0] = pack_edge(to_low, 0, rows)
        ypack[step, 1] = pack_edge(to_high, 127, rows)
        copies += start_copies(
            [(ypack.at[step, 0], yhi.at[step], (me_x, dn_y)), (ypack.at[step, 1], ylo.at[step], (me_x, up_y))],
            ysend.at[step],
            yrecv.at[step],
        )
        if step == STEPS - 1:
            for copy in h_copies:
                copy.wait_recv()
            sent += h_copies
            total = drag_acc
            for number in range(1, 19):
                gathered = shifted(hfield[number - 1], h_speeds[number], number, h_sets, h_bufs, rows)
                total = total + jnp.sum((src[number] * gathered).reshape(rows // 8, 8, 128), axis=0)
            for number in range(1, 19):
                cx = lattice_speeds[number][0]
                weight = drag_weight(number, last_flow, fluid_all)
                bounced = jnp.where(blk_ref[number - 1] == 1, src[opposite_of(number)] + 2.0 * cx, 0.0)
                total = total + jnp.sum((weight * bounced).reshape(rows // 8, 8, 128), axis=0)
            part[...] = jnp.broadcast_to(jnp.sum(total), (8, 128))
            g1_copies = start_gather(part, g1_buf, slot12, peers12, g1_send, g1_recv)
            g1_buf[slot12] = part[...]
        for copy in copies:
            copy.wait_recv()
        sent += copies

        moved[0] = src[0]
        for number in range(1, 19):
            source = shifted(src[number], lam_speeds[number], number, lam_sets, bufs, rows)
            bounced = src[opposite_of(number)] + 2.0 * lam_speeds[number][0]
            moved[number] = jnp.where(blk_ref[number - 1] == 1, bounced, source)


        if step == STEPS - 1:
            for copy in g1_copies:
                copy.wait_recv()
            sent += g1_copies
            total = g1_buf[0]
            for j in range(1, len(peers12) + 1):
                total = total + g1_buf[j]
            g2_sum[...] = total
            g3_copies = start_gather(g2_sum, g3_buf, slot3, peers3, g3_send, g3_recv)
            g3_buf[slot3] = total

        dest = out_ref if step == STEPS - 1 else state

        def chunk(c, acc):
            at = pl.ds(pl.multiple_of(c * 8, 8), 8)
            flow = [vel_ref[step, axis, at] for axis in range(3)]
            mu = [moved[number, at] for number in range(19)]
            fresh, drag = collide(mu, flow, fluid_ref[at])
            for number in range(19):
                dest[number, at] = fresh[number]
            return acc + drag

        if step < STEPS - 1:
            drag_acc = lax.fori_loop(0, rows // 8, chunk, drag_acc)
        else:
            lax.fori_loop(0, rows // 8, chunk, drag_acc)

    for copy in g3_copies:
        copy.wait_recv()
    sent += g3_copies
    total = g3_buf[0]
    for j in range(1, n3):
        total = total + g3_buf[j]
    drag_ref[0] = -scale * total[0, 0]
    for copy in sent:
        copy.wait_send()


def per_device(adjoint_in, velocity, solid_tiles, link_blocked):
    nx = lax.axis_size("gx")
    ny = lax.axis_size("gy")
    q, rows_x, levels, rows_y = adjoint_in.shape
    rows = rows_x * levels
    lam = adjoint_in.reshape(q, rows, rows_y)
    flow = velocity.reshape(STEPS, 3, rows, rows_y)
    blocked = link_blocked.reshape(q - 1, rows, rows_y)
    cell_count = rows_x * nx * rows_y * ny * levels
    scale = drag_factor / math.sqrt(cell_count)
    vmem = pl.BlockSpec(memory_space=pltpu.VMEM)
    x_tiles = max(
        (len(crossing(MOVING)[face]) + len(crossing(REVERSED)[face]) + 1) // 2 for face in (0, 1)
    )
    state, drag = pl.pallas_call(
        functools.partial(lbm_kernel, nx, ny, rows, scale),
        out_shape=(
            jax.ShapeDtypeStruct((q, rows, rows_y), jnp.float32),
            jax.ShapeDtypeStruct((1,), jnp.float32),
        ),
        in_specs=[pl.BlockSpec(memory_space=pl.ANY)] * 3,
        out_specs=(vmem, pl.BlockSpec(memory_space=pltpu.SMEM)),
        scratch_shapes=[
            pltpu.VMEM((q, rows, rows_y), jnp.float32),
            pltpu.VMEM((STEPS, 3, rows, rows_y), velocity.dtype),
            pltpu.VMEM((q - 1, rows, rows_y), link_blocked.dtype),
            pltpu.SemaphoreType.DMA((3,)),
            pltpu.VMEM((STEPS, 3, rows, rows_y), jnp.float32),
            pltpu.VMEM((rows, rows_y), jnp.float32),
            pltpu.VMEM((q, rows, rows_y), jnp.float32),
            pltpu.VMEM((q, rows, rows_y), jnp.float32),
            pltpu.VMEM((q - 1, rows, rows_y), jnp.float32),
        ]
        + [pltpu.VMEM((STEPS, 8 * x_tiles, rows_y), jnp.float32)] * 2
        + [pltpu.VMEM((STEPS, rows, rows_y), jnp.float32)] * 2
        + [pltpu.VMEM((STEPS, 8 * len(crossing(MOVING)[4]), rows_y), jnp.float32)] * 2
        + [
            pltpu.VMEM((STEPS, 2, rows, rows_y), jnp.float32),
            pltpu.SemaphoreType.DMA((STEPS, 2)),
            pltpu.SemaphoreType.DMA((STEPS, 2)),
            pltpu.VMEM((STEPS, 8 * x_tiles, rows_y), jnp.float32),
            pltpu.VMEM((STEPS, 8 * x_tiles, rows_y), jnp.float32),
            pltpu.SemaphoreType.DMA((STEPS, 2)),
            pltpu.SemaphoreType.DMA((STEPS, 2)),
        ]
        + [
            pltpu.VMEM((8, 128), jnp.float32),
            pltpu.VMEM((nx // 2 * SPAN_X, 8, 128), jnp.float32),
            pltpu.VMEM((SPAN_X, 8, 128), jnp.float32),
            pltpu.VMEM((2 * ny // SPAN_X, 8, 128), jnp.float32),
            pltpu.VMEM((8, 128), jnp.float32),
            pltpu.VMEM((8, 128), jnp.float32),
            pltpu.SemaphoreType.DMA((STEPS, N_COPIES)),
            pltpu.SemaphoreType.DMA((STEPS, N_COPIES)),
            pltpu.SemaphoreType.DMA((N_COPIES,)),
            pltpu.SemaphoreType.DMA((N_COPIES,)),
            pltpu.SemaphoreType.DMA((nx // 2 * SPAN_X,)),
            pltpu.SemaphoreType.DMA((nx // 2 * SPAN_X,)),
            pltpu.SemaphoreType.DMA((SPAN_X,)),
            pltpu.SemaphoreType.DMA((SPAN_X,)),
            pltpu.SemaphoreType.DMA((2 * ny // SPAN_X,)),
            pltpu.SemaphoreType.DMA((2 * ny // SPAN_X,)),
        ],
        compiler_params=pltpu.CompilerParams(collective_id=0, has_side_effects=True),
    )(lam, flow, blocked)
    return (state.reshape(q, rows_x, levels, rows_y), drag)


def solution(mesh):
    placed = (
        P(None, "gx", None, "gy"),
        P(None, None, "gx", None, "gy"),
        P("gx", None, "gy"),
        P(None, "gx", None, "gy"),
    )
    return jax.shard_map(
        per_device,
        mesh=mesh,
        in_specs=placed,
        out_specs=(P(None, "gx", None, "gy"), P()),
        check_vma=False,
    )
```

```python
import functools
import math

import jax
import jax.numpy as jnp
from jax import lax
from jax.experimental import pallas as pl
from jax.experimental.pallas import tpu as pltpu
from jax.sharding import PartitionSpec as P

MESH = pl.DeviceIdType.MESH
SPAN_X = 4
TILE = 4
STEPS = 2

lattice_speeds = (
    (0, 0, 0),
    (1, 0, 0),
    (-1, 0, 0),
    (0, 1, 0),
    (0, -1, 0),
    (0, 0, 1),
    (0, 0, -1),
    (1, 1, 0),
    (-1, -1, 0),
    (1, -1, 0),
    (-1, 1, 0),
    (1, 0, 1),
    (-1, 0, -1),
    (1, 0, -1),
    (-1, 0, 1),
    (0, 1, 1),
    (0, -1, -1),
    (0, 1, -1),
    (0, -1, 1),
)
lattice_weights = (1.0 / 3.0,) + (1.0 / 18.0,) * 6 + (1.0 / 36.0,) * 12
relax_rate = 1.6
drag_factor = 20.0


def crossing(speeds):
    return (
        tuple(n for n, c in speeds if c[0] == 1),
        tuple(n for n, c in speeds if c[0] == -1),
        tuple(n for n, c in speeds if c[1] == 1),
        tuple(n for n, c in speeds if c[1] == -1),
        tuple(n for n, c in speeds if c[0] != 0 and c[1] != 0),
    )


MOVING = tuple((n, lattice_speeds[n]) for n in range(1, 19))
REVERSED = tuple((n, tuple(-v for v in lattice_speeds[n])) for n in range(1, 19))
N_COPIES = len(crossing(MOVING)[4])


def opposite_of(number):
    return number + 1 if number % 2 == 1 else number - 1


def along_of(speed, flow):
    along = None
    for axis in range(3):
        if speed[axis] == 0:
            continue
        term = flow[axis] if speed[axis] == 1 else -flow[axis]
        along = term if along is None else along + term
    return along


def collide(moved, flow, fluid):
    speed_sq = flow[0] * flow[0] + flow[1] * flow[1] + flow[2] * flow[2]
    scalar_part = None
    vector_part = [None, None, None]
    drag_local = None
    for number in range(19):
        speed = lattice_speeds[number]
        weighted = lattice_weights[number] * moved[number]
        along = along_of(speed, flow)
        if along is None:
            scalar_term = weighted * (1.0 - 1.5 * speed_sq)
        else:
            scalar_term = weighted * (1.0 + 3.0 * along + 4.5 * along * along - 1.5 * speed_sq)
            drag_term = 3.0 * weighted * along
            drag_local = drag_term if drag_local is None else drag_local + drag_term
        scalar_part = scalar_term if scalar_part is None else scalar_part + scalar_term
        for axis in range(3):
            if speed[axis] == 0:
                term = weighted * (-3.0 * flow[axis])
            else:
                term = weighted * (3.0 * speed[axis] + 9.0 * along * speed[axis] - 3.0 * flow[axis])
            vector_part[axis] = term if vector_part[axis] is None else vector_part[axis] + term
    results = []
    for number in range(19):
        speed = lattice_speeds[number]
        projected = scalar_part
        for axis in range(3):
            projected = projected + vector_part[axis] * (speed[axis] - flow[axis])
        results.append(fluid * ((1.0 - relax_rate) * moved[number] + relax_rate * projected))
    return results, fluid * drag_local


def send_plan(sets, speeds, field, bufs, top, near):
    up_x, dn_x, up_y, dn_y, me_x, me_y = near
    x_high, x_low, _, _, corners = sets
    xhi, xlo, _, _, corner = bufs
    plan = []
    for j, n in enumerate(()):
        cx, cy, _ = speeds[n]
        rows_at = pl.ds(0, 8) if cx == 1 else pl.ds(top, 8)
        dev_x = dn_x if cx == 1 else up_x
        dev_y = dn_y if cy == 1 else up_y
        plan.append((field(n).at[rows_at], corner.at[j], (dev_x, dev_y)))
    return plan


def start_copies(plan, send_sems, recv_sems):
    copies = []
    for k, (from_ref, to_ref, dev) in enumerate(plan):
        copy = pltpu.make_async_remote_copy(
            src_ref=from_ref, dst_ref=to_ref, send_sem=send_sems.at[k],
            recv_sem=recv_sems.at[k], device_id=dev, device_id_type=MESH)
        copy.start()
        copies.append(copy)
    return copies


def shifted(own, speed, n, sets, bufs, rows):
    x_high, x_low, y_high, y_low, corners = sets
    xhi, xlo, yhi, ylo, corner = bufs
    cx, cy, cz = speed
    top = rows - 8
    row8 = lax.broadcasted_iota(jnp.int32, (8, 128), 0)
    lane = lax.broadcasted_iota(jnp.int32, (rows, 128), 1)
    level = lax.rem(lax.broadcasted_iota(jnp.int32, (rows, 128), 0), 4)

    def patch_x(block, tile):
        if cx == 1:
            head = jnp.where(row8 < 4, tile, block[0:8])
            return jnp.concatenate([head, block[8:]], axis=0)
        tail = jnp.where(row8 >= 4, tile, block[top:])
        return jnp.concatenate([block[:top], tail], axis=0)

    if cx == 1:
        own = patch_x(own, xhi(n))
    elif cx == -1:
        own = patch_x(own, xlo(n))
    if cy != 0:
        side = yhi(n) if cy == 1 else ylo(n)
        if cx != 0:
            side = patch_x(side, corner(n))
        edge = 0 if cy == 1 else 127
        own = jnp.where(lane == edge, side, own)
    shift = 4 * cx + cz
    if shift % rows:
        own = pltpu.roll(own, (-shift) % rows, 0)
    if cy != 0:
        own = pltpu.roll(own, (-cy) % 128, 1)
    if cz == 1:
        own = jnp.where(level == 3, 0.0, own)
    elif cz == -1:
        own = jnp.where(level == 0, 0.0, own)
    return own


def pack_edge(fields, from_lane, rows):
    lane = lax.broadcasted_iota(jnp.int32, (rows, 128), 1)
    packed = jnp.zeros((rows, 128), jnp.float32)
    for k, field in enumerate(fields):
        moved = field if k == from_lane else pltpu.roll(field, (k - from_lane) % 128, 1)
        packed = jnp.where(lane == k, moved, packed)
    return packed


def pack_rows(tiles, low_half):
    row8 = lax.broadcasted_iota(jnp.int32, (8, 128), 0)
    if len(tiles) % 2:
        tiles = tiles + [jnp.zeros((8, 128), jnp.float32)]
    packed = []
    for a, b in zip(tiles[0::2], tiles[1::2]):
        if low_half:
            packed.append(jnp.where(row8 < 4, a, pltpu.roll(b, 4, 0)))
        else:
            packed.append(jnp.where(row8 >= 4, b, pltpu.roll(a, 4, 0)))
    return jnp.concatenate(packed, axis=0)


def unpack_rows(packed_ref, k, low_half):
    tile = packed_ref[pl.ds(8 * (k // 2), 8)]
    if (k % 2 == 0) == low_half:
        return tile
    return pltpu.roll(tile, 4, 0)


def unpack_edge(packed_ref, k, to_lane):
    packed = packed_ref[...]
    return packed if k == to_lane else pltpu.roll(packed, (to_lane - k) % 128, 1)


def drag_weight(number, flow, fluid):
    return (3.0 * lattice_weights[number]) * along_of(lattice_speeds[number], flow) * fluid


def start_gather(value_ref, buf, slot, peers, send_sems, recv_sems):
    copies = []
    for k, dev in peers:
        copy = pltpu.make_async_remote_copy(
            src_ref=value_ref, dst_ref=buf.at[slot], send_sem=send_sems.at[k],
            recv_sem=recv_sems.at[k], device_id=dev, device_id_type=MESH)
        copy.start()
        copies.append(copy)
    return copies


def gather_sum(value_ref, buf, slot, peers, send_sems, recv_sems, sent):
    copies = start_gather(value_ref, buf, slot, peers, send_sems, recv_sems)
    buf[slot] = value_ref[...]
    for copy in copies:
        copy.wait_recv()
    sent += copies
    total = buf[0]
    for j in range(1, len(peers) + 1):
        total = total + buf[j]
    return total


def lbm_kernel(nx, ny, rows, scale, lam_hbm, vel_hbm, blk_hbm, out_ref, drag_ref,
               lam_ref, vel_in, blk_ref, load_sem, vel_ref, fluid_ref, moved, state, hfield, xhi, xlo, yhi, ylo, corner, hcorner, ypack, ysend, yrecv,
               xpack_lo, xpack_hi, xsend, xrecv,
               part, g1_buf, g2_buf, g3_buf, g1_sum, g2_sum,
               ssem, rsem, hsend, hrecv, g1_send, g1_recv, g2_send, g2_recv, g3_send, g3_recv):
    me_x = lax.axis_index("gx")
    me_y = lax.axis_index("gy")
    up_x = lax.rem(me_x + 1, nx)
    dn_x = lax.rem(me_x + nx - 1, nx)
    up_y = lax.rem(me_y + 1, ny)
    dn_y = lax.rem(me_y + ny - 1, ny)
    near = (up_x, dn_x, up_y, dn_y, me_x, me_y)
    top = rows - 8

    loads = [
        pltpu.make_async_copy(hbm, vmem, load_sem.at[k])
        for k, (hbm, vmem) in enumerate(((lam_hbm, lam_ref), (vel_hbm, vel_in), (blk_hbm, blk_ref)))
    ]
    for load in loads:
        load.start()

    b1, b2 = nx // 2, SPAN_X
    n3 = 2 * (ny // b2)
    slot1 = lax.rem(me_x, b1)
    slot2 = lax.rem(me_y, b2)
    slot3 = (me_x // b1) * (ny // b2) + me_y // b2
    slot12 = slot1 * b2 + slot2
    peers12 = []
    for k in range(1, b1 * b2):
        t = lax.rem(slot12 + k, b1 * b2)
        peers12.append((k, ((me_x // b1) * b1 + t // b2, (me_y // b2) * b2 + lax.rem(t, b2))))
    peers3 = []
    for k in range(1, n3):
        t = lax.rem(slot3 + k, n3)
        peers3.append((k, ((t // (ny // b2)) * b1 + slot1, lax.rem(t, ny // b2) * b2 + slot2)))

    barrier = pltpu.get_barrier_semaphore()
    for _, dev in peers12 + peers3:
        pl.semaphore_signal(barrier, inc=1, device_id=dev, device_id_type=MESH)
    for dev in ((up_x, up_y), (up_x, dn_y), (dn_x, up_y), (dn_x, dn_y), (up_x, me_y), (dn_x, me_y), (me_x, up_y), (me_x, dn_y)):
        pl.semaphore_signal(barrier, inc=1, device_id=dev, device_id_type=MESH)

    loads[1].wait()
    loads[2].wait()
    for step in range(STEPS):
        for axis in range(3):
            vel_ref[step, axis] = vel_in[step, axis].astype(jnp.float32)
    level = lax.rem(lax.broadcasted_iota(jnp.int32, (rows, 128), 0), 4)
    from_below = pltpu.roll(blk_ref[4], 1, 0)
    from_above = pltpu.roll(blk_ref[5], rows - 1, 0)
    solid = jnp.where(level == 3, from_below, from_above)
    fluid_ref[...] = 1.0 - solid.astype(jnp.float32)

    last_flow = [vel_ref[STEPS - 1, axis] for axis in range(3)]
    fluid_all = fluid_ref[...]
    for number in range(1, 19):
        weight = drag_weight(number, last_flow, fluid_all)
        hfield[number - 1] = jnp.where(blk_ref[number - 1] == 1, 0.0, weight)

    pl.semaphore_wait(barrier, len(peers12) + len(peers3) + 8)

    lam_sets = crossing(MOVING)
    h_sets = crossing(REVERSED)
    h_speeds = dict(REVERSED)
    lam_speeds = dict(MOVING)
    n_hi = len(lam_sets[2])
    n_lo = len(lam_sets[3])
    nx_hi = len(lam_sets[0])
    nx_lo = len(lam_sets[1])
    h_bufs = (
        lambda n: unpack_rows(xhi.at[0], nx_hi + h_sets[0].index(n), True),
        lambda n: unpack_rows(xlo.at[0], nx_lo + h_sets[1].index(n), False),
        lambda n: unpack_edge(yhi.at[0], n_hi + h_sets[2].index(n), 0),
        lambda n: unpack_edge(ylo.at[0], n_lo + h_sets[3].index(n), 127),
        lambda n: unpack_rows(corner.at[0], 2 * lam_sets[4].index(opposite_of(n)) + 1, h_speeds[n][0] == 1),
    )
    h_copies = None
    sent = []
    drag_acc = jnp.zeros((8, 128), jnp.float32)

    for step in range(STEPS):
        src = lam_ref if step == 0 else state
        origin = lam_hbm if step == 0 else state
        bufs = (
            lambda n, s=step: unpack_rows(xhi.at[s], lam_sets[0].index(n), True),
            lambda n, s=step: unpack_rows(xlo.at[s], lam_sets[1].index(n), False),
            lambda n, s=step: unpack_edge(yhi.at[s], lam_sets[2].index(n), 0),
            lambda n, s=step: unpack_edge(ylo.at[s], lam_sets[3].index(n), 127),
            lambda n, s=step: unpack_rows(corner.at[s], 2 * lam_sets[4].index(n), lam_speeds[n][0] == 1),
        )
        plan = send_plan(lam_sets, lam_speeds, lambda n: origin.at[n], bufs, top, near)
        copies = start_copies(plan, ssem.at[step], rsem.at[step])
        if step == 0:
            h_plan = send_plan(h_sets, h_speeds, lambda n: hfield.at[n - 1], h_bufs, top, near)
            h_copies = start_copies(h_plan, hsend, hrecv)
            loads[0].wait()
        corner_plan = []
        for d, n in enumerate(lam_sets[4]):
            cx, cy, _ = lam_speeds[n]
            rows_at = slice(0, 8) if cx == 1 else slice(top, rows)
            tiles = [src[n, rows_at]]
            if step == 0:
                tiles.append(hfield[opposite_of(n) - 1, rows_at])
            hcorner[step, pl.ds(8 * d, 8)] = pack_rows(tiles, cx == 1)
            dev = (dn_x if cx == 1 else up_x, dn_y if cy == 1 else up_y)
            corner_plan.append((hcorner.at[step, pl.ds(8 * d, 8)], corner.at[step, pl.ds(8 * d, 8)], dev))
        copies += start_copies(corner_plan, ssem.at[step], rsem.at[step])
        to_low = [src[n] for n in lam_sets[2]]
        to_high = [src[n] for n in lam_sets[3]]
        if step == 0:
            to_low += [hfield[n - 1] for n in h_sets[2]]
            to_high += [hfield[n - 1] for n in h_sets[3]]
        x_low_tiles = [src[n, 0:8] for n in lam_sets[0]]
        x_high_tiles = [src[n, top:rows] for n in lam_sets[1]]
        if step == 0:
            x_low_tiles += [hfield[n - 1, 0:8] for n in h_sets[0]]
            x_high_tiles += [hfield[n - 1, top:rows] for n in h_sets[1]]
        count_lo = (len(x_low_tiles) + 1) // 2
        count_hi = (len(x_high_tiles) + 1) // 2
        xpack_lo[step, pl.ds(0, 8 * count_lo)] = pack_rows(x_low_tiles, True)
        xpack_hi[step, pl.ds(0, 8 * count_hi)] = pack_rows(x_high_tiles, False)
        copies += start_copies(
            [
                (xpack_lo.at[step, pl.ds(0, 8 * count_lo)], xhi.at[step, pl.ds(0, 8 * count_lo)], (dn_x, me_y)),
                (xpack_hi.at[step, pl.ds(0, 8 * count_hi)], xlo.at[step, pl.ds(0, 8 * count_hi)], (up_x, me_y)),
            ],
            xsend.at[step],
            xrecv.at[step],
        )
        ypack[step, 0] = pack_edge(to_low, 0, rows)
        ypack[step, 1] = pack_edge(to_high, 127, rows)
        copies += start_copies(
            [(ypack.at[step, 0], yhi.at[step], (me_x, dn_y)), (ypack.at[step, 1], ylo.at[step], (me_x, up_y))],
            ysend.at[step],
            yrecv.at[step],
        )
        if step == STEPS - 1:
            for copy in h_copies:
                copy.wait_recv()
            sent += h_copies
            total = drag_acc
            for number in range(1, 19):
                gathered = shifted(hfield[number - 1], h_speeds[number], number, h_sets, h_bufs, rows)
                total = total + jnp.sum((src[number] * gathered).reshape(rows // 8, 8, 128), axis=0)
            for number in range(1, 19):
                cx = lattice_speeds[number][0]
                weight = drag_weight(number, last_flow, fluid_all)
                bounced = jnp.where(blk_ref[number - 1] == 1, src[opposite_of(number)] + 2.0 * cx, 0.0)
                total = total + jnp.sum((weight * bounced).reshape(rows // 8, 8, 128), axis=0)
            part[...] = jnp.broadcast_to(jnp.sum(total), (8, 128))
            g1_copies = start_gather(part, g1_buf, slot12, peers12, g1_send, g1_recv)
            g1_buf[slot12] = part[...]
        local = tuple(n for n in range(1, 19) if lam_speeds[n][0] == 0 and lam_speeds[n][1] == 0)
        moved[0] = src[0]
        for number in local:
            source = shifted(src[number], lam_speeds[number], number, lam_sets, bufs, rows)
            bounced = src[opposite_of(number)] + 2.0 * lam_speeds[number][0]
            moved[number] = jnp.where(blk_ref[number - 1] == 1, bounced, source)
        for copy in copies:
            copy.wait_recv()
        sent += copies

        for number in (n for n in range(1, 19) if n not in local):
            source = shifted(src[number], lam_speeds[number], number, lam_sets, bufs, rows)
            bounced = src[opposite_of(number)] + 2.0 * lam_speeds[number][0]
            moved[number] = jnp.where(blk_ref[number - 1] == 1, bounced, source)


        if step == STEPS - 1:
            for copy in g1_copies:
                copy.wait_recv()
            sent += g1_copies
            total = g1_buf[0]
            for j in range(1, len(peers12) + 1):
                total = total + g1_buf[j]
            g2_sum[...] = total
            g3_copies = start_gather(g2_sum, g3_buf, slot3, peers3, g3_send, g3_recv)
            g3_buf[slot3] = total

        dest = out_ref if step == STEPS - 1 else state

        def chunk(c, acc):
            at = pl.ds(pl.multiple_of(c * 8, 8), 8)
            flow = [vel_ref[step, axis, at] for axis in range(3)]
            mu = [moved[number, at] for number in range(19)]
            fresh, drag = collide(mu, flow, fluid_ref[at])
            for number in range(19):
                dest[number, at] = fresh[number]
            return acc + drag

        if step < STEPS - 1:
            drag_acc = lax.fori_loop(0, rows // 8, chunk, drag_acc)
        else:
            lax.fori_loop(0, rows // 8, chunk, drag_acc)

    for copy in g3_copies:
        copy.wait_recv()
    sent += g3_copies
    total = g3_buf[0]
    for j in range(1, n3):
        total = total + g3_buf[j]
    drag_ref[0] = -scale * total[0, 0]
    for copy in sent:
        copy.wait_send()


def per_device(adjoint_in, velocity, solid_tiles, link_blocked):
    nx = lax.axis_size("gx")
    ny = lax.axis_size("gy")
    q, rows_x, levels, rows_y = adjoint_in.shape
    rows = rows_x * levels
    lam = adjoint_in.reshape(q, rows, rows_y)
    flow = velocity.reshape(STEPS, 3, rows, rows_y)
    blocked = link_blocked.reshape(q - 1, rows, rows_y)
    cell_count = rows_x * nx * rows_y * ny * levels
    scale = drag_factor / math.sqrt(cell_count)
    vmem = pl.BlockSpec(memory_space=pltpu.VMEM)
    x_tiles = max(
        (len(crossing(MOVING)[face]) + len(crossing(REVERSED)[face]) + 1) // 2 for face in (0, 1)
    )
    state, drag = pl.pallas_call(
        functools.partial(lbm_kernel, nx, ny, rows, scale),
        out_shape=(
            jax.ShapeDtypeStruct((q, rows, rows_y), jnp.float32),
            jax.ShapeDtypeStruct((1,), jnp.float32),
        ),
        in_specs=[pl.BlockSpec(memory_space=pl.ANY)] * 3,
        out_specs=(vmem, pl.BlockSpec(memory_space=pltpu.SMEM)),
        scratch_shapes=[
            pltpu.VMEM((q, rows, rows_y), jnp.float32),
            pltpu.VMEM((STEPS, 3, rows, rows_y), velocity.dtype),
            pltpu.VMEM((q - 1, rows, rows_y), link_blocked.dtype),
            pltpu.SemaphoreType.DMA((3,)),
            pltpu.VMEM((STEPS, 3, rows, rows_y), jnp.float32),
            pltpu.VMEM((rows, rows_y), jnp.float32),
            pltpu.VMEM((q, rows, rows_y), jnp.float32),
            pltpu.VMEM((q, rows, rows_y), jnp.float32),
            pltpu.VMEM((q - 1, rows, rows_y), jnp.float32),
        ]
        + [pltpu.VMEM((STEPS, 8 * x_tiles, rows_y), jnp.float32)] * 2
        + [pltpu.VMEM((STEPS, rows, rows_y), jnp.float32)] * 2
        + [pltpu.VMEM((STEPS, 8 * len(crossing(MOVING)[4]), rows_y), jnp.float32)] * 2
        + [
            pltpu.VMEM((STEPS, 2, rows, rows_y), jnp.float32),
            pltpu.SemaphoreType.DMA((STEPS, 2)),
            pltpu.SemaphoreType.DMA((STEPS, 2)),
            pltpu.VMEM((STEPS, 8 * x_tiles, rows_y), jnp.float32),
            pltpu.VMEM((STEPS, 8 * x_tiles, rows_y), jnp.float32),
            pltpu.SemaphoreType.DMA((STEPS, 2)),
            pltpu.SemaphoreType.DMA((STEPS, 2)),
        ]
        + [
            pltpu.VMEM((8, 128), jnp.float32),
            pltpu.VMEM((nx // 2 * SPAN_X, 8, 128), jnp.float32),
            pltpu.VMEM((SPAN_X, 8, 128), jnp.float32),
            pltpu.VMEM((2 * ny // SPAN_X, 8, 128), jnp.float32),
            pltpu.VMEM((8, 128), jnp.float32),
            pltpu.VMEM((8, 128), jnp.float32),
            pltpu.SemaphoreType.DMA((STEPS, N_COPIES)),
            pltpu.SemaphoreType.DMA((STEPS, N_COPIES)),
            pltpu.SemaphoreType.DMA((N_COPIES,)),
            pltpu.SemaphoreType.DMA((N_COPIES,)),
            pltpu.SemaphoreType.DMA((nx // 2 * SPAN_X,)),
            pltpu.SemaphoreType.DMA((nx // 2 * SPAN_X,)),
            pltpu.SemaphoreType.DMA((SPAN_X,)),
            pltpu.SemaphoreType.DMA((SPAN_X,)),
            pltpu.SemaphoreType.DMA((2 * ny // SPAN_X,)),
            pltpu.SemaphoreType.DMA((2 * ny // SPAN_X,)),
        ],
        compiler_params=pltpu.CompilerParams(collective_id=0, has_side_effects=True),
    )(lam, flow, blocked)
    return (state.reshape(q, rows_x, levels, rows_y), drag)


def solution(mesh):
    placed = (
        P(None, "gx", None, "gy"),
        P(None, None, "gx", None, "gy"),
        P("gx", None, "gy"),
        P(None, "gx", None, "gy"),
    )
    return jax.shard_map(
        per_device,
        mesh=mesh,
        in_specs=placed,
        out_specs=(P(None, "gx", None, "gy"), P()),
        check_vma=False,
    )
```

```python
import functools
import math

import jax
import jax.numpy as jnp
from jax import lax
from jax.experimental import pallas as pl
from jax.experimental.pallas import tpu as pltpu
from jax.sharding import PartitionSpec as P

MESH = pl.DeviceIdType.MESH
SPAN_X = 4
TILE = 4
STEPS = 2

lattice_speeds = (
    (0, 0, 0),
    (1, 0, 0),
    (-1, 0, 0),
    (0, 1, 0),
    (0, -1, 0),
    (0, 0, 1),
    (0, 0, -1),
    (1, 1, 0),
    (-1, -1, 0),
    (1, -1, 0),
    (-1, 1, 0),
    (1, 0, 1),
    (-1, 0, -1),
    (1, 0, -1),
    (-1, 0, 1),
    (0, 1, 1),
    (0, -1, -1),
    (0, 1, -1),
    (0, -1, 1),
)
lattice_weights = (1.0 / 3.0,) + (1.0 / 18.0,) * 6 + (1.0 / 36.0,) * 12
relax_rate = 1.6
drag_factor = 20.0


def crossing(speeds):
    return (
        tuple(n for n, c in speeds if c[0] == 1),
        tuple(n for n, c in speeds if c[0] == -1),
        tuple(n for n, c in speeds if c[1] == 1),
        tuple(n for n, c in speeds if c[1] == -1),
        tuple(n for n, c in speeds if c[0] != 0 and c[1] != 0),
    )


MOVING = tuple((n, lattice_speeds[n]) for n in range(1, 19))
REVERSED = tuple((n, tuple(-v for v in lattice_speeds[n])) for n in range(1, 19))
N_COPIES = len(crossing(MOVING)[4])


def opposite_of(number):
    return number + 1 if number % 2 == 1 else number - 1


def along_of(speed, flow):
    along = None
    for axis in range(3):
        if speed[axis] == 0:
            continue
        term = flow[axis] if speed[axis] == 1 else -flow[axis]
        along = term if along is None else along + term
    return along


def collide(moved, flow, fluid):
    speed_sq = flow[0] * flow[0] + flow[1] * flow[1] + flow[2] * flow[2]
    scalar_part = None
    vector_part = [None, None, None]
    drag_local = None
    for number in range(19):
        speed = lattice_speeds[number]
        weighted = lattice_weights[number] * moved[number]
        along = along_of(speed, flow)
        if along is None:
            scalar_term = weighted * (1.0 - 1.5 * speed_sq)
        else:
            scalar_term = weighted * (1.0 + 3.0 * along + 4.5 * along * along - 1.5 * speed_sq)
            drag_term = 3.0 * weighted * along
            drag_local = drag_term if drag_local is None else drag_local + drag_term
        scalar_part = scalar_term if scalar_part is None else scalar_part + scalar_term
        for axis in range(3):
            if speed[axis] == 0:
                term = weighted * (-3.0 * flow[axis])
            else:
                term = weighted * (3.0 * speed[axis] + 9.0 * along * speed[axis] - 3.0 * flow[axis])
            vector_part[axis] = term if vector_part[axis] is None else vector_part[axis] + term
    results = []
    for number in range(19):
        speed = lattice_speeds[number]
        projected = scalar_part
        for axis in range(3):
            projected = projected + vector_part[axis] * (speed[axis] - flow[axis])
        results.append(fluid * ((1.0 - relax_rate) * moved[number] + relax_rate * projected))
    return results, fluid * drag_local


def send_plan(sets, speeds, field, bufs, top, near):
    up_x, dn_x, up_y, dn_y, me_x, me_y = near
    x_high, x_low, _, _, corners = sets
    xhi, xlo, _, _, corner = bufs
    plan = []
    for j, n in enumerate(()):
        cx, cy, _ = speeds[n]
        rows_at = pl.ds(0, 8) if cx == 1 else pl.ds(top, 8)
        dev_x = dn_x if cx == 1 else up_x
        dev_y = dn_y if cy == 1 else up_y
        plan.append((field(n).at[rows_at], corner.at[j], (dev_x, dev_y)))
    return plan


def start_copies(plan, send_sems, recv_sems):
    copies = []
    for k, (from_ref, to_ref, dev) in enumerate(plan):
        copy = pltpu.make_async_remote_copy(
            src_ref=from_ref, dst_ref=to_ref, send_sem=send_sems.at[k],
            recv_sem=recv_sems.at[k], device_id=dev, device_id_type=MESH)
        copy.start()
        copies.append(copy)
    return copies


def shifted(own, speed, n, sets, bufs, rows):
    x_high, x_low, y_high, y_low, corners = sets
    xhi, xlo, yhi, ylo, corner = bufs
    cx, cy, cz = speed
    top = rows - 8
    row8 = lax.broadcasted_iota(jnp.int32, (8, 128), 0)
    lane = lax.broadcasted_iota(jnp.int32, (rows, 128), 1)
    level = lax.rem(lax.broadcasted_iota(jnp.int32, (rows, 128), 0), 4)

    def patch_x(block, tile):
        if cx == 1:
            head = jnp.where(row8 < 4, tile, block[0:8])
            return jnp.concatenate([head, block[8:]], axis=0)
        tail = jnp.where(row8 >= 4, tile, block[top:])
        return jnp.concatenate([block[:top], tail], axis=0)

    if cx == 1:
        own = patch_x(own, xhi(n))
    elif cx == -1:
        own = patch_x(own, xlo(n))
    if cy != 0:
        side = yhi(n) if cy == 1 else ylo(n)
        if cx != 0:
            side = patch_x(side, corner(n))
        edge = 0 if cy == 1 else 127
        own = jnp.where(lane == edge, side, own)
    shift = 4 * cx + cz
    if shift % rows:
        own = pltpu.roll(own, (-shift) % rows, 0)
    if cy != 0:
        own = pltpu.roll(own, (-cy) % 128, 1)
    if cz == 1:
        own = jnp.where(level == 3, 0.0, own)
    elif cz == -1:
        own = jnp.where(level == 0, 0.0, own)
    return own


def pack_edge(fields, from_lane, rows):
    lane = lax.broadcasted_iota(jnp.int32, (rows, 128), 1)
    packed = jnp.zeros((rows, 128), jnp.float32)
    for k, field in enumerate(fields):
        moved = field if k == from_lane else pltpu.roll(field, (k - from_lane) % 128, 1)
        packed = jnp.where(lane == k, moved, packed)
    return packed


def pack_rows(tiles, low_half):
    row8 = lax.broadcasted_iota(jnp.int32, (8, 128), 0)
    if len(tiles) % 2:
        tiles = tiles + [jnp.zeros((8, 128), jnp.float32)]
    packed = []
    for a, b in zip(tiles[0::2], tiles[1::2]):
        if low_half:
            packed.append(jnp.where(row8 < 4, a, pltpu.roll(b, 4, 0)))
        else:
            packed.append(jnp.where(row8 >= 4, b, pltpu.roll(a, 4, 0)))
    return jnp.concatenate(packed, axis=0)


def unpack_rows(packed_ref, k, low_half):
    tile = packed_ref[pl.ds(8 * (k // 2), 8)]
    if (k % 2 == 0) == low_half:
        return tile
    return pltpu.roll(tile, 4, 0)


def unpack_edge(packed_ref, k, to_lane):
    packed = packed_ref[...]
    return packed if k == to_lane else pltpu.roll(packed, (to_lane - k) % 128, 1)


def drag_weight(number, flow, fluid):
    return (3.0 * lattice_weights[number]) * along_of(lattice_speeds[number], flow) * fluid


def start_gather(value_ref, buf, slot, peers, send_sems, recv_sems):
    copies = []
    for k, dev in peers:
        copy = pltpu.make_async_remote_copy(
            src_ref=value_ref, dst_ref=buf.at[slot], send_sem=send_sems.at[k],
            recv_sem=recv_sems.at[k], device_id=dev, device_id_type=MESH)
        copy.start()
        copies.append(copy)
    return copies


def gather_sum(value_ref, buf, slot, peers, send_sems, recv_sems, sent):
    copies = start_gather(value_ref, buf, slot, peers, send_sems, recv_sems)
    buf[slot] = value_ref[...]
    for copy in copies:
        copy.wait_recv()
    sent += copies
    total = buf[0]
    for j in range(1, len(peers) + 1):
        total = total + buf[j]
    return total


def lbm_kernel(nx, ny, rows, scale, lam_hbm, vel_hbm, blk_hbm, out_ref, drag_ref,
               lam_ref, vel_in, blk_ref, load_sem, vel_ref, fluid_ref, moved, state, hfield, xhi, xlo, yhi, ylo, corner, hcorner, ypack, ysend, yrecv,
               xpack_lo, xpack_hi, xsend, xrecv,
               part, g1_buf, g2_buf, g3_buf, g1_sum, g2_sum,
               ssem, rsem, hsend, hrecv, g1_send, g1_recv, g2_send, g2_recv, g3_send, g3_recv):
    me_x = lax.axis_index("gx")
    me_y = lax.axis_index("gy")
    up_x = lax.rem(me_x + 1, nx)
    dn_x = lax.rem(me_x + nx - 1, nx)
    up_y = lax.rem(me_y + 1, ny)
    dn_y = lax.rem(me_y + ny - 1, ny)
    near = (up_x, dn_x, up_y, dn_y, me_x, me_y)
    top = rows - 8

    loads = [
        pltpu.make_async_copy(hbm, vmem, load_sem.at[k])
        for k, (hbm, vmem) in enumerate(((lam_hbm, lam_ref), (vel_hbm, vel_in), (blk_hbm, blk_ref)))
    ]
    for load in loads:
        load.start()

    b1, b2 = nx // 2, SPAN_X
    n3 = 2 * (ny // b2)
    slot1 = lax.rem(me_x, b1)
    slot2 = lax.rem(me_y, b2)
    slot3 = (me_x // b1) * (ny // b2) + me_y // b2
    slot12 = slot1 * b2 + slot2
    peers12 = []
    for k in range(1, b1 * b2):
        t = lax.rem(slot12 + k, b1 * b2)
        peers12.append((k, ((me_x // b1) * b1 + t // b2, (me_y // b2) * b2 + lax.rem(t, b2))))
    peers3 = []
    for k in range(1, n3):
        t = lax.rem(slot3 + k, n3)
        peers3.append((k, ((t // (ny // b2)) * b1 + slot1, lax.rem(t, ny // b2) * b2 + slot2)))

    barrier = pltpu.get_barrier_semaphore()
    for _, dev in peers12 + peers3:
        pl.semaphore_signal(barrier, inc=1, device_id=dev, device_id_type=MESH)
    for dev in ((up_x, up_y), (up_x, dn_y), (dn_x, up_y), (dn_x, dn_y), (up_x, me_y), (dn_x, me_y), (me_x, up_y), (me_x, dn_y)):
        pl.semaphore_signal(barrier, inc=1, device_id=dev, device_id_type=MESH)

    loads[1].wait()
    loads[2].wait()
    for step in range(STEPS):
        for axis in range(3):
            vel_ref[step, axis] = vel_in[step, axis].astype(jnp.float32)
    level = lax.rem(lax.broadcasted_iota(jnp.int32, (rows, 128), 0), 4)
    from_below = pltpu.roll(blk_ref[4], 1, 0)
    from_above = pltpu.roll(blk_ref[5], rows - 1, 0)
    solid = jnp.where(level == 3, from_below, from_above)
    fluid_ref[...] = 1.0 - solid.astype(jnp.float32)

    last_flow = [vel_ref[STEPS - 1, axis] for axis in range(3)]
    fluid_all = fluid_ref[...]
    for number in range(1, 19):
        weight = drag_weight(number, last_flow, fluid_all)
        hfield[number - 1] = jnp.where(blk_ref[number - 1] == 1, 0.0, weight)

    pl.semaphore_wait(barrier, len(peers12) + len(peers3) + 8)

    lam_sets = crossing(MOVING)
    h_sets = crossing(REVERSED)
    h_speeds = dict(REVERSED)
    lam_speeds = dict(MOVING)
    n_hi = len(lam_sets[2])
    n_lo = len(lam_sets[3])
    nx_hi = len(lam_sets[0])
    nx_lo = len(lam_sets[1])
    h_bufs = (
        lambda n: unpack_rows(xhi.at[0], nx_hi + h_sets[0].index(n), True),
        lambda n: unpack_rows(xlo.at[0], nx_lo + h_sets[1].index(n), False),
        lambda n: unpack_edge(yhi.at[0], n_hi + h_sets[2].index(n), 0),
        lambda n: unpack_edge(ylo.at[0], n_lo + h_sets[3].index(n), 127),
        lambda n: unpack_rows(corner.at[0], 2 * lam_sets[4].index(opposite_of(n)) + 1, h_speeds[n][0] == 1),
    )
    h_copies = None
    sent = []
    drag_acc = jnp.zeros((8, 128), jnp.float32)

    for step in range(STEPS):
        src = lam_ref if step == 0 else state
        origin = lam_hbm if step == 0 else state
        bufs = (
            lambda n, s=step: unpack_rows(xhi.at[s], lam_sets[0].index(n), True),
            lambda n, s=step: unpack_rows(xlo.at[s], lam_sets[1].index(n), False),
            lambda n, s=step: unpack_edge(yhi.at[s], lam_sets[2].index(n), 0),
            lambda n, s=step: unpack_edge(ylo.at[s], lam_sets[3].index(n), 127),
            lambda n, s=step: unpack_rows(corner.at[s], 2 * lam_sets[4].index(n), lam_speeds[n][0] == 1),
        )
        plan = send_plan(lam_sets, lam_speeds, lambda n: origin.at[n], bufs, top, near)
        copies = start_copies(plan, ssem.at[step], rsem.at[step])
        if step == 0:
            h_plan = send_plan(h_sets, h_speeds, lambda n: hfield.at[n - 1], h_bufs, top, near)
            h_copies = start_copies(h_plan, hsend, hrecv)
            loads[0].wait()
        corner_plan = []
        for d, n in enumerate(lam_sets[4]):
            cx, cy, _ = lam_speeds[n]
            rows_at = slice(0, 8) if cx == 1 else slice(top, rows)
            tiles = [src[n, rows_at]]
            if step == 0:
                tiles.append(hfield[opposite_of(n) - 1, rows_at])
            hcorner[step, pl.ds(8 * d, 8)] = pack_rows(tiles, cx == 1)
            dev = (dn_x if cx == 1 else up_x, dn_y if cy == 1 else up_y)
            corner_plan.append((hcorner.at[step, pl.ds(8 * d, 8)], corner.at[step, pl.ds(8 * d, 8)], dev))
        copies += start_copies(corner_plan, ssem.at[step], rsem.at[step])
        to_low = [src[n] for n in lam_sets[2]]
        to_high = [src[n] for n in lam_sets[3]]
        if step == 0:
            to_low += [hfield[n - 1] for n in h_sets[2]]
            to_high += [hfield[n - 1] for n in h_sets[3]]
        x_low_tiles = [src[n, 0:8] for n in lam_sets[0]]
        x_high_tiles = [src[n, top:rows] for n in lam_sets[1]]
        if step == 0:
            x_low_tiles += [hfield[n - 1, 0:8] for n in h_sets[0]]
            x_high_tiles += [hfield[n - 1, top:rows] for n in h_sets[1]]
        count_lo = (len(x_low_tiles) + 1) // 2
        count_hi = (len(x_high_tiles) + 1) // 2
        xpack_lo[step, pl.ds(0, 8 * count_lo)] = pack_rows(x_low_tiles, True)
        xpack_hi[step, pl.ds(0, 8 * count_hi)] = pack_rows(x_high_tiles, False)
        copies += start_copies(
            [
                (xpack_lo.at[step, pl.ds(0, 8 * count_lo)], xhi.at[step, pl.ds(0, 8 * count_lo)], (dn_x, me_y)),
                (xpack_hi.at[step, pl.ds(0, 8 * count_hi)], xlo.at[step, pl.ds(0, 8 * count_hi)], (up_x, me_y)),
            ],
            xsend.at[step],
            xrecv.at[step],
        )
        ypack[step, 0] = pack_edge(to_low, 0, rows)
        ypack[step, 1] = pack_edge(to_high, 127, rows)
        copies += start_copies(
            [(ypack.at[step, 0], yhi.at[step], (me_x, dn_y)), (ypack.at[step, 1], ylo.at[step], (me_x, up_y))],
            ysend.at[step],
            yrecv.at[step],
        )
        if step == STEPS - 1:
            for copy in h_copies:
                copy.wait_recv()
            sent += h_copies
            total = drag_acc
            for number in range(1, 19):
                gathered = shifted(hfield[number - 1], h_speeds[number], number, h_sets, h_bufs, rows)
                total = total + jnp.sum((src[number] * gathered).reshape(rows // 8, 8, 128), axis=0)
            for number in range(1, 19):
                cx = lattice_speeds[number][0]
                weight = drag_weight(number, last_flow, fluid_all)
                bounced = jnp.where(blk_ref[number - 1] == 1, src[opposite_of(number)] + 2.0 * cx, 0.0)
                total = total + jnp.sum((weight * bounced).reshape(rows // 8, 8, 128), axis=0)
            part[...] = jnp.broadcast_to(jnp.sum(total), (8, 128))
            g1_copies = start_gather(part, g1_buf, slot12, peers12, g1_send, g1_recv)
            g1_buf[slot12] = part[...]
        local = tuple(n for n in range(1, 19) if lam_speeds[n][0] == 0 and lam_speeds[n][1] == 0)
        moved[0] = src[0]
        for number in local:
            source = shifted(src[number], lam_speeds[number], number, lam_sets, bufs, rows)
            bounced = src[opposite_of(number)] + 2.0 * lam_speeds[number][0]
            moved[number] = jnp.where(blk_ref[number - 1] == 1, bounced, source)
        n_corner = len(lam_sets[4])
        waves = (
            (copies[n_corner + 2:], lambda c: c[0] == 0 and c[1] != 0),
            (copies[n_corner:n_corner + 2], lambda c: c[0] != 0 and c[1] == 0),
            (copies[:n_corner], lambda c: c[0] != 0 and c[1] != 0),
        )
        for wave, wanted in waves:
            for copy in wave:
                copy.wait_recv()
            for number in range(1, 19):
                if number in local or not wanted(lam_speeds[number]):
                    continue
                source = shifted(src[number], lam_speeds[number], number, lam_sets, bufs, rows)
                bounced = src[opposite_of(number)] + 2.0 * lam_speeds[number][0]
                moved[number] = jnp.where(blk_ref[number - 1] == 1, bounced, source)
        sent += copies


        if step == STEPS - 1:
            for copy in g1_copies:
                copy.wait_recv()
            sent += g1_copies
            total = g1_buf[0]
            for j in range(1, len(peers12) + 1):
                total = total + g1_buf[j]
            g2_sum[...] = total
            g3_copies = start_gather(g2_sum, g3_buf, slot3, peers3, g3_send, g3_recv)
            g3_buf[slot3] = total

        dest = out_ref if step == STEPS - 1 else state

        def chunk(c, acc):
            at = pl.ds(pl.multiple_of(c * 8, 8), 8)
            flow = [vel_ref[step, axis, at] for axis in range(3)]
            mu = [moved[number, at] for number in range(19)]
            fresh, drag = collide(mu, flow, fluid_ref[at])
            for number in range(19):
                dest[number, at] = fresh[number]
            return acc + drag

        if step < STEPS - 1:
            drag_acc = lax.fori_loop(0, rows // 8, chunk, drag_acc)
        else:
            lax.fori_loop(0, rows // 8, chunk, drag_acc)

    for copy in g3_copies:
        copy.wait_recv()
    sent += g3_copies
    total = g3_buf[0]
    for j in range(1, n3):
        total = total + g3_buf[j]
    drag_ref[0] = -scale * total[0, 0]
    for copy in sent:
        copy.wait_send()


def per_device(adjoint_in, velocity, solid_tiles, link_blocked):
    nx = lax.axis_size("gx")
    ny = lax.axis_size("gy")
    q, rows_x, levels, rows_y = adjoint_in.shape
    rows = rows_x * levels
    lam = adjoint_in.reshape(q, rows, rows_y)
    flow = velocity.reshape(STEPS, 3, rows, rows_y)
    blocked = link_blocked.reshape(q - 1, rows, rows_y)
    cell_count = rows_x * nx * rows_y * ny * levels
    scale = drag_factor / math.sqrt(cell_count)
    vmem = pl.BlockSpec(memory_space=pltpu.VMEM)
    x_tiles = max(
        (len(crossing(MOVING)[face]) + len(crossing(REVERSED)[face]) + 1) // 2 for face in (0, 1)
    )
    state, drag = pl.pallas_call(
        functools.partial(lbm_kernel, nx, ny, rows, scale),
        out_shape=(
            jax.ShapeDtypeStruct((q, rows, rows_y), jnp.float32),
            jax.ShapeDtypeStruct((1,), jnp.float32),
        ),
        in_specs=[pl.BlockSpec(memory_space=pl.ANY)] * 3,
        out_specs=(vmem, pl.BlockSpec(memory_space=pltpu.SMEM)),
        scratch_shapes=[
            pltpu.VMEM((q, rows, rows_y), jnp.float32),
            pltpu.VMEM((STEPS, 3, rows, rows_y), velocity.dtype),
            pltpu.VMEM((q - 1, rows, rows_y), link_blocked.dtype),
            pltpu.SemaphoreType.DMA((3,)),
            pltpu.VMEM((STEPS, 3, rows, rows_y), jnp.float32),
            pltpu.VMEM((rows, rows_y), jnp.float32),
            pltpu.VMEM((q, rows, rows_y), jnp.float32),
            pltpu.VMEM((q, rows, rows_y), jnp.float32),
            pltpu.VMEM((q - 1, rows, rows_y), jnp.float32),
        ]
        + [pltpu.VMEM((STEPS, 8 * x_tiles, rows_y), jnp.float32)] * 2
        + [pltpu.VMEM((STEPS, rows, rows_y), jnp.float32)] * 2
        + [pltpu.VMEM((STEPS, 8 * len(crossing(MOVING)[4]), rows_y), jnp.float32)] * 2
        + [
            pltpu.VMEM((STEPS, 2, rows, rows_y), jnp.float32),
            pltpu.SemaphoreType.DMA((STEPS, 2)),
            pltpu.SemaphoreType.DMA((STEPS, 2)),
            pltpu.VMEM((STEPS, 8 * x_tiles, rows_y), jnp.float32),
            pltpu.VMEM((STEPS, 8 * x_tiles, rows_y), jnp.float32),
            pltpu.SemaphoreType.DMA((STEPS, 2)),
            pltpu.SemaphoreType.DMA((STEPS, 2)),
        ]
        + [
            pltpu.VMEM((8, 128), jnp.float32),
            pltpu.VMEM((nx // 2 * SPAN_X, 8, 128), jnp.float32),
            pltpu.VMEM((SPAN_X, 8, 128), jnp.float32),
            pltpu.VMEM((2 * ny // SPAN_X, 8, 128), jnp.float32),
            pltpu.VMEM((8, 128), jnp.float32),
            pltpu.VMEM((8, 128), jnp.float32),
            pltpu.SemaphoreType.DMA((STEPS, N_COPIES)),
            pltpu.SemaphoreType.DMA((STEPS, N_COPIES)),
            pltpu.SemaphoreType.DMA((N_COPIES,)),
            pltpu.SemaphoreType.DMA((N_COPIES,)),
            pltpu.SemaphoreType.DMA((nx // 2 * SPAN_X,)),
            pltpu.SemaphoreType.DMA((nx // 2 * SPAN_X,)),
            pltpu.SemaphoreType.DMA((SPAN_X,)),
            pltpu.SemaphoreType.DMA((SPAN_X,)),
            pltpu.SemaphoreType.DMA((2 * ny // SPAN_X,)),
            pltpu.SemaphoreType.DMA((2 * ny // SPAN_X,)),
        ],
        compiler_params=pltpu.CompilerParams(collective_id=0, has_side_effects=True),
    )(lam, flow, blocked)
    return (state.reshape(q, rows_x, levels, rows_y), drag)


def solution(mesh):
    placed = (
        P(None, "gx", None, "gy"),
        P(None, None, "gx", None, "gy"),
        P("gx", None, "gy"),
        P(None, "gx", None, "gy"),
    )
    return jax.shard_map(
        per_device,
        mesh=mesh,
        in_specs=placed,
        out_specs=(P(None, "gx", None, "gy"), P()),
        check_vma=False,
    )
```
